32 devices in a mesh: dp: 8 (over z, y), mp: 4 (over x, core).
Axes of the slice: x: 2, y: 2, z: 4, core: 2. Of those that a mesh axis runs over, the one named last changes fastest.
Arguments:
- tokens: bfloat16 [8192, 2048], P('dp'), may hold values from -6 to 6
- documents: int32 [8, 1024], P('dp'), may hold values from 0 to 3, never falling along the last dimension, each value on 1 to 512 neighbouring positions
- cotangent: bfloat16 [8192, 2048], P('dp'), may hold values from -6 to 6
- attn_gain: float32 [2048], P('dp'), may hold values from 0.5 to 1.5
- query_gain: float32 [128], P('dp'), may hold values from 1 to 2
- key_norm_scale: float32 [128], P('dp'), may hold values from 0.25 to 1.75
- query_weight: float32 [2048, 2048], P('dp', 'mp'), may hold values from -0.125 to 0.125
- key_projection: float32 [2048, 1024], P('dp', 'mp'), may hold values from -0.125 to 0.125
- value_projection: float32 [2048, 1024], P('dp', 'mp'), may hold values from -0.125 to 0.125
- output_weight: float32 [2048, 2048], P('mp', 'dp'), may hold values from -1 to 1
- mlp_gain: float32 [2048], P('dp'), may hold values from 0.5 to 1.5
- gate_weight: float32 [2048, 6144], P('dp', 'mp'), may hold values from -0.125 to 0.125
- up_weight: float32 [2048, 6144], P('dp', 'mp'), may hold values from -0.125 to 0.125
- down_weight: float32 [6144, 2048], P('mp', 'dp'), may hold values from -0.078125 to 0.078125
Outputs:
- layer_output: bfloat16 [8192, 2048], P(('dp', 'mp'))
- input_grad: float32 [8192, 2048], P(('dp', 'mp'))
- attn_gain_grad: float32 [2048], P('dp')
- query_gain_grad: float32 [128], P('dp')
- key_gain_grad: float32 [128], P('dp')
- query_weight_grad: float32 [2048, 2048], P('dp', 'mp')
- key_weight_grad: float32 [2048, 1024], P('dp', 'mp')
- value_weight_grad: float32 [2048, 1024], P('dp', 'mp')
- output_weight_grad: float32 [2048, 2048], P('mp', 'dp')
- mlp_gain_grad: float32 [2048], P('dp')
- gate_weight_grad: float32 [2048, 6144], P('dp', 'mp')
- up_weight_grad: float32 [2048, 6144], P('dp', 'mp')
- down_weight_grad: float32 [6144, 2048], P('mp', 'dp')
The draws below stay inside these ranges and needn't reach their ends.
Inputs may be any that keep to these rules, and one draw needn't show every extreme that they name: `documents`: document numbers never fall along a sequence; each document holds 1 to 512 positions, and some document holds exactly 512.
All inputs are finite; a program needn't handle non-finite values.
Results may differ from the reference program's by a relative error of at most 0.023.
Values may be sent and summed in bfloat16 or wider, within the bound.
A program may use at most 256 MiB of HBM per device.

```python
import math
import jax
import jax.numpy as jnp
import numpy as np
from jax import lax

MODEL_WIDTH = 2048
QUERY_HEADS = 16
KEY_VALUE_HEADS = 8
HEAD_WIDTH = 128
FF = 6144
SEQUENCE_LENGTH = 1024
SEQUENCE_COUNT = 8
TOKEN_COUNT = 8192


def level_of(rng, extent, pieces, low, largest):
    def one(dim, blocks):
        draws = jax.random.uniform(jax.random.fold_in(jax.random.fold_in(rng, 6), dim), (blocks,), jnp.float32, low / len(pieces), largest / len(pieces))
        return jnp.repeat(jnp.exp(draws), extent[dim] // blocks).reshape((-1,) + (1,) * (len(extent) - dim - 1))

    level = one(*pieces[0])
    for cut in pieces[1:]:
        level = level * one(*cut)
    return level


def length_profile(number_of, total, bound, slope):
    weights = [(1 << 20) // math.isqrt(standing ** slope) + 1 for standing in range(2, number_of + 1)]
    rest, counts = total - bound - (number_of - 1), [1] * (number_of - 1)
    while rest > 0:
        candidates = [i for i in range(number_of - 1) if counts[i] < bound]
        pool, budget = sum([weights[i] for i in candidates]), rest
        for i in candidates:
            more = min(bound - counts[i], max(1, budget * weights[i] // pool), rest)
            counts[i] = counts[i] + more
            rest = rest - more
    return np.array([bound] + counts)


def ragged(key, amount, total, limit, skew):
    if amount == 2:
        one = jax.random.randint(key, (), max(1, total - limit), min(limit, total - 1) + 1)
        return jnp.stack([one, total - one])
    sizes = jnp.asarray(length_profile(amount, total, limit, skew), jnp.int32)
    pairs = (amount - 1) // 2
    giver, receiver = sizes[1:1 + 2 * pairs:2], sizes[2:2 + 2 * pairs:2]
    slack = jnp.minimum(giver - 1, limit - receiver)
    moved = jax.random.randint(jax.random.fold_in(key, 1), (pairs,), 0, 1 << 20) % (slack + 1)
    sizes = sizes.at[1:1 + 2 * pairs:2].set(giver - moved).at[2:2 + 2 * pairs:2].set(receiver + moved)
    return sizes[jax.random.permutation(jax.random.fold_in(key, 2), amount)]


def centred(own_key, shape, width, bound, split=(), kind=jnp.bfloat16):
    entries = width * jax.random.normal(own_key, shape, jnp.float32)
    if split:
        entries = entries * level_of(own_key, shape, split, -0.22, 0.18)
    return jnp.clip(entries, -bound, bound).astype(kind)


def setup_inputs(seed: int = 0) -> dict:
    key_list = jax.random.split(jax.random.key(seed), 15)
    return {
        "tokens": centred(key_list[0], (TOKEN_COUNT, MODEL_WIDTH), 1.0, 6.0, ((0, 8),)),
        "documents": jax.vmap(lambda own: jnp.searchsorted(jnp.cumsum(ragged(own, 4, SEQUENCE_LENGTH, SEQUENCE_LENGTH // 2, 0)), jnp.arange(SEQUENCE_LENGTH), side="right"))(jax.random.split(key_list[1], SEQUENCE_COUNT)).reshape((SEQUENCE_COUNT, SEQUENCE_LENGTH)).astype(jnp.int32),
        "cotangent": centred(key_list[2], (TOKEN_COUNT, MODEL_WIDTH), 1.0, 6.0, ((0, 8),)),
        "attn_gain": jnp.clip(1.0 + 0.1 * jax.random.normal(key_list[3], (MODEL_WIDTH,), jnp.float32), 0.5, 1.5),
        "query_gain": jnp.clip(jnp.exp(math.log(2.0) - 0.6931472 * jax.random.uniform(key_list[4], (HEAD_WIDTH,), jnp.float32) ** level_of(key_list[4], (HEAD_WIDTH,), ((0, 8),), -0.2, 0.2)), 1.0, 2.0),
        "key_norm_scale": jnp.clip(1.0 + 0.15 * jax.random.normal(key_list[5], (HEAD_WIDTH,), jnp.float32), 0.25, 1.75),
        "query_weight": centred(key_list[6], (MODEL_WIDTH, QUERY_HEADS * HEAD_WIDTH), MODEL_WIDTH ** -0.5, 0.125, ((0, 8), (1, 4)), jnp.float32),
        "key_projection": centred(key_list[7], (MODEL_WIDTH, KEY_VALUE_HEADS * HEAD_WIDTH), MODEL_WIDTH ** -0.5, 0.125, ((0, 8), (1, 4)), jnp.float32),
        "value_projection": centred(key_list[8], (MODEL_WIDTH, KEY_VALUE_HEADS * HEAD_WIDTH), MODEL_WIDTH ** -0.5, 0.125, ((0, 8), (1, 4)), jnp.float32),
        "output_weight": centred(key_list[9], (QUERY_HEADS * HEAD_WIDTH, MODEL_WIDTH), (QUERY_HEADS * HEAD_WIDTH // 64) ** -0.5, 1.0, ((0, 4), (1, 8)), jnp.float32),
        "mlp_gain": jnp.clip(1.0 + 0.1 * jax.random.normal(key_list[10], (MODEL_WIDTH,), jnp.float32), 0.5, 1.5),
        "gate_weight": centred(key_list[11], (MODEL_WIDTH, FF), MODEL_WIDTH ** -0.5, 0.125, ((0, 8), (1, 4)), jnp.float32),
        "up_weight": centred(key_list[12], (MODEL_WIDTH, FF), MODEL_WIDTH ** -0.5, 0.125, ((0, 8), (1, 4)), jnp.float32),
        "down_weight": centred(key_list[13], (FF, MODEL_WIDTH), FF ** -0.5, 0.078125, ((0, 4), (1, 8)), jnp.float32),
    }


@jax.custom_vjp
def lower_precision(v):
    return lax.optimization_barrier(v.astype(jnp.bfloat16)).astype(jnp.float32)

@jax.custom_vjp
def low_back(v):
    return v

def low_keep(v):
    return (lower_precision(v), None)

def low_pass(kept, grad):
    return (grad,)

def back_keep(v):
    return (v, None)

def back_low(kept, grad):
    return (lower_precision(grad),)
lower_precision.defvjp(low_keep, low_pass)
low_back.defvjp(back_keep, back_low)
EPSILON = 1e-06

def matmul(left, right):
    return jnp.dot(left, right, precision=lax.Precision.HIGHEST, preferred_element_type=jnp.float32)

def rowwise_norm(values, scaling):
    return values * lax.rsqrt(lax.optimization_barrier(jnp.mean(values * values, -1, keepdims=True)) + EPSILON) * scaling

def doc_positions(documents):
    indices = jnp.arange(documents.shape[-1], dtype=jnp.int32)
    boundary = jnp.concatenate([jnp.ones(documents.shape[:-1] + (1,), dtype=jnp.bool_), documents[:, 1:] != documents[:, :-1]], -1)
    starts = lax.cummax(jnp.where(boundary, indices[None, :], 0), axis=1)
    return indices[None, :] - starts

def rope_tables(positions, head_size):
    middle = head_size // 2
    frequency = jnp.power(1000000.0, -2.0 * jnp.arange(middle, dtype=jnp.float32) / head_size)
    angles = positions.astype(jnp.float32)[:, None] * frequency[None, :]
    cosine_table = jnp.cos(angles)
    sine_table = jnp.sin(angles)
    return (jnp.concatenate([cosine_table, cosine_table], -1), jnp.concatenate([sine_table, sine_table], -1))

def rotate(values):
    middle = values.shape[-1] // 2
    return jnp.concatenate([-values[..., middle:], values[..., :middle]], -1)

def rotary_embed(values, cosine_table, sine_table):
    return values * cosine_table + rotate(values) * sine_table

def sequence_attend(items):
    query_rows, key_token_rows, value_token_rows, doc_row = items
    scores = jnp.einsum('qgrd,kgd->grqk', query_rows, key_token_rows, precision=lax.Precision.HIGHEST) * HEAD_WIDTH ** (-0.5)
    scores = low_back(scores)
    indices = jnp.arange(SEQUENCE_LENGTH)
    allowed = (doc_row[:, None] == doc_row[None, :]) & (indices[None, :] <= indices[:, None])
    scores = jnp.where(allowed, scores, -1e+30)
    attention = jax.nn.softmax(scores, axis=-1)
    return jnp.einsum('grqk,kgd->qgrd', lower_precision(attention), value_token_rows, precision=lax.Precision.HIGHEST)

def forward(documents, inputs, attn_gain, query_gain, key_norm_scale, query_weight, key_projection, value_projection, output_weight, mlp_gain, gate_weight, up_weight, down_weight):
    query_group = QUERY_HEADS // KEY_VALUE_HEADS
    normed_one = lower_precision(rowwise_norm(inputs, lower_precision(attn_gain)))
    query_raw = low_back(matmul(normed_one, lower_precision(query_weight)))
    key_unnormed = low_back(matmul(normed_one, lower_precision(key_projection)))
    value_token_rows = lower_precision(low_back(matmul(normed_one, lower_precision(value_projection))))
    positions = doc_positions(documents).reshape(TOKEN_COUNT)
    cosine_table, sine_table = rope_tables(positions, HEAD_WIDTH)
    cosine_table = cosine_table[:, None, :]
    sine_table = sine_table[:, None, :]
    query_rows = lower_precision(rotary_embed(rowwise_norm(query_raw.reshape(TOKEN_COUNT, QUERY_HEADS, HEAD_WIDTH), lower_precision(query_gain)), cosine_table, sine_table))
    key_token_rows = lower_precision(rotary_embed(rowwise_norm(key_unnormed.reshape(TOKEN_COUNT, KEY_VALUE_HEADS, HEAD_WIDTH), lower_precision(key_norm_scale)), cosine_table, sine_table))
    attention_output = lax.map(jax.checkpoint(sequence_attend), (query_rows.reshape(SEQUENCE_COUNT, SEQUENCE_LENGTH, KEY_VALUE_HEADS, query_group, HEAD_WIDTH), key_token_rows.reshape(SEQUENCE_COUNT, SEQUENCE_LENGTH, KEY_VALUE_HEADS, HEAD_WIDTH), value_token_rows.reshape(SEQUENCE_COUNT, SEQUENCE_LENGTH, KEY_VALUE_HEADS, HEAD_WIDTH), documents))
    attention_output = lower_precision(low_back(attention_output.reshape(TOKEN_COUNT, QUERY_HEADS * HEAD_WIDTH)))
    hidden = inputs + low_back(matmul(attention_output, lower_precision(output_weight)))
    normed_two = lower_precision(rowwise_norm(hidden, lower_precision(mlp_gain)))
    gate_pre = low_back(matmul(normed_two, lower_precision(gate_weight)))
    up_pre = low_back(matmul(normed_two, lower_precision(up_weight)))
    active = lower_precision(jax.nn.silu(gate_pre) * up_pre)
    return hidden + matmul(active, lower_precision(down_weight))

def reference(tokens, documents, cotangent, attn_gain, query_gain, key_norm_scale, query_weight, key_projection, value_projection, output_weight, mlp_gain, gate_weight, up_weight, down_weight):
    inputs = tokens.astype(jnp.float32)

    def layer(*params):
        return forward(documents, *params)
    result, pullback = jax.vjp(layer, inputs, attn_gain, query_gain, key_norm_scale, query_weight, key_projection, value_projection, output_weight, mlp_gain, gate_weight, up_weight, down_weight)
    grads = pullback(cotangent.astype(jnp.float32))
    return (result.astype(jnp.bfloat16), grads[0], grads[1], grads[2], grads[3], grads[4], grads[5], grads[6], grads[7], grads[8], grads[9], grads[10], grads[11])
```

```python
import functools

import jax
import jax.numpy as jnp
from jax import lax
from jax.experimental import pallas as pl
from jax.experimental.pallas import tpu as pltpu
from jax.sharding import PartitionSpec as P

QUERY_HEADS = 16
KEY_VALUE_HEADS = 8
HEAD_WIDTH = 128
GROUP = QUERY_HEADS // KEY_VALUE_HEADS

EPSILON = 1e-06
MASKED = -1e30
MESH = pl.DeviceIdType.MESH
F32 = jnp.float32
BF16 = jnp.bfloat16
MIB = 2**20


def rope_tables(positions, head_size):
    middle = head_size // 2
    frequency = jnp.power(1000000.0, -2.0 * jnp.arange(middle, dtype=F32) / head_size)
    angles = positions.astype(F32)[:, None] * frequency[None, :]
    cosine_table = jnp.cos(angles)
    sine_table = jnp.sin(angles)
    return (
        jnp.concatenate([cosine_table, cosine_table], -1),
        jnp.concatenate([sine_table, sine_table], -1),
    )


def rotate(values):
    middle = values.shape[-1] // 2
    return jnp.concatenate([-values[..., middle:], values[..., :middle]], -1)


def rotate_back(values):
    middle = values.shape[-1] // 2
    return jnp.concatenate([values[..., middle:], -values[..., :middle]], -1)


def norm_parts(values):
    scaling = lax.rsqrt(jnp.mean(values * values, -1, keepdims=True) + EPSILON)
    return (values * scaling, scaling)


def norm_back(grad_normed, normed_hat, scaling, gains):
    scaled = grad_normed * gains
    return scaling * (scaled - normed_hat * jnp.mean(scaled * normed_hat, -1, keepdims=True))


def dot(left, right, left_dim=1, right_dim=0):
    return lax.dot_general(
        left, right, (((left_dim,), (right_dim,)), ((), ())), preferred_element_type=F32
    )


CHUNKS = 2
TILE = 32


def neighbours():
    dp, mp = lax.axis_index("dp"), lax.axis_index("mp")
    x, c = mp // 2, mp % 2
    return (
        x,
        c,
        (dp, x * 2 + 1 - c),
        (dp, (1 - x) * 2 + c),
        (dp + 1 - 2 * (dp % 2), mp),
    )


def enter(peers):
    barrier = pltpu.get_barrier_semaphore()
    for peer in peers:
        pl.semaphore_signal(barrier, inc=1, device_id=peer, device_id_type=MESH)
    pl.semaphore_wait(barrier, len(peers))


def remote(src, dst, send, recv, peer):
    return pltpu.make_async_remote_copy(
        src_ref=src, dst_ref=dst, send_sem=send, recv_sem=recv, device_id=peer, device_id_type=MESH
    )


def tiles(start, rows, step):
    def body(i, carry):
        step(pl.ds(pl.multiple_of(start + i * TILE, TILE), TILE))
        return carry

    lax.fori_loop(0, rows // TILE, body, 0)


class Reduce:
    STAGES = 5

    def __init__(self, part, mine, got, gx, gy, fx, fy, local, send, recv):
        self.refs = (part, mine, got, gx, gy, fx, fy, local, send, recv)
        self.rows = part.shape[3] // CHUNKS
        self.half = part.shape[4] // 2

    @staticmethod
    def scratch(rows, width):
        half = width // 2
        return [
            pltpu.VMEM((2, 2, rows, width), BF16),
            pltpu.VMEM((2, 2, rows, width), BF16),
            pltpu.VMEM((2, rows, half), BF16),
            pltpu.VMEM((2, rows, half), BF16),
            pltpu.VMEM((rows, half), BF16),
            pltpu.VMEM((rows, half), BF16),
            pltpu.SemaphoreType.DMA((CHUNKS,)),
            pltpu.SemaphoreType.DMA((Reduce.STAGES, CHUNKS)),
            pltpu.SemaphoreType.DMA((Reduce.STAGES, CHUNKS)),
        ]

    def copy(self, k, i):
        part, mine, got, gx, gy, fx, fy, local, send, recv = self.refs
        x, c, core_peer, x_peer, y_peer = neighbours()
        rows = pl.ds(k * self.rows, self.rows)
        low, high = pl.ds(0, self.half), pl.ds(self.half, self.half)
        s = [send.at[j, k] for j in range(self.STAGES)]
        r = [recv.at[j, k] for j in range(self.STAGES)]
        all_copies = (
            lambda: pltpu.make_async_copy(part.at[:, :, c, rows], mine.at[:, :, rows], local.at[k]),
            lambda: remote(part.at[:, :, 1 - c, rows], got.at[:, :, rows], s[0], r[0], core_peer),
            lambda: remote(mine.at[:, 1 - x, rows, low], gx.at[:, rows], s[1], r[1], x_peer),
            lambda: remote(mine.at[1, :, rows, high], gy.at[:, rows], s[2], r[2], y_peer),
            lambda: remote(mine.at[1, x, rows, low], fy.at[rows], s[3], r[3], y_peer),
            lambda: remote(mine.at[0, 1 - x, rows, high], fx.at[rows], s[4], r[4], x_peer),
        )
        return all_copies[i]()

    def begin(self, k):
        self.copy(k, 1).start()
        self.copy(k, 0).start()

    def first(self, k):
        _, mine, got = self.refs[:3]
        self.copy(k, 0).wait()
        self.copy(k, 1).wait_recv()

        def add(i, carry):
            def step(rows):
                at = (i // 2, i % 2, rows)
                mine[at] = (mine[at].astype(F32) + got[at].astype(F32)).astype(BF16)

            tiles(k * self.rows, self.rows, step)
            return carry

        lax.fori_loop(0, 4, add, 0)
        self.copy(k, 2).start()
        self.copy(k, 3).start()

    def second(self, k):
        _, mine, _, gx, gy = self.refs[:5]
        x = neighbours()[0]
        low, high = pl.ds(0, self.half), pl.ds(self.half, self.half)
        self.copy(k, 2).wait_recv()
        self.copy(k, 3).wait_recv()

        def step(rows):
            for i in range(2):
                at = (i, x, rows, low)
                mine[at] = (mine[at].astype(F32) + gx[i, rows].astype(F32)).astype(BF16)
                at = (0, i, rows, high)
                mine[at] = (mine[at].astype(F32) + gy[i, rows].astype(F32)).astype(BF16)

        tiles(k * self.rows, self.rows, step)
        self.copy(k, 4).start()
        self.copy(k, 5).start()

    def arrive(self, k):
        self.copy(k, 4).wait_recv()
        self.copy(k, 5).wait_recv()

    def take(self, rows):
        _, mine, _, _, _, fx, fy = self.refs[:7]
        x = neighbours()[0]
        low, high = pl.ds(0, self.half), pl.ds(self.half, self.half)
        return jnp.concatenate(
            [
                mine[0, x, rows, low].astype(F32) + fy[rows].astype(F32),
                mine[0, x, rows, high].astype(F32) + fx[rows].astype(F32),
            ],
            -1,
        )

    def finish(self):
        for k in range(CHUNKS):
            for i in range(1, 6):
                self.copy(k, i).wait_send()


class Gather:
    STAGES = 9

    def __init__(self, mine, full, local, send, recv):
        self.refs = (mine, full, local, send, recv)
        self.rows = mine.shape[0] // CHUNKS
        self.half = mine.shape[1] // 2

    @staticmethod
    def scratch(rows, width):
        return [
            pltpu.VMEM((rows, width), BF16),
            pltpu.SemaphoreType.DMA((CHUNKS,)),
            pltpu.SemaphoreType.DMA((Gather.STAGES, CHUNKS)),
            pltpu.SemaphoreType.DMA((Gather.STAGES, CHUNKS)),
        ]

    def copy(self, k, i):
        mine, full, local, send, recv = self.refs
        x, c, core_peer, x_peer, y_peer = neighbours()
        rows = pl.ds(k * self.rows, self.rows)
        low, high = pl.ds(0, self.half), pl.ds(self.half, self.half)
        s = [send.at[j, k] for j in range(self.STAGES)]
        r = [recv.at[j, k] for j in range(self.STAGES)]

        def pass_on(j, at, peer):
            return lambda: remote(full.at[at], full.at[at], s[j], r[j], peer)

        all_copies = (
            lambda: pltpu.make_async_copy(mine.at[rows], full.at[0, x, c, rows], local.at[k]),
            lambda: remote(mine.at[rows, low], full.at[1, x, c, rows, low], s[0], r[0], y_peer),
            lambda: remote(mine.at[rows, high], full.at[0, x, c, rows, high], s[1], r[1], x_peer),
            lambda: remote(mine.at[rows], full.at[0, x, c, rows], s[2], r[2], core_peer),
            pass_on(3, (slice(None), x, c, rows, low), x_peer),
            lambda: remote(
                full.at[0, :, c, rows, high], full.at[1, :, c, rows, high], s[4], r[4], y_peer
            ),
            pass_on(5, (1, x, c, rows, low), core_peer),
            pass_on(6, (0, 1 - x, c, rows, high), core_peer),
            pass_on(7, (slice(None), 1 - x, c, rows, low), core_peer),
            pass_on(8, (1, slice(None), c, rows, high), core_peer),
        )
        return all_copies[i]()

    def begin(self, k):
        for i in (1, 2, 0, 3):
            self.copy(k, i).start()

    def second(self, k):
        self.copy(k, 0).wait()
        self.copy(k, 1).wait_recv()
        self.copy(k, 4).start()
        self.copy(k, 2).wait_recv()
        for i in (5, 6, 7):
            self.copy(k, i).start()

    def third(self, k):
        for i in (4, 5):
            self.copy(k, i).wait_recv()
            self.copy(k, i + 4).start()

    def finish(self):
        for k in range(CHUNKS):
            for i in (3, 6, 7, 8, 9):
                self.copy(k, i).wait_recv()
            for i in range(1, 10):
                self.copy(k, i).wait_send()


def attention_leg(part, tokens, gain, hidden, normed, *scratch):
    n = len(Reduce.scratch(32, 256))
    reduce, gather = Reduce(part, *scratch[:n]), Gather(scratch[n], normed, *scratch[n + 1 :])
    mine = scratch[n]
    enter(neighbours()[2:])
    for k in range(CHUNKS):
        reduce.begin(k)
    for k in range(CHUNKS):
        reduce.first(k)
    for k in range(CHUNKS):
        reduce.second(k)

    def step(rows):
        h = tokens[rows].astype(F32) + reduce.take(rows)
        hidden[rows] = h
        mine[rows] = (norm_parts(h)[0] * gain[...]).astype(BF16)

    for k in range(CHUNKS):
        reduce.arrive(k)
        tiles(k * reduce.rows, reduce.rows, step)
        gather.begin(k)
    for k in range(CHUNKS):
        gather.second(k)
    for k in range(CHUNKS):
        gather.third(k)
    gather.finish()
    reduce.finish()


def hidden_leg(part, hidden, cotangent, gain, grad_hidden, gain_grad, full, *scratch):
    n = len(Reduce.scratch(32, 256))
    reduce, gather = Reduce(part, *scratch[:n]), Gather(scratch[n], full, *scratch[n + 1 :])
    mine = scratch[n]
    enter(neighbours()[2:])
    for k in range(CHUNKS):
        reduce.begin(k)
    gain_grad[...] = jnp.zeros_like(gain_grad)
    for k in range(CHUNKS):
        reduce.first(k)
    for k in range(CHUNKS):
        reduce.second(k)

    def step(rows):
        grad = reduce.take(rows)
        hat, inv = norm_parts(hidden[rows])
        gain_grad[...] += jnp.sum(grad * hat, 0, keepdims=True)
        grad = cotangent[rows].astype(F32) + norm_back(grad, hat, inv, gain[...])
        grad_hidden[rows] = grad
        mine[rows] = grad.astype(BF16)

    for k in range(CHUNKS):
        reduce.arrive(k)
        tiles(k * reduce.rows, reduce.rows, step)
        gather.begin(k)
    for k in range(CHUNKS):
        gather.second(k)
    for k in range(CHUNKS):
        gather.third(k)
    gather.finish()
    reduce.finish()


def output_leg(
    part, mlp_part, tokens, hidden, grad_hidden, gain, input_grad, output, gain_grad, *scratch
):
    n = len(Reduce.scratch(32, 256))
    legs = Reduce(part, *scratch[:n]), Reduce(mlp_part, *scratch[n:])
    enter(neighbours()[2:])
    for reduce in legs:
        for k in range(CHUNKS):
            reduce.begin(k)
    gain_grad[...] = jnp.zeros_like(gain_grad)
    for reduce in legs:
        for k in range(CHUNKS):
            reduce.first(k)
    for reduce in legs:
        for k in range(CHUNKS):
            reduce.second(k)

    def step_grad(rows):
        grad = legs[0].take(rows)
        hat, inv = norm_parts(tokens[rows].astype(F32))
        gain_grad[...] += jnp.sum(grad * hat, 0, keepdims=True)
        input_grad[rows] = grad_hidden[rows] + norm_back(grad, hat, inv, gain[...])

    def step_output(rows):
        output[rows] = (hidden[rows] + legs[1].take(rows)).astype(BF16)

    for reduce, step in zip(legs, (step_grad, step_output)):
        for k in range(CHUNKS):
            reduce.arrive(k)
            tiles(k * reduce.rows, reduce.rows, step)
    for reduce in legs:
        reduce.finish()


ANY = pl.BlockSpec(memory_space=pl.ANY)
VM = pl.BlockSpec(memory_space=pltpu.VMEM)


def call_leg(kernel, ident, name, in_specs, out_shape, out_specs, scratch, bytes_moved):
    return pl.pallas_call(
        kernel,
        out_shape=out_shape,
        in_specs=in_specs,
        out_specs=out_specs,
        scratch_shapes=scratch,
        name=name,
        cost_estimate=pl.CostEstimate(flops=0, bytes_accessed=bytes_moved, transcendentals=0),
        compiler_params=pltpu.CompilerParams(
            collective_id=ident, has_side_effects=True, vmem_limit_bytes=56 * MIB
        ),
    )


def scores_of(queries, keys, doc_rows, start, factor):
    scores = jnp.einsum("sqrd,skd->srqk", queries, keys, preferred_element_type=F32) * factor
    query_index = start + jnp.arange(queries.shape[1])
    key_index = jnp.arange(keys.shape[1])
    allowed = (doc_rows[:, start : start + queries.shape[1], None] == doc_rows[:, None, : keys.shape[1]]) & (
        key_index[None, None, :] <= query_index[None, :, None]
    )
    return jnp.where(allowed[:, None], scores, MASKED)


def on_device(
    tokens,
    documents,
    cotangent,
    attn_gain,
    query_gain,
    key_norm_scale,
    query_weight,
    key_projection,
    value_projection,
    output_weight,
    mlp_gain,
    gate_weight,
    up_weight,
    down_weight,
):
    n_dp = lax.axis_size("dp")
    dp, mp = lax.axis_index("dp"), lax.axis_index("mp")
    y, core = dp % 2, mp % 2
    slabs = [[i + 2 * k for k in range(n_dp // 2)] for i in range(2)]
    rows, width = tokens.shape
    seq_length = documents.shape[1]
    seqs = 2 * documents.shape[0]
    share = rows // 4
    head = HEAD_WIDTH
    factor = head ** (-0.5)
    query_cols, key_cols, hidden_cols = (
        query_weight.shape[1] // 2,
        key_projection.shape[1] // 2,
        gate_weight.shape[1] // 2,
    )
    attn_cols = query_cols + 2 * key_cols

    def y_swap(values):
        return lax.ppermute(values, "dp", [(i, i ^ 1) for i in range(n_dp)])

    def core_swap(values):
        return lax.ppermute(values, "mp", [(i, i ^ 1) for i in range(4)])

    def in_order(where, mine, other, axis):
        return jnp.where(
            where == 0,
            jnp.concatenate([mine, other], axis),
            jnp.concatenate([other, mine], axis),
        )

    def half(values, which, axis):
        size = values.shape[axis] // 2
        return lax.dynamic_slice_in_dim(values, which * size, size, axis)

    def slab_gather(values):
        return lax.all_gather(values, "dp", axis=0, tiled=True, axis_index_groups=slabs)

    def slab_scatter(values):
        return lax.psum_scatter(
            values, "dp", scatter_dimension=0, tiled=True, axis_index_groups=slabs
        )

    attn_low = [w.astype(BF16) for w in (query_weight, key_projection, value_projection)]
    output_low = output_weight.astype(BF16)

    def attn_pack(which):
        return jnp.concatenate(
            [half(w, which, 1) for w in attn_low] + [half(output_low, which, 0).T], 1
        )

    attn_mine = in_order(y, attn_pack(y), y_swap(attn_pack(1 - y)), 0)
    attn_full = slab_gather(attn_mine)

    mlp_low = [w.astype(BF16) for w in (gate_weight, up_weight)]
    down_low = down_weight.astype(BF16)

    def mlp_pack(which):
        return jnp.concatenate([half(w, which, 1) for w in mlp_low], 1)

    mlp_mine = in_order(y, mlp_pack(y), y_swap(mlp_pack(1 - y)), 0)
    down_mine = in_order(y, half(down_low, y, 0).T, y_swap(half(down_low, 1 - y, 0).T), 0)
    gate_up_full = slab_gather(mlp_mine)
    down_full = slab_gather(down_mine)

    gains = lax.all_gather(
        jnp.concatenate(
            [
                g.astype(BF16).reshape(1, -1)
                for g in (attn_gain, mlp_gain, query_gain, key_norm_scale)
            ],
            1,
        ),
        "dp",
        axis=0,
        tiled=True,
    ).astype(F32)
    n_gain, n_head = attn_gain.shape[0], query_gain.shape[0]
    gain_one = gains[:, :n_gain].reshape(1, width)
    gain_two = gains[:, n_gain : 2 * n_gain].reshape(1, width)
    gain_query = gains[:, 2 * n_gain : 2 * n_gain + n_head].reshape(head)
    gain_key = gains[:, 2 * n_gain + n_head :].reshape(head)

    def partner_rows(values):
        got = y_swap(half(values, core, 0))
        return in_order(core, got, core_swap(got), 0)

    tokens_pair = jnp.concatenate([tokens, partner_rows(tokens)], 0)
    cot_pair = jnp.concatenate([cotangent, partner_rows(cotangent)], 0)
    docs = jnp.concatenate([documents, y_swap(documents)], 0)
    pair_rows = 2 * rows
    tokens_share = lax.dynamic_slice_in_dim(tokens, mp * share, share, 0)
    cot_share = lax.dynamic_slice_in_dim(cotangent, mp * share, share, 0)

    inputs = tokens_pair.astype(F32)
    normed_one = (norm_parts(inputs)[0] * gain_one).astype(BF16)
    raw = dot(normed_one, attn_full[:, :attn_cols])
    query_raw, key_raw = raw[:, :query_cols], raw[:, query_cols : query_cols + key_cols]
    values = raw[:, query_cols + key_cols :].astype(BF16)
    starts = sum((docs < i).sum(1, keepdims=True) * (docs == i) for i in range(1, 4))
    positions = (jnp.arange(seq_length, dtype=jnp.int32)[None] - starts).reshape(pair_rows)
    cosine, sine = rope_tables(positions, head)
    cosine, sine = cosine[:, None, :], sine[:, None, :]
    query_hat, query_inv = norm_parts(query_raw.reshape(pair_rows, GROUP, head))
    key_hat, key_inv = norm_parts(key_raw.reshape(pair_rows, 1, head))
    query_normed, key_normed = query_hat * gain_query, key_hat * gain_key
    queries = (query_normed * cosine + rotate(query_normed) * sine).astype(BF16)
    keys = (key_normed * cosine + rotate(key_normed) * sine).astype(BF16)
    queries = queries.reshape(seqs, seq_length, GROUP, head)
    keys = keys.reshape(seqs, seq_length, head)
    values = values.reshape(seqs, seq_length, head)
    block = min(512, seq_length)
    outputs, log_totals = [], []
    for start in range(0, seq_length, block):
        end = start + block
        scores = scores_of(queries[:, start:end], keys[:, :end], docs, start, factor)
        highest = jnp.max(scores, -1, keepdims=True)
        exponent = jnp.exp(scores - highest)
        totals = jnp.sum(exponent, -1, keepdims=True)
        weights = (exponent / totals).astype(BF16)
        outputs.append(
            jnp.einsum("srqk,skd->sqrd", weights, values[:, :end], preferred_element_type=F32)
        )
        log_totals.append(highest + jnp.log(totals))
    attended = jnp.concatenate(outputs, 1).reshape(pair_rows, GROUP * head).astype(BF16)
    out_mat = attn_full[:, attn_cols:]
    attn_part = dot(attended, out_mat, 1, 1).astype(BF16)

    grouped = (2, 2, 2, share, width)
    reduce_scratch, gather_scratch = Reduce.scratch(share, width), Gather.scratch(share, width)
    hidden, normed_two = call_leg(
        attention_leg,
        0,
        "attention_leg",
        [ANY, VM, VM],
        (jax.ShapeDtypeStruct((share, width), F32), jax.ShapeDtypeStruct(grouped, BF16)),
        (VM, ANY),
        reduce_scratch + gather_scratch,
        200 * MIB,
    )(attn_part.reshape(grouped), tokens_share, gain_two)
    normed_two = normed_two.reshape(pair_rows, width)

    gate_up = dot(normed_two, gate_up_full)
    gate_pre, up_pre = gate_up[:, :hidden_cols], gate_up[:, hidden_cols:]
    sigmoid = jax.nn.sigmoid(gate_pre)
    swish = gate_pre * sigmoid
    active = (swish * up_pre).astype(BF16)
    down_grad = slab_scatter(dot(cot_pair, active, 0, 0).astype(BF16))
    mlp_part = dot(active, down_full, 1, 1).astype(BF16)
    grad_active = dot(cot_pair, down_full)
    grad_gate = (grad_active * up_pre * sigmoid * (1.0 + gate_pre * (1.0 - sigmoid))).astype(BF16)
    grad_up = (grad_active * swish).astype(BF16)
    grad_gate_up = jnp.concatenate([grad_gate, grad_up], 1)
    gate_up_grad = slab_scatter(dot(normed_two, grad_gate_up, 0, 0).astype(BF16))
    normed_two_part = dot(grad_gate_up, gate_up_full, 1, 1).astype(BF16)

    grad_hidden, mlp_gain_part, grad_hidden_low = call_leg(
        hidden_leg,
        1,
        "hidden_leg",
        [ANY, VM, VM, VM],
        (
            jax.ShapeDtypeStruct((share, width), F32),
            jax.ShapeDtypeStruct((1, width), F32),
            jax.ShapeDtypeStruct(grouped, BF16),
        ),
        (VM, VM, ANY),
        reduce_scratch + gather_scratch,
        200 * MIB,
    )(normed_two_part.reshape(grouped), hidden, cot_share, gain_two)
    grad_hidden_low = grad_hidden_low.reshape(pair_rows, width)

    output_grad = dot(grad_hidden_low, attended, 0, 0).astype(BF16)
    grad_attended = dot(grad_hidden_low, out_mat).astype(BF16)
    grad_attended = grad_attended.reshape(seqs, seq_length, GROUP, head)
    query_grads = []
    key_rot_grad = jnp.zeros((seqs, seq_length, head), F32)
    value_grad = jnp.zeros((seqs, seq_length, head), F32)
    for i, start in enumerate(range(0, seq_length, block)):
        end = start + block
        block_queries, block_grad = queries[:, start:end], grad_attended[:, start:end]
        scores = scores_of(block_queries, keys[:, :end], docs, start, factor)
        weights = jnp.exp(scores - log_totals[i])
        grad_weights = jnp.einsum(
            "sqrd,skd->srqk", block_grad, values[:, :end], preferred_element_type=F32
        )
        inner = jnp.sum(weights * grad_weights, -1, keepdims=True)
        grad_scores = (weights * (grad_weights - inner)).astype(BF16)
        query_grads.append(
            jnp.einsum("srqk,skd->sqrd", grad_scores, keys[:, :end], preferred_element_type=F32)
            * factor
        )
        key_rot_grad = key_rot_grad.at[:, :end].add(
            jnp.einsum("srqk,sqrd->skd", grad_scores, block_queries, preferred_element_type=F32)
            * factor
        )
        value_grad = value_grad.at[:, :end].add(
            jnp.einsum(
                "srqk,sqrd->skd", weights.astype(BF16), block_grad, preferred_element_type=F32
            )
        )
    query_rot_grad = jnp.concatenate(query_grads, 1).reshape(pair_rows, GROUP, head)
    key_rot_grad = key_rot_grad.reshape(pair_rows, 1, head)
    query_norm_grad = query_rot_grad * cosine + rotate_back(query_rot_grad * sine)
    key_norm_grad = key_rot_grad * cosine + rotate_back(key_rot_grad * sine)
    query_gain_part = jnp.sum(query_norm_grad * query_hat, (0, 1))
    key_gain_part = jnp.sum(key_norm_grad * key_hat, (0, 1))
    raw_grad = jnp.concatenate(
        [
            norm_back(query_norm_grad, query_hat, query_inv, gain_query)
            .reshape(pair_rows, query_cols)
            .astype(BF16),
            norm_back(key_norm_grad, key_hat, key_inv, gain_key)
            .reshape(pair_rows, key_cols)
            .astype(BF16),
            value_grad.reshape(pair_rows, key_cols).astype(BF16),
        ],
        1,
    )
    attn_grad = slab_scatter(
        jnp.concatenate([dot(normed_one, raw_grad, 0, 0).astype(BF16), output_grad], 1)
    )
    normed_one_part = dot(raw_grad, attn_full[:, :attn_cols], 1, 1).astype(BF16)

    input_grad, layer_output, attn_gain_part = call_leg(
        output_leg,
        2,
        "output_leg",
        [ANY, ANY, VM, VM, VM, VM],
        (
            jax.ShapeDtypeStruct((share, width), F32),
            jax.ShapeDtypeStruct((share, width), BF16),
            jax.ShapeDtypeStruct((1, width), F32),
        ),
        (VM, VM, VM),
        reduce_scratch + reduce_scratch,
        200 * MIB,
    )(
        normed_one_part.reshape(grouped),
        mlp_part.reshape(grouped),
        tokens_share,
        hidden,
        grad_hidden,
        gain_one,
    )

    def back(values):
        other = y_swap(half(values, 1 - y, 0)).astype(F32)
        return half(values, y, 0).astype(F32), other

    attn_own, attn_other = back(attn_grad)
    gate_up_own, gate_up_other = back(gate_up_grad)
    down_own, down_other = back(down_grad)

    def columns(own, other, start, size, axis=1):
        own, other = own[:, start : start + size], other[:, start : start + size]
        if axis == 0:
            own, other = own.T, other.T
        return in_order(y, own, other, axis)

    gain_parts = jnp.concatenate(
        [
            attn_gain_part.reshape(-1, n_gain),
            mlp_gain_part.reshape(-1, n_gain),
            query_gain_part.reshape(-1, n_head),
            key_gain_part.reshape(-1, n_head),
        ],
        1,
    )
    gain_sums = lax.psum(gain_parts, ("dp", "mp"))
    gain_sums = lax.dynamic_slice_in_dim(gain_sums, dp, 1, 0)[0]
    return (
        layer_output,
        input_grad,
        gain_sums[:n_gain],
        gain_sums[2 * n_gain : 2 * n_gain + n_head],
        gain_sums[2 * n_gain + n_head :],
        columns(attn_own, attn_other, 0, query_cols),
        columns(attn_own, attn_other, query_cols, key_cols),
        columns(attn_own, attn_other, query_cols + key_cols, key_cols),
        columns(attn_own, attn_other, attn_cols, query_cols, 0),
        gain_sums[n_gain : 2 * n_gain],
        columns(gate_up_own, gate_up_other, 0, hidden_cols),
        columns(gate_up_own, gate_up_other, hidden_cols, hidden_cols),
        columns(down_own, down_other, 0, hidden_cols, 0),
    )


def solution(mesh):
    in_specs = (
        P("dp", None),
        P("dp", None),
        P("dp", None),
        P("dp"),
        P("dp"),
        P("dp"),
        P("dp", "mp"),
        P("dp", "mp"),
        P("dp", "mp"),
        P("mp", "dp"),
        P("dp"),
        P("dp", "mp"),
        P("dp", "mp"),
        P("mp", "dp"),
    )
    out_specs = (
        P(("dp", "mp"), None),
        P(("dp", "mp"), None),
        P("dp"),
        P("dp"),
        P("dp"),
        P("dp", "mp"),
        P("dp", "mp"),
        P("dp", "mp"),
        P("mp", "dp"),
        P("dp"),
        P("dp", "mp"),
        P("dp", "mp"),
        P("mp", "dp"),
    )
    return jax.shard_map(
        on_device, mesh=mesh, in_specs=in_specs, out_specs=out_specs, check_vma=False
    )
```

```python
import functools

import jax
import jax.numpy as jnp
from jax import lax
from jax.experimental import pallas as pl
from jax.experimental.pallas import tpu as pltpu
from jax.sharding import PartitionSpec as P

QUERY_HEADS = 16
KEY_VALUE_HEADS = 8
HEAD_WIDTH = 128
GROUP = QUERY_HEADS // KEY_VALUE_HEADS

EPSILON = 1e-06
MASKED = -1e30
MESH = pl.DeviceIdType.MESH
F32 = jnp.float32
BF16 = jnp.bfloat16
MIB = 2**20


def rope_tables(positions, head_size):
    middle = head_size // 2
    frequency = jnp.power(1000000.0, -2.0 * jnp.arange(middle, dtype=F32) / head_size)
    angles = positions.astype(F32)[:, None] * frequency[None, :]
    cosine_table = jnp.cos(angles)
    sine_table = jnp.sin(angles)
    return (
        jnp.concatenate([cosine_table, cosine_table], -1),
        jnp.concatenate([-sine_table, sine_table], -1),
    )


def norm_parts(values):
    scaling = lax.rsqrt(jnp.mean(values * values, -1, keepdims=True) + EPSILON)
    return (values * scaling, scaling)


def norm_back(grad_normed, normed_hat, scaling, gains):
    scaled = grad_normed * gains
    return scaling * (scaled - normed_hat * jnp.mean(scaled * normed_hat, -1, keepdims=True))


def dot(left, right, left_dim=1, right_dim=0):
    return lax.dot_general(
        left, right, (((left_dim,), (right_dim,)), ((), ())), preferred_element_type=F32
    )


CHUNKS = 2
TILE = 32


def neighbours():
    dp, mp = lax.axis_index("dp"), lax.axis_index("mp")
    x, c = mp // 2, mp % 2
    return (
        x,
        c,
        (dp, x * 2 + 1 - c),
        (dp, (1 - x) * 2 + c),
        (dp + 1 - 2 * (dp % 2), mp),
    )


def enter(peers):
    barrier = pltpu.get_barrier_semaphore()
    for peer in peers:
        pl.semaphore_signal(barrier, inc=1, device_id=peer, device_id_type=MESH)
    pl.semaphore_wait(barrier, len(peers))


def remote(src, dst, send, recv, peer):
    return pltpu.make_async_remote_copy(
        src_ref=src, dst_ref=dst, send_sem=send, recv_sem=recv, device_id=peer, device_id_type=MESH
    )


def tiles(start, rows, step):
    def body(i, carry):
        step(pl.ds(pl.multiple_of(start + i * TILE, TILE), TILE))
        return carry

    lax.fori_loop(0, rows // TILE, body, 0)


class Reduce:
    STAGES = 5

    def __init__(self, part, mine, got, gx, gy, fx, fy, local, send, recv):
        self.refs = (part, mine, got, gx, gy, fx, fy, local, send, recv)
        self.rows = part.shape[3] // CHUNKS
        self.half = part.shape[4] // 2

    @staticmethod
    def scratch(rows, width):
        half = width // 2
        return [
            pltpu.VMEM((2, 2, rows, width), BF16),
            pltpu.VMEM((2, 2, rows, width), BF16),
            pltpu.VMEM((2, rows, half), BF16),
            pltpu.VMEM((2, rows, half), BF16),
            pltpu.VMEM((rows, half), BF16),
            pltpu.VMEM((rows, half), BF16),
            pltpu.SemaphoreType.DMA((CHUNKS,)),
            pltpu.SemaphoreType.DMA((Reduce.STAGES, CHUNKS)),
            pltpu.SemaphoreType.DMA((Reduce.STAGES, CHUNKS)),
        ]

    def copy(self, k, i):
        part, mine, got, gx, gy, fx, fy, local, send, recv = self.refs
        x, c, core_peer, x_peer, y_peer = neighbours()
        rows = pl.ds(k * self.rows, self.rows)
        low, high = pl.ds(0, self.half), pl.ds(self.half, self.half)
        s = [send.at[j, k] for j in range(self.STAGES)]
        r = [recv.at[j, k] for j in range(self.STAGES)]
        all_copies = (
            lambda: pltpu.make_async_copy(part.at[:, :, c, rows], mine.at[:, :, rows], local.at[k]),
            lambda: remote(part.at[:, :, 1 - c, rows], got.at[:, :, rows], s[0], r[0], core_peer),
            lambda: remote(mine.at[:, 1 - x, rows, low], gx.at[:, rows], s[1], r[1], x_peer),
            lambda: remote(mine.at[1, :, rows, high], gy.at[:, rows], s[2], r[2], y_peer),
            lambda: remote(mine.at[1, x, rows, low], fy.at[rows], s[3], r[3], y_peer),
            lambda: remote(mine.at[0, 1 - x, rows, high], fx.at[rows], s[4], r[4], x_peer),
        )
        return all_copies[i]()

    def begin(self, k):
        self.copy(k, 1).start()
        self.copy(k, 0).start()

    def first(self, k):
        _, mine, got = self.refs[:3]
        self.copy(k, 0).wait()
        self.copy(k, 1).wait_recv()

        def add(i, carry):
            def step(rows):
                at = (i // 2, i % 2, rows)
                mine[at] = (mine[at].astype(F32) + got[at].astype(F32)).astype(BF16)

            tiles(k * self.rows, self.rows, step)
            return carry

        lax.fori_loop(0, 4, add, 0)
        self.copy(k, 2).start()
        self.copy(k, 3).start()

    def second(self, k):
        _, mine, _, gx, gy = self.refs[:5]
        x = neighbours()[0]
        low, high = pl.ds(0, self.half), pl.ds(self.half, self.half)
        self.copy(k, 2).wait_recv()
        self.copy(k, 3).wait_recv()

        def step(rows):
            for i in range(2):
                at = (i, x, rows, low)
                mine[at] = (mine[at].astype(F32) + gx[i, rows].astype(F32)).astype(BF16)
                at = (0, i, rows, high)
                mine[at] = (mine[at].astype(F32) + gy[i, rows].astype(F32)).astype(BF16)

        tiles(k * self.rows, self.rows, step)
        self.copy(k, 4).start()
        self.copy(k, 5).start()

    def arrive(self, k):
        self.copy(k, 4).wait_recv()
        self.copy(k, 5).wait_recv()

    def take(self, rows):
        _, mine, _, _, _, fx, fy = self.refs[:7]
        x = neighbours()[0]
        low, high = pl.ds(0, self.half), pl.ds(self.half, self.half)
        return jnp.concatenate(
            [
                mine[0, x, rows, low].astype(F32) + fy[rows].astype(F32),
                mine[0, x, rows, high].astype(F32) + fx[rows].astype(F32),
            ],
            -1,
        )

    def finish(self):
        for k in range(CHUNKS):
            for i in range(1, 6):
                self.copy(k, i).wait_send()


class Gather:
    STAGES = 9

    def __init__(self, mine, full, local, send, recv):
        self.refs = (mine, full, local, send, recv)
        self.rows = mine.shape[0] // CHUNKS
        self.half = mine.shape[1] // 2

    @staticmethod
    def scratch(rows, width):
        return [
            pltpu.VMEM((rows, width), BF16),
            pltpu.SemaphoreType.DMA((CHUNKS,)),
            pltpu.SemaphoreType.DMA((Gather.STAGES, CHUNKS)),
            pltpu.SemaphoreType.DMA((Gather.STAGES, CHUNKS)),
        ]

    def copy(self, k, i):
        mine, full, local, send, recv = self.refs
        x, c, core_peer, x_peer, y_peer = neighbours()
        rows = pl.ds(k * self.rows, self.rows)
        low, high = pl.ds(0, self.half), pl.ds(self.half, self.half)
        s = [send.at[j, k] for j in range(self.STAGES)]
        r = [recv.at[j, k] for j in range(self.STAGES)]

        def pass_on(j, at, peer):
            return lambda: remote(full.at[at], full.at[at], s[j], r[j], peer)

        all_copies = (
            lambda: pltpu.make_async_copy(mine.at[rows], full.at[0, x, c, rows], local.at[k]),
            lambda: remote(mine.at[rows, low], full.at[1, x, c, rows, low], s[0], r[0], y_peer),
            lambda: remote(mine.at[rows, high], full.at[0, x, c, rows, high], s[1], r[1], x_peer),
            lambda: remote(mine.at[rows], full.at[0, x, c, rows], s[2], r[2], core_peer),
            pass_on(3, (slice(None), x, c, rows, low), x_peer),
            lambda: remote(
                full.at[0, :, c, rows, high], full.at[1, :, c, rows, high], s[4], r[4], y_peer
            ),
            pass_on(5, (1, x, c, rows, low), core_peer),
            pass_on(6, (0, 1 - x, c, rows, high), core_peer),
            pass_on(7, (slice(None), 1 - x, c, rows, low), core_peer),
            pass_on(8, (1, slice(None), c, rows, high), core_peer),
        )
        return all_copies[i]()

    def begin(self, k):
        for i in (1, 2, 0, 3):
            self.copy(k, i).start()

    def second(self, k):
        self.copy(k, 0).wait()
        self.copy(k, 1).wait_recv()
        self.copy(k, 4).start()
        self.copy(k, 2).wait_recv()
        for i in (5, 6, 7):
            self.copy(k, i).start()

    def third(self, k):
        for i in (4, 5):
            self.copy(k, i).wait_recv()
            self.copy(k, i + 4).start()

    def finish(self):
        for k in range(CHUNKS):
            for i in (3, 6, 7, 8, 9):
                self.copy(k, i).wait_recv()
            for i in range(1, 10):
                self.copy(k, i).wait_send()


def attention_leg(part, tokens, gain, hidden, normed, *scratch):
    n = len(Reduce.scratch(32, 256))
    reduce, gather = Reduce(part, *scratch[:n]), Gather(scratch[n], normed, *scratch[n + 1 :])
    mine = scratch[n]
    enter(neighbours()[2:])
    for k in range(CHUNKS):
        reduce.begin(k)
    for k in range(CHUNKS):
        reduce.first(k)
    for k in range(CHUNKS):
        reduce.second(k)

    def step(rows):
        h = tokens[rows].astype(F32) + reduce.take(rows)
        hidden[rows] = h
        mine[rows] = (norm_parts(h)[0] * gain[...]).astype(BF16)

    for k in range(CHUNKS):
        reduce.arrive(k)
        tiles(k * reduce.rows, reduce.rows, step)
        gather.begin(k)
    for k in range(CHUNKS):
        gather.second(k)
    for k in range(CHUNKS):
        gather.third(k)
    gather.finish()
    reduce.finish()


def hidden_leg(part, hidden, cotangent, gain, grad_hidden, gain_grad, full, *scratch):
    n = len(Reduce.scratch(32, 256))
    reduce, gather = Reduce(part, *scratch[:n]), Gather(scratch[n], full, *scratch[n + 1 :])
    mine = scratch[n]
    enter(neighbours()[2:])
    for k in range(CHUNKS):
        reduce.begin(k)
    gain_grad[...] = jnp.zeros_like(gain_grad)
    for k in range(CHUNKS):
        reduce.first(k)
    for k in range(CHUNKS):
        reduce.second(k)

    def step(rows):
        grad = reduce.take(rows)
        hat, inv = norm_parts(hidden[rows])
        gain_grad[...] += jnp.sum(grad * hat, 0, keepdims=True)
        grad = cotangent[rows].astype(F32) + norm_back(grad, hat, inv, gain[...])
        grad_hidden[rows] = grad
        mine[rows] = grad.astype(BF16)

    for k in range(CHUNKS):
        reduce.arrive(k)
        tiles(k * reduce.rows, reduce.rows, step)
        gather.begin(k)
    for k in range(CHUNKS):
        gather.second(k)
    for k in range(CHUNKS):
        gather.third(k)
    gather.finish()
    reduce.finish()


def output_leg(
    part, mlp_part, tokens, hidden, grad_hidden, gain, input_grad, output, gain_grad, *scratch
):
    n = len(Reduce.scratch(32, 256))
    legs = Reduce(part, *scratch[:n]), Reduce(mlp_part, *scratch[n:])
    enter(neighbours()[2:])
    for reduce in legs:
        for k in range(CHUNKS):
            reduce.begin(k)
    gain_grad[...] = jnp.zeros_like(gain_grad)
    for reduce in legs:
        for k in range(CHUNKS):
            reduce.first(k)
    for reduce in legs:
        for k in range(CHUNKS):
            reduce.second(k)

    def step_grad(rows):
        grad = legs[0].take(rows)
        hat, inv = norm_parts(tokens[rows].astype(F32))
        gain_grad[...] += jnp.sum(grad * hat, 0, keepdims=True)
        input_grad[rows] = grad_hidden[rows] + norm_back(grad, hat, inv, gain[...])

    def step_output(rows):
        output[rows] = (hidden[rows] + legs[1].take(rows)).astype(BF16)

    for reduce, step in zip(legs, (step_grad, step_output)):
        for k in range(CHUNKS):
            reduce.arrive(k)
            tiles(k * reduce.rows, reduce.rows, step)
    for reduce in legs:
        reduce.finish()


ANY = pl.BlockSpec(memory_space=pl.ANY)
VM = pl.BlockSpec(memory_space=pltpu.VMEM)


def call_leg(kernel, ident, name, in_specs, out_shape, out_specs, scratch, bytes_moved):
    return pl.pallas_call(
        kernel,
        out_shape=out_shape,
        in_specs=in_specs,
        out_specs=out_specs,
        scratch_shapes=scratch,
        name=name,
        cost_estimate=pl.CostEstimate(flops=0, bytes_accessed=bytes_moved, transcendentals=0),
        compiler_params=pltpu.CompilerParams(
            collective_id=ident, has_side_effects=True, vmem_limit_bytes=56 * MIB
        ),
    )


def prepare(q, k, v, o, gain, docs, pack, gains, docs_other, stage, swap, send, recv):
    dp, mp = lax.axis_index("dp"), lax.axis_index("mp")
    n_dp = gains.shape[0]
    y, y_peer = dp % 2, (dp + 1 - 2 * (dp % 2), mp)
    rows = q.shape[0]

    def peer(j):
        return (lax.rem(dp + j, n_dp), mp)

    barrier = pltpu.get_barrier_semaphore()

    def greet(j, carry):
        pl.semaphore_signal(barrier, inc=1, device_id=peer(j), device_id_type=MESH)
        return carry

    lax.fori_loop(1, n_dp, greet, 0)
    widths = [w.shape[1] // 2 for w in (q, k, v)]
    first = sum(widths)

    def fill_inputs(target, row, which):
        at = 0
        for w, size in zip((q, k, v), widths):
            cols = pl.ds(pl.multiple_of(which * size, 128), size)
            target[pl.ds(row, rows), at : at + size] = w[:, cols].astype(BF16)
            at += size

    def fill_output(target, row, which):
        size = o.shape[0] // 2
        part = o[pl.ds(pl.multiple_of(which * size, 128), size), :].astype(BF16)
        target[pl.ds(row, rows), first : first + size] = part.T

    mine = pl.multiple_of(y * rows, rows)

    def swapped(i):
        cols = pl.ds(0, first) if i == 0 else pl.ds(first, o.shape[0] // 2)
        target = pack.at[pl.ds(mine, rows), cols]
        return remote(stage.at[:, cols], target, swap.at[0, i], swap.at[1, i], y_peer)

    fill_inputs(stage, 0, 1 - y)
    pl.semaphore_wait(barrier, n_dp - 1)
    swapped(0).start()
    fill_output(stage, 0, 1 - y)
    swapped(1).start()
    docs_swapped = remote(docs, docs_other, swap.at[0, 2], swap.at[1, 2], y_peer)
    docs_swapped.start()

    def gain_to(j):
        return remote(gain, gains.at[dp], send.at[j], recv.at[j], peer(j))

    def share(j, carry):
        gain_to(j).start()
        return carry

    lax.fori_loop(1, n_dp, share, 0)
    gains[dp] = gain[...]
    fill_inputs(pack, mine, y)
    fill_output(pack, mine, y)

    def settle(j, carry):
        gain_to(j).wait()
        return carry

    lax.fori_loop(1, n_dp, settle, 0)
    docs_swapped.wait()
    swapped(0).wait()
    swapped(1).wait()


class Spread:
    STAGES = 4

    def __init__(self, mine, other, send, recv):
        self.refs = (mine, other, send, recv)
        self.rows = mine.shape[0] // 4 // CHUNKS

    @staticmethod
    def scratch():
        return [
            pltpu.SemaphoreType.DMA((Spread.STAGES, CHUNKS)),
            pltpu.SemaphoreType.DMA((Spread.STAGES, CHUNKS)),
        ]

    def copy(self, k, i):
        mine, other, send, recv = self.refs
        x, c, core_peer, x_peer, y_peer = neighbours()

        def rows(at_x):
            start = (at_x * 2 + c) * (mine.shape[0] // 4) + k * self.rows
            return pl.ds(pl.multiple_of(start, self.rows), self.rows)

        at = rows(1 - x) if i == 3 else rows(x)
        peer = (y_peer, x_peer, core_peer, core_peer)[i]
        source = mine if i == 0 else other
        return remote(source.at[at], other.at[at], send.at[i, k], recv.at[i, k], peer)

    def pass_on(self, k):
        self.copy(k, 0).wait_recv()
        self.copy(k, 1).start()
        self.copy(k, 2).start()

    def pass_last(self, k):
        self.copy(k, 1).wait_recv()
        self.copy(k, 3).start()

    def finish(self):
        for k in range(CHUNKS):
            for i in (2, 3):
                self.copy(k, i).wait_recv()
            for i in range(4):
                self.copy(k, i).wait_send()


def spread(tokens, gate_up_send, down_send, tokens_other, gate_up, down, send, recv, *scratch):
    rows = Spread(tokens, tokens_other, *scratch)
    y_peer = neighbours()[4]
    sent = [
        remote(gate_up_send, gate_up, send.at[0], recv.at[0], y_peer),
        remote(down_send, down, send.at[1], recv.at[1], y_peer),
    ]
    enter(neighbours()[2:])
    for k in range(CHUNKS):
        rows.copy(k, 0).start()
    for k in range(CHUNKS):
        rows.pass_on(k)
        sent[k % 2].start()
    for k in range(CHUNKS):
        rows.pass_last(k)
    rows.finish()
    for i in range(2):
        sent[i].wait()


def sum_gains(parts, total, got, mid, others, send, recv, send_mp, recv_mp):
    dp, mp = lax.axis_index("dp"), lax.axis_index("mp")
    n_dp, n_mp = parts.shape[0], others.shape[0] + 1
    barrier = pltpu.get_barrier_semaphore()

    def across(j):
        return (lax.rem(dp + j, n_dp), mp)

    def along(j):
        return (dp, lax.rem(mp + j, n_mp))

    def greet(j, carry):
        pl.semaphore_signal(barrier, inc=1, device_id=across(j), device_id_type=MESH)
        return carry

    lax.fori_loop(1, n_dp, greet, 0)
    for j in range(1, n_mp):
        pl.semaphore_signal(barrier, inc=1, device_id=along(j), device_id_type=MESH)
    pl.semaphore_wait(barrier, n_dp + n_mp - 2)

    def first(j):
        slot = lax.rem(dp + j, n_dp)
        return remote(parts.at[slot], got.at[j], send.at[j], recv.at[j], across(j))

    def start(j, carry):
        first(j).start()
        return carry

    lax.fori_loop(1, n_dp, start, 0)
    mid[...] = parts[dp]

    def add(j, carry):
        first(j).wait()
        mid[...] += got[j]
        return carry

    lax.fori_loop(1, n_dp, add, 0)

    def second(j):
        return remote(mid, others.at[j - 1], send_mp.at[j], recv_mp.at[j], along(j))

    for j in range(1, n_mp):
        second(j).start()
    result = mid[...]
    for j in range(1, n_mp):
        second(j).wait()
        result += others[j - 1]
    total[...] = result


def finish_attention(grads, q, k, v, o, other, send, recv):
    dp, mp = lax.axis_index("dp"), lax.axis_index("mp")
    y, y_peer = dp % 2, (dp + 1 - 2 * (dp % 2), mp)
    rows = q.shape[0]
    enter([y_peer])
    theirs = pl.multiple_of((1 - y) * rows, rows)
    swapped = remote(grads.at[pl.ds(theirs, rows)], other, send, recv, y_peer)
    swapped.start()

    def place(source, row, which):
        at = 0
        for w in (q, k, v):
            size = w.shape[1] // 2
            cols = pl.ds(pl.multiple_of(which * size, 128), size)
            w[:, cols] = source[pl.ds(row, rows), at : at + size].astype(F32)
            at += size
        size = o.shape[0] // 2
        part = source[pl.ds(row, rows), at : at + size].astype(F32).T
        o[pl.ds(pl.multiple_of(which * size, 128), size), :] = part

    place(grads, pl.multiple_of(y * rows, rows), y)
    swapped.wait_recv()
    place(other, 0, 1 - y)
    swapped.wait_send()


QUERY_BLOCK = 256
LONGEST = 512


def rolled(values):
    return pltpu.roll(values, HEAD_WIDTH // 2, 1)


def head_norm(raw, h):
    return norm_parts(raw[:, h * HEAD_WIDTH : (h + 1) * HEAD_WIDTH])


def rope_into(target, at, normed, cosine, sine):
    target[:, at : at + HEAD_WIDTH] = (normed * cosine[...] + rolled(normed) * sine[...]).astype(
        BF16
    )


def blocks_of(length):
    for start in range(0, length, QUERY_BLOCK):
        first = max(0, start - LONGEST)
        yield slice(start, start + QUERY_BLOCK), slice(first, start + QUERY_BLOCK)


def weights_of(query, key, starts, rows, cols):
    scores = dot(query, key, 1, 1) * HEAD_WIDTH ** (-0.5)
    query_index = rows.start + lax.broadcasted_iota(jnp.int32, scores.shape, 0)
    key_index = cols.start + lax.broadcasted_iota(jnp.int32, scores.shape, 1)
    allowed = (key_index <= query_index) & (key_index >= starts[rows])
    scores = jnp.where(allowed, scores, MASKED)
    exponent = jnp.exp(scores - jnp.max(scores, -1, keepdims=True))
    return exponent / jnp.sum(exponent, -1, keepdims=True)


def attend_forward(raw, cosine, sine, starts, gain_query, gain_key, out, q, k):
    for h in range(GROUP):
        rope_into(q, h * HEAD_WIDTH, head_norm(raw, h)[0] * gain_query[...], cosine, sine)
    rope_into(k, 0, head_norm(raw, GROUP)[0] * gain_key[...], cosine, sine)
    at = (GROUP + 1) * HEAD_WIDTH
    for rows, cols in blocks_of(raw.shape[0]):
        for h in range(GROUP):
            lanes = slice(h * HEAD_WIDTH, (h + 1) * HEAD_WIDTH)
            weights = weights_of(q[rows, lanes], k[cols], starts, rows, cols).astype(BF16)
            value = raw[cols, at : at + HEAD_WIDTH].astype(BF16)
            out[rows, lanes] = dot(weights, value).astype(BF16)


def attend_backward(
    raw, cosine, sine, starts, gain_query, gain_key, grad, out, gains, q, k, v, dq, dk, dv
):
    factor = HEAD_WIDTH ** (-0.5)
    at = (GROUP + 1) * HEAD_WIDTH
    for h in range(GROUP):
        rope_into(q, h * HEAD_WIDTH, head_norm(raw, h)[0] * gain_query[...], cosine, sine)
    rope_into(k, 0, head_norm(raw, GROUP)[0] * gain_key[...], cosine, sine)
    v[...] = raw[:, at : at + HEAD_WIDTH].astype(BF16)
    dk[...] = jnp.zeros_like(dk)
    dv[...] = jnp.zeros_like(dv)
    for rows, cols in blocks_of(raw.shape[0]):
        for h in range(GROUP):
            lanes = slice(h * HEAD_WIDTH, (h + 1) * HEAD_WIDTH)
            weights = weights_of(q[rows, lanes], k[cols], starts, rows, cols)
            grad_weights = dot(grad[rows, lanes], v[cols], 1, 1)
            inner = jnp.sum(weights * grad_weights, -1, keepdims=True)
            grad_scores = (weights * (grad_weights - inner)).astype(BF16)
            dq[rows, lanes] = dot(grad_scores, k[cols]) * factor
            dk[cols] += dot(grad_scores, q[rows, lanes], 0, 0) * factor
            dv[cols] += dot(weights.astype(BF16), grad[rows, lanes], 0, 0)
    gains[...] = jnp.zeros_like(gains)

    def undo(rot_grad, h, gain, row):
        normed_grad = rot_grad * cosine[...] - rolled(rot_grad) * sine[...]
        hat, inv = head_norm(raw, h)
        gains[0, row : row + 1] += jnp.sum(normed_grad * hat, 0, keepdims=True)
        lanes = slice(h * HEAD_WIDTH, (h + 1) * HEAD_WIDTH)
        out[:, lanes] = norm_back(normed_grad, hat, inv, gain[...]).astype(BF16)

    for h in range(GROUP):
        undo(dq[:, h * HEAD_WIDTH : (h + 1) * HEAD_WIDTH], h, gain_query, 0)
    undo(dk[...], GROUP, gain_key, 1)
    out[:, at : at + HEAD_WIDTH] = dv[...].astype(BF16)


def call_attention(kernel, length, rows, out_shape, out_specs, scratch, flops):
    def seq(cols):
        return pl.BlockSpec((length, cols), lambda i: (i, 0))

    gain = pl.BlockSpec((1, HEAD_WIDTH), lambda i: (0, 0))
    specs = [seq((GROUP + 2) * HEAD_WIDTH), seq(HEAD_WIDTH), seq(HEAD_WIDTH), seq(1), gain, gain]
    if len(scratch) > 2:
        specs.append(seq(GROUP * HEAD_WIDTH))
    return pl.pallas_call(
        kernel,
        out_shape=out_shape,
        grid=(rows // length,),
        in_specs=specs,
        out_specs=out_specs,
        scratch_shapes=scratch,
        name=kernel.__name__,
        cost_estimate=pl.CostEstimate(
            flops=flops, bytes_accessed=8 * MIB, transcendentals=rows * length * GROUP // 2
        ),
        compiler_params=pltpu.CompilerParams(
            dimension_semantics=("arbitrary",), vmem_limit_bytes=56 * MIB
        ),
    )


def on_device(
    tokens,
    documents,
    cotangent,
    attn_gain,
    query_gain,
    key_norm_scale,
    query_weight,
    key_projection,
    value_projection,
    output_weight,
    mlp_gain,
    gate_weight,
    up_weight,
    down_weight,
):
    n_dp = lax.axis_size("dp")
    dp, mp = lax.axis_index("dp"), lax.axis_index("mp")
    y = dp % 2
    slabs = [[i + 2 * k for k in range(n_dp // 2)] for i in range(2)]
    rows, width = tokens.shape
    seq_length = documents.shape[1]
    seqs = 2 * documents.shape[0]
    share = rows // 4
    head = HEAD_WIDTH
    query_cols, key_cols, hidden_cols = (
        query_weight.shape[1] // 2,
        key_projection.shape[1] // 2,
        gate_weight.shape[1] // 2,
    )
    attn_cols = query_cols + 2 * key_cols

    def y_swap(values):
        return lax.ppermute(values, "dp", [(i, i ^ 1) for i in range(n_dp)])

    def mp_swap(values, bit):
        return lax.ppermute(values, "mp", [(i, i ^ bit) for i in range(4)])

    def in_order(where, mine, other, axis):
        return jnp.where(
            where == 0,
            jnp.concatenate([mine, other], axis),
            jnp.concatenate([other, mine], axis),
        )

    def half(values, which, axis):
        size = values.shape[axis] // 2
        return lax.dynamic_slice_in_dim(values, which * size, size, axis)

    def slab_gather(values):
        return lax.all_gather(values, "dp", axis=0, tiled=True, axis_index_groups=slabs)

    def slab_scatter(values):
        return lax.psum_scatter(
            values, "dp", scatter_dimension=0, tiled=True, axis_index_groups=slabs
        )

    n_gain, n_head = attn_gain.shape[0], query_gain.shape[0]

    def gain_rows(*parts):
        lead = parts[0].shape[:-1]
        pad = [(0, 0)] * len(lead)
        rows_of = jnp.concatenate(
            [
                jnp.pad(part, pad + [(0, -part.shape[-1] % 128)]).reshape(*lead, -1, 128)
                for part in parts
            ],
            -2,
        )
        return jnp.pad(rows_of, pad + [(0, 8 - rows_of.shape[-2]), (0, 0)])

    def gain_parts_of(rows_of):
        lead, parts, at = rows_of.shape[:-2], [], 0
        for size in (n_gain, n_gain, n_head, n_head):
            n = -(-size // 128)
            part = rows_of[..., at : at + n, :].reshape(*lead, n * 128)
            parts.append(part[..., :size])
            at += n
        return parts

    my_gains = gain_rows(
        *(g.astype(BF16).astype(F32) for g in (attn_gain, mlp_gain, query_gain, key_norm_scale))
    )
    model_rows = query_weight.shape[0]
    pack_cols = attn_cols + query_cols
    attn_mine, gains, docs_other = call_leg(
        prepare,
        3,
        "prepare",
        [VM] * 6,
        (
            jax.ShapeDtypeStruct((2 * model_rows, pack_cols), BF16),
            jax.ShapeDtypeStruct((n_dp, 8, 128), F32),
            jax.ShapeDtypeStruct(documents.shape, jnp.int32),
        ),
        (VM, VM, VM),
        [
            pltpu.VMEM((model_rows, pack_cols), BF16),
            pltpu.SemaphoreType.DMA((2, 3)),
            pltpu.SemaphoreType.DMA((n_dp,)),
            pltpu.SemaphoreType.DMA((n_dp,)),
        ],
        3 * MIB,
    )(query_weight, key_projection, value_projection, output_weight, my_gains, documents)
    attn_full = slab_gather(attn_mine)

    mlp_low = [w.astype(BF16) for w in (gate_weight, up_weight)]
    down_low = down_weight.astype(BF16)

    def mlp_pack(which):
        return jnp.concatenate([half(w, which, 1) for w in mlp_low], 1)

    pair_rows = 2 * rows
    tokens_other, mlp_got, down_got = call_leg(
        spread,
        6,
        "spread",
        [ANY] * 3,
        (
            jax.ShapeDtypeStruct((rows, width), BF16),
            jax.ShapeDtypeStruct((model_rows, 2 * hidden_cols), BF16),
            jax.ShapeDtypeStruct((model_rows, hidden_cols), BF16),
        ),
        (ANY,) * 3,
        [pltpu.SemaphoreType.DMA((2,))] * 2 + Spread.scratch(),
        150 * MIB,
    )(tokens, mlp_pack(1 - y), half(down_low, 1 - y, 0).T)
    mlp_mine = in_order(y, mlp_pack(y), mlp_got, 0)
    down_mine = in_order(y, half(down_low, y, 0).T, down_got, 0)
    tokens_pair = jnp.concatenate([tokens, tokens_other], 0)

    cot_part = lax.dynamic_slice_in_dim(cotangent, mp * share, share, 0)
    cot_part, _ = lax.optimization_barrier((cot_part, tokens_other))
    cot_part = y_swap(cot_part)
    gate_up_full = slab_gather(mlp_mine)
    down_full = slab_gather(down_mine)
    gain_one, gain_two, gain_query, gain_key = (g.reshape(1, -1) for g in gain_parts_of(gains))
    docs = jnp.concatenate([documents, docs_other], 0)
    tokens_share = lax.dynamic_slice_in_dim(tokens, mp * share, share, 0)
    cot_share = lax.dynamic_slice_in_dim(cotangent, mp * share, share, 0)

    inputs = tokens_pair.astype(F32)
    normed_one = (norm_parts(inputs)[0] * gain_one).astype(BF16)
    raw = dot(normed_one, attn_full[:, :attn_cols])
    starts = sum((docs < i).sum(1, keepdims=True) * (docs == i) for i in range(1, 4))
    positions = (jnp.arange(seq_length, dtype=jnp.int32)[None] - starts).reshape(pair_rows)
    cosine, sine = rope_tables(positions, head)
    starts = starts.reshape(pair_rows, 1).astype(jnp.int32)
    raw, cot_part = lax.optimization_barrier((raw, cot_part))
    cot_pieces = in_order(mp // 2, cot_part[None], mp_swap(cot_part, 2)[None], 0)
    attention_args = (raw, cosine, sine, starts, gain_query, gain_key)
    pair_flops = pair_rows * seq_length * query_cols
    attended = call_attention(
        attend_forward,
        seq_length,
        pair_rows,
        jax.ShapeDtypeStruct((pair_rows, query_cols), BF16),
        pl.BlockSpec((seq_length, query_cols), lambda i: (i, 0)),
        [pltpu.VMEM((seq_length, query_cols), BF16), pltpu.VMEM((seq_length, head), BF16)],
        2 * pair_flops,
    )(*attention_args)
    attended, cot_pieces = lax.optimization_barrier((attended, cot_pieces))
    cot_pieces = in_order(mp % 2, cot_pieces[:, None], mp_swap(cot_pieces, 1)[:, None], 1)
    cot_pair = jnp.concatenate([cotangent, cot_pieces.reshape(rows, width)], 0)
    out_mat = attn_full[:, attn_cols:]
    attn_part = dot(attended, out_mat, 1, 1).astype(BF16)

    grouped = (2, 2, 2, share, width)
    reduce_scratch, gather_scratch = Reduce.scratch(share, width), Gather.scratch(share, width)
    hidden, normed_two = call_leg(
        attention_leg,
        0,
        "attention_leg",
        [ANY, VM, VM],
        (jax.ShapeDtypeStruct((share, width), F32), jax.ShapeDtypeStruct(grouped, BF16)),
        (VM, ANY),
        reduce_scratch + gather_scratch,
        200 * MIB,
    )(attn_part.reshape(grouped), tokens_share, gain_two)
    normed_two = normed_two.reshape(pair_rows, width)

    gate_up = dot(normed_two, gate_up_full)
    gate_pre, up_pre = gate_up[:, :hidden_cols], gate_up[:, hidden_cols:]
    sigmoid = jax.nn.sigmoid(gate_pre)
    swish = gate_pre * sigmoid
    active = (swish * up_pre).astype(BF16)
    down_part = dot(cot_pair, active, 0, 0).astype(BF16)
    down_grad = slab_scatter(down_part)
    mlp_part = dot(active, down_full, 1, 1).astype(BF16)
    cot_late, _ = lax.optimization_barrier((cot_pair, down_part))
    grad_active = dot(cot_late, down_full)
    grad_gate = (grad_active * up_pre * sigmoid * (1.0 + gate_pre * (1.0 - sigmoid))).astype(BF16)
    grad_up = (grad_active * swish).astype(BF16)
    grad_gate_up = jnp.concatenate([grad_gate, grad_up], 1)
    gate_up_part = dot(normed_two, grad_gate_up, 0, 0).astype(BF16)
    gate_up_grad = slab_scatter(gate_up_part)
    grad_gate_up, _, _ = lax.optimization_barrier((grad_gate_up, gate_up_part, down_part))
    normed_two_part = dot(grad_gate_up, gate_up_full, 1, 1).astype(BF16)

    grad_hidden, mlp_gain_part, grad_hidden_low = call_leg(
        hidden_leg,
        1,
        "hidden_leg",
        [ANY, VM, VM, VM],
        (
            jax.ShapeDtypeStruct((share, width), F32),
            jax.ShapeDtypeStruct((1, width), F32),
            jax.ShapeDtypeStruct(grouped, BF16),
        ),
        (VM, VM, ANY),
        reduce_scratch + gather_scratch,
        200 * MIB,
    )(normed_two_part.reshape(grouped), hidden, cot_share, gain_two)
    grad_hidden_low = grad_hidden_low.reshape(pair_rows, width)

    output_grad = dot(grad_hidden_low, attended, 0, 0).astype(BF16)
    grad_attended = dot(grad_hidden_low, out_mat).astype(BF16)
    raw_grad, head_gain_parts = call_attention(
        attend_backward,
        seq_length,
        pair_rows,
        (
            jax.ShapeDtypeStruct((pair_rows, attn_cols), BF16),
            jax.ShapeDtypeStruct((seqs, 8, head), F32),
        ),
        (
            pl.BlockSpec((seq_length, attn_cols), lambda i: (i, 0)),
            pl.BlockSpec((1, 8, head), lambda i: (i, 0, 0)),
        ),
        [
            pltpu.VMEM((seq_length, query_cols), BF16),
            pltpu.VMEM((seq_length, head), BF16),
            pltpu.VMEM((seq_length, head), BF16),
            pltpu.VMEM((seq_length, query_cols), F32),
            pltpu.VMEM((seq_length, head), F32),
            pltpu.VMEM((seq_length, head), F32),
        ],
        5 * pair_flops,
    )(*attention_args, grad_attended)
    head_gain_parts = head_gain_parts.sum(0)
    attn_grad = jnp.concatenate([dot(normed_one, raw_grad, 0, 0).astype(BF16), output_grad], 1)
    attn_grad, gate_up_grad, down_grad = lax.optimization_barrier(
        (attn_grad, gate_up_grad, down_grad)
    )
    attn_grad = slab_scatter(attn_grad)
    normed_one_part = dot(raw_grad, attn_full[:, :attn_cols], 1, 1).astype(BF16)

    input_grad, layer_output, attn_gain_part = call_leg(
        output_leg,
        2,
        "output_leg",
        [ANY, ANY, VM, VM, VM, VM],
        (
            jax.ShapeDtypeStruct((share, width), F32),
            jax.ShapeDtypeStruct((share, width), BF16),
            jax.ShapeDtypeStruct((1, width), F32),
        ),
        (VM, VM, VM),
        reduce_scratch + reduce_scratch,
        200 * MIB,
    )(
        normed_one_part.reshape(grouped),
        mlp_part.reshape(grouped),
        tokens_share,
        hidden,
        grad_hidden,
        gain_one,
    )

    def back(values):
        other = y_swap(half(values, 1 - y, 0)).astype(F32)
        return half(values, y, 0).astype(F32), other

    query_grad, key_grad, value_grad, output_grad = call_leg(
        finish_attention,
        5,
        "finish_attention",
        [VM],
        tuple(
            jax.ShapeDtypeStruct(w.shape, F32)
            for w in (query_weight, key_projection, value_projection, output_weight)
        ),
        (VM,) * 4,
        [
            pltpu.VMEM((model_rows, pack_cols), BF16),
            pltpu.SemaphoreType.DMA,
            pltpu.SemaphoreType.DMA,
        ],
        3 * MIB,
    )(attn_grad)
    gate_up_own, gate_up_other = back(gate_up_grad)
    down_own, down_other = back(down_grad)

    def columns(own, other, start, size, axis=1):
        own, other = own[:, start : start + size], other[:, start : start + size]
        if axis == 0:
            own, other = own.T, other.T
        return in_order(y, own, other, axis)

    gain_parts = gain_rows(
        attn_gain_part.reshape(-1, n_gain),
        mlp_gain_part.reshape(-1, n_gain),
        head_gain_parts[0].reshape(-1, n_head),
        head_gain_parts[1].reshape(-1, n_head),
    )
    gain_sums = call_leg(
        sum_gains,
        4,
        "sum_gains",
        [VM],
        jax.ShapeDtypeStruct((8, 128), F32),
        VM,
        [
            pltpu.VMEM((n_dp, 8, 128), F32),
            pltpu.VMEM((8, 128), F32),
            pltpu.VMEM((3, 8, 128), F32),
            pltpu.SemaphoreType.DMA((n_dp,)),
            pltpu.SemaphoreType.DMA((n_dp,)),
            pltpu.SemaphoreType.DMA((4,)),
            pltpu.SemaphoreType.DMA((4,)),
        ],
        1 * MIB,
    )(gain_parts)
    attn_gain_grad, mlp_gain_grad, query_gain_grad, key_gain_grad = gain_parts_of(gain_sums)
    return (
        layer_output,
        input_grad,
        attn_gain_grad,
        query_gain_grad,
        key_gain_grad,
        query_grad,
        key_grad,
        value_grad,
        output_grad,
        mlp_gain_grad,
        columns(gate_up_own, gate_up_other, 0, hidden_cols),
        columns(gate_up_own, gate_up_other, hidden_cols, hidden_cols),
        columns(down_own, down_other, 0, hidden_cols, 0),
    )


def solution(mesh):
    in_specs = (
        P("dp", None),
        P("dp", None),
        P("dp", None),
        P("dp"),
        P("dp"),
        P("dp"),
        P("dp", "mp"),
        P("dp", "mp"),
        P("dp", "mp"),
        P("mp", "dp"),
        P("dp"),
        P("dp", "mp"),
        P("dp", "mp"),
        P("mp", "dp"),
    )
    out_specs = (
        P(("dp", "mp"), None),
        P(("dp", "mp"), None),
        P("dp"),
        P("dp"),
        P("dp"),
        P("dp", "mp"),
        P("dp", "mp"),
        P("dp", "mp"),
        P("mp", "dp"),
        P("dp"),
        P("dp", "mp"),
        P("dp", "mp"),
        P("mp", "dp"),
    )
    return jax.shard_map(
        on_device, mesh=mesh, in_specs=in_specs, out_specs=out_specs, check_vma=False
    )
```

```python
import functools

import jax
import jax.numpy as jnp
from jax import lax
from jax.experimental import pallas as pl
from jax.experimental.pallas import tpu as pltpu
from jax.sharding import PartitionSpec as P

QUERY_HEADS = 16
KEY_VALUE_HEADS = 8
HEAD_WIDTH = 128
GROUP = QUERY_HEADS // KEY_VALUE_HEADS

EPSILON = 1e-06
MASKED = -1e30
MESH = pl.DeviceIdType.MESH
F32 = jnp.float32
BF16 = jnp.bfloat16
MIB = 2**20


def rope_tables(positions, head_size):
    middle = head_size // 2
    frequency = jnp.power(1000000.0, -2.0 * jnp.arange(middle, dtype=F32) / head_size)
    angles = positions.astype(F32)[:, None] * frequency[None, :]
    cosine_table = jnp.cos(angles)
    sine_table = jnp.sin(angles)
    return (
        jnp.concatenate([cosine_table, cosine_table], -1),
        jnp.concatenate([-sine_table, sine_table], -1),
    )


def norm_parts(values):
    scaling = lax.rsqrt(jnp.mean(values * values, -1, keepdims=True) + EPSILON)
    return (values * scaling, scaling)


def norm_back(grad_normed, normed_hat, scaling, gains):
    scaled = grad_normed * gains
    return scaling * (scaled - normed_hat * jnp.mean(scaled * normed_hat, -1, keepdims=True))


def dot(left, right, left_dim=1, right_dim=0):
    return lax.dot_general(
        left, right, (((left_dim,), (right_dim,)), ((), ())), preferred_element_type=F32
    )


CHUNKS = 2
TILE = 32
COLUMNS = 512


def neighbours():
    dp, mp = lax.axis_index("dp"), lax.axis_index("mp")
    x, c = mp // 2, mp % 2
    return (
        x,
        c,
        (dp, x * 2 + 1 - c),
        (dp, (1 - x) * 2 + c),
        (dp + 1 - 2 * (dp % 2), mp),
    )


def greet(peers):
    barrier = pltpu.get_barrier_semaphore()
    for peer in peers:
        pl.semaphore_signal(barrier, inc=1, device_id=peer, device_id_type=MESH)


def meet(count):
    pl.semaphore_wait(pltpu.get_barrier_semaphore(), count)


def remote(src, dst, send, recv, peer):
    return pltpu.make_async_remote_copy(
        src_ref=src, dst_ref=dst, send_sem=send, recv_sem=recv, device_id=peer, device_id_type=MESH
    )


def tiles(start, rows, step):
    def body(i, carry):
        step(pl.ds(pl.multiple_of(start + i * TILE, TILE), TILE))
        return carry

    lax.fori_loop(0, rows // TILE, body, 0)


class Reduce:
    STAGES = 5

    def __init__(self, left, right, low, part, mine, got, gx, gy, fx, fy, send, recv):
        self.left, self.right, self.low = left, right, low
        self.refs = (part, mine, got, gx, gy, fx, fy, send, recv)
        self.rows = mine.shape[2] // CHUNKS
        self.width = mine.shape[3]

    @staticmethod
    def scratch(rows, width, low, part=True):
        high = width - low
        return [pltpu.VMEM((2, 2, rows, width), BF16)] * part + [
            pltpu.VMEM((2, 2, rows, width), BF16),
            pltpu.VMEM((2, 2, rows, width), BF16),
            pltpu.VMEM((2, rows, low), BF16),
            pltpu.VMEM((2, rows, high), BF16),
            pltpu.VMEM((rows, high), BF16),
            pltpu.VMEM((rows, low), BF16),
            pltpu.SemaphoreType.DMA((Reduce.STAGES, CHUNKS)),
            pltpu.SemaphoreType.DMA((Reduce.STAGES, CHUNKS)),
        ]

    def lanes(self):
        return pl.ds(0, self.low), pl.ds(self.low, self.width - self.low)

    def copy(self, k, i):
        part, mine, got, gx, gy, fx, fy, send, recv = self.refs
        x, _, core_peer, x_peer, y_peer = neighbours()
        rows = pl.ds(k * self.rows, self.rows)
        low, high = self.lanes()
        s = [send.at[j, k] for j in range(self.STAGES)]
        r = [recv.at[j, k] for j in range(self.STAGES)]
        all_copies = (
            lambda: remote(part.at[:, :, rows], got.at[:, :, rows], s[0], r[0], core_peer),
            lambda: remote(mine.at[:, 1 - x, rows, low], gx.at[:, rows], s[1], r[1], x_peer),
            lambda: remote(mine.at[1, :, rows, high], gy.at[:, rows], s[2], r[2], y_peer),
            lambda: remote(mine.at[1, x, rows, low], fy.at[rows], s[3], r[3], y_peer),
            lambda: remote(mine.at[0, 1 - x, rows, high], fx.at[rows], s[4], r[4], x_peer),
        )
        return all_copies[i]()

    def produce(self, k, own):
        target = self.refs[1] if own else self.refs[0]
        core = neighbours()[1]
        core = core if own else 1 - core
        rows = pl.ds(k * self.rows, self.rows)
        depth = self.left.shape[4]

        def tile(j, carry):
            cols = pl.ds(pl.multiple_of(j * COLUMNS, COLUMNS), COLUMNS)
            left = self.left[:, :, core, rows, :].reshape(4 * self.rows, depth)
            product = dot(left, self.right[cols, :], 1, 1).astype(BF16)
            target[:, :, rows, cols] = product.reshape(2, 2, self.rows, COLUMNS)
            return carry

        lax.fori_loop(0, self.width // COLUMNS, tile, 0)

    def begin(self, k):
        self.copy(k, 0).start()

    def release(self, k):
        self.copy(k, 0).wait_send()

    def first(self, k):
        mine, got = self.refs[1:3]
        self.copy(k, 0).wait_recv()

        def add(i, carry):
            def step(rows):
                at = (i // 2, i % 2, rows)
                mine[at] = (mine[at].astype(F32) + got[at].astype(F32)).astype(BF16)

            tiles(k * self.rows, self.rows, step)
            return carry

        lax.fori_loop(0, 4, add, 0)
        self.copy(k, 1).start()
        self.copy(k, 2).start()

    def second(self, k):
        mine, _, gx, gy = self.refs[1:5]
        x = neighbours()[0]
        low, high = self.lanes()
        self.copy(k, 1).wait_recv()
        self.copy(k, 2).wait_recv()

        def step(rows):
            for i in range(2):
                at = (i, x, rows, low)
                mine[at] = (mine[at].astype(F32) + gx[i, rows].astype(F32)).astype(BF16)
                at = (0, i, rows, high)
                mine[at] = (mine[at].astype(F32) + gy[i, rows].astype(F32)).astype(BF16)

        tiles(k * self.rows, self.rows, step)
        self.copy(k, 3).start()
        self.copy(k, 4).start()

    def arrive(self, k):
        self.copy(k, 3).wait_recv()
        self.copy(k, 4).wait_recv()

    def take(self, rows):
        mine, fx, fy = self.refs[1], *self.refs[5:7]
        x = neighbours()[0]
        low, high = self.lanes()
        return jnp.concatenate(
            [
                mine[0, x, rows, low].astype(F32) + fy[rows].astype(F32),
                mine[0, x, rows, high].astype(F32) + fx[rows].astype(F32),
            ],
            -1,
        )

    def finish(self):
        for k in range(CHUNKS):
            for i in range(1, 5):
                self.copy(k, i).wait_send()


class Gather:
    STAGES = 9

    def __init__(self, mine, full, local, send, recv):
        self.refs = (mine, full, local, send, recv)
        self.rows = mine.shape[0] // CHUNKS
        self.half = mine.shape[1] // 2

    @staticmethod
    def scratch(rows, width):
        return [
            pltpu.VMEM((rows, width), BF16),
            pltpu.SemaphoreType.DMA((CHUNKS,)),
            pltpu.SemaphoreType.DMA((Gather.STAGES, CHUNKS)),
            pltpu.SemaphoreType.DMA((Gather.STAGES, CHUNKS)),
        ]

    def copy(self, k, i):
        mine, full, local, send, recv = self.refs
        x, c, core_peer, x_peer, y_peer = neighbours()
        rows = pl.ds(k * self.rows, self.rows)
        low, high = pl.ds(0, self.half), pl.ds(self.half, self.half)
        s = [send.at[j, k] for j in range(self.STAGES)]
        r = [recv.at[j, k] for j in range(self.STAGES)]

        def pass_on(j, at, peer):
            return lambda: remote(full.at[at], full.at[at], s[j], r[j], peer)

        all_copies = (
            lambda: pltpu.make_async_copy(mine.at[rows], full.at[0, x, c, rows], local.at[k]),
            lambda: remote(mine.at[rows, low], full.at[1, x, c, rows, low], s[0], r[0], y_peer),
            lambda: remote(mine.at[rows, high], full.at[0, x, c, rows, high], s[1], r[1], x_peer),
            lambda: remote(mine.at[rows], full.at[0, x, c, rows], s[2], r[2], core_peer),
            pass_on(3, (slice(None), x, c, rows, low), x_peer),
            lambda: remote(
                full.at[0, :, c, rows, high], full.at[1, :, c, rows, high], s[4], r[4], y_peer
            ),
            pass_on(5, (1, x, c, rows, low), core_peer),
            pass_on(6, (0, 1 - x, c, rows, high), core_peer),
            pass_on(7, (slice(None), 1 - x, c, rows, low), core_peer),
            pass_on(8, (1, slice(None), c, rows, high), core_peer),
        )
        return all_copies[i]()

    def begin(self, k):
        for i in (1, 2, 0, 3):
            self.copy(k, i).start()

    def second(self, k):
        self.copy(k, 0).wait()
        self.copy(k, 1).wait_recv()
        self.copy(k, 4).start()
        self.copy(k, 2).wait_recv()
        for i in (5, 6, 7):
            self.copy(k, i).start()

    def third(self, k):
        for i in (4, 5):
            self.copy(k, i).wait_recv()
            self.copy(k, i + 4).start()

    def finish(self):
        for k in range(CHUNKS):
            for i in (3, 6, 7, 8, 9):
                self.copy(k, i).wait_recv()
            for i in range(1, 10):
                self.copy(k, i).wait_send()


N_REDUCE = len(Reduce.scratch(32, 256, 128))


def nothing():
    pass


def leg(left, right, low, full, step, scratch, at_start=nothing, at_middle=nothing):
    reduce = Reduce(left, right, low, *scratch[:N_REDUCE])
    gather = Gather(scratch[N_REDUCE], full, *scratch[N_REDUCE + 1 :])
    mine = scratch[N_REDUCE]
    greet(neighbours()[2:])
    for k in range(CHUNKS):
        reduce.produce(k, False)
        if k == 0:
            meet(3)
        reduce.begin(k)
    for k in range(CHUNKS):
        reduce.produce(k, True)
        reduce.first(k)
    at_start()
    for k in range(CHUNKS):
        reduce.second(k)
    at_middle()

    def step_at(rows):
        mine[rows] = step(rows, reduce.take(rows)).astype(BF16)

    for k in range(CHUNKS):
        reduce.arrive(k)
        tiles(k * reduce.rows, reduce.rows, step_at)
        gather.begin(k)
    for k in range(CHUNKS):
        gather.second(k)
    for k in range(CHUNKS):
        gather.third(k)
    gather.finish()
    for k in range(CHUNKS):
        reduce.release(k)
    reduce.finish()


def attention_leg(
    left,
    packed,
    tokens,
    gain,
    cotangent,
    cot_part,
    cot_across,
    hidden,
    normed,
    cot_pair,
    cot_buffer,
    cot_in,
    cot_out,
    cot_send,
    cot_recv,
    *scratch
):
    def step(rows, total):
        h = tokens[rows].astype(F32) + total
        hidden[rows] = h
        return norm_parts(h)[0] * gain[...]

    x, core, core_peer = neighbours()[:3]
    own, share = cotangent.shape[0], cot_part.shape[0]

    def place(at_x, at_core):
        start = own + (at_x * 2 + at_core) * share
        return pl.ds(pl.multiple_of(start, share), share)

    sources = (cotangent, cot_part, cot_across)
    starts = (0, own, own + share)
    places = (pl.ds(0, own), place(x, core), place(1 - x, core))
    loads, stores, sends = [], [], []
    for i in range(3):
        held = cot_buffer.at[pl.ds(starts[i], sources[i].shape[0])]
        loads.append(pltpu.make_async_copy(sources[i], held, cot_in.at[i]))
        stores.append(pltpu.make_async_copy(held, cot_pair.at[places[i]], cot_out.at[i]))
        if i > 0:
            to = cot_pair.at[places[i]]
            sends.append(remote(sources[i], to, cot_send.at[i - 1], cot_recv.at[i - 1], core_peer))

    def at_start():
        for copy in loads + sends:
            copy.start()

    def at_middle():
        for load, store in zip(loads, stores):
            load.wait()
            store.start()

    depth = left.shape[4]
    right = packed.at[:, pl.ds(packed.shape[1] - depth, depth)]
    leg(left, right, right.shape[0] // 2, normed, step, scratch, at_start, at_middle)
    for copy in stores + sends:
        copy.wait()


def hidden_leg(left, right, hidden, cotangent, gain, grad_hidden, gain_grad, full, *scratch):
    gain_grad[...] = jnp.zeros_like(gain_grad)

    def step(rows, grad):
        hat, inv = norm_parts(hidden[rows])
        gain_grad[...] += jnp.sum(grad * hat, 0, keepdims=True)
        grad = cotangent[rows].astype(F32) + norm_back(grad, hat, inv, gain[...])
        grad_hidden[rows] = grad
        return grad

    leg(left, right, right.shape[0] // 2, full, step, scratch)


class SumGains:
    def __init__(self, parts, total, got, mid, others, send, recv, send_mp, recv_mp):
        self.refs = (parts, total, got, mid, others, send, recv, send_mp, recv_mp)
        self.n_dp, self.n_mp = parts.shape[0], others.shape[0] + 1

    @staticmethod
    def scratch(n_dp, n_mp):
        return [
            pltpu.VMEM((n_dp, 8, 128), F32),
            pltpu.VMEM((8, 128), F32),
            pltpu.VMEM((n_mp - 1, 8, 128), F32),
            pltpu.SemaphoreType.DMA((n_dp,)),
            pltpu.SemaphoreType.DMA((n_dp,)),
            pltpu.SemaphoreType.DMA((n_mp,)),
            pltpu.SemaphoreType.DMA((n_mp,)),
        ]

    def across(self, j):
        return (lax.rem(lax.axis_index("dp") + j, self.n_dp), lax.axis_index("mp"))

    def along(self, j):
        return (lax.axis_index("dp"), lax.rem(lax.axis_index("mp") + j, self.n_mp))

    def greet(self):
        barrier = pltpu.get_barrier_semaphore()

        def one(j, carry):
            pl.semaphore_signal(barrier, inc=1, device_id=self.across(j), device_id_type=MESH)
            return carry

        lax.fori_loop(1, self.n_dp, one, 0)
        greet([self.along(j) for j in range(1, self.n_mp)])

    def first(self, j):
        parts, _, got, _, _, send, recv = self.refs[:7]
        to = self.across(j)
        return remote(parts.at[to[0]], got.at[j], send.at[j], recv.at[j], to)

    def second(self, j):
        mid, others = self.refs[3:5]
        send, recv = self.refs[7:]
        return remote(mid, others.at[j - 1], send.at[j], recv.at[j], self.along(j))

    def begin(self):
        def start(j, carry):
            self.first(j).start()
            return carry

        lax.fori_loop(1, self.n_dp, start, 0)

    def pass_on(self):
        parts, _, got, mid = self.refs[:4]
        mid[...] = parts[lax.axis_index("dp")]

        def add(j, carry):
            self.first(j).wait()
            mid[...] += got[j]
            return carry

        lax.fori_loop(1, self.n_dp, add, 0)
        for j in range(1, self.n_mp):
            self.second(j).start()

    def finish(self):
        _, total, _, mid, others = self.refs[:5]
        result = mid[...]
        for j in range(1, self.n_mp):
            self.second(j).wait()
            result += others[j - 1]
        total[...] = result


def output_leg(
    left,
    packed,
    mlp_left,
    mlp_right,
    tokens,
    hidden,
    grad_hidden,
    gain,
    gain_parts,
    gate_up_grad,
    down_grad,
    input_grad,
    output,
    gain_total,
    gate,
    up,
    down,
    part,
    gain_grad,
    slots,
    gate_up_other,
    down_other,
    swap_send,
    swap_recv,
    *scratch
):
    low = scratch[2].shape[2]
    n = N_REDUCE - 1
    first = Reduce(left, packed.at[:, pl.ds(0, left.shape[4])], low, part, *scratch[:n])
    second = Reduce(mlp_left, mlp_right, low, part, *scratch[n : 2 * n])
    sums = SumGains(slots, gain_total, *scratch[2 * n :])
    y, y_peer = lax.axis_index("dp") % 2, neighbours()[4]
    half = gate.shape[0]
    mine, theirs = (pl.ds(pl.multiple_of(i * half, half), half) for i in (y, 1 - y))
    swaps = [
        remote(gate_up_grad.at[theirs], gate_up_other, swap_send.at[0], swap_recv.at[0], y_peer),
        remote(down_grad.at[theirs], down_other, swap_send.at[1], swap_recv.at[1], y_peer),
    ]

    def place(source, down_source, which):
        size = gate.shape[1] // 2
        cols = pl.ds(pl.multiple_of(which * size, 128), size)
        gate[:, cols] = source[:, :size].astype(F32)
        up[:, cols] = source[:, size:].astype(F32)
        down[cols, :] = down_source[...].T.astype(F32)

    def step_grad(rows):
        grad = first.take(rows)
        hat, inv = norm_parts(tokens[rows].astype(F32))
        gain_grad[...] += jnp.sum(grad * hat, 0, keepdims=True)
        input_grad[rows] = grad_hidden[rows] + norm_back(grad, hat, inv, gain[...])

    def step_output(rows):
        output[rows] = (hidden[rows] + second.take(rows)).astype(BF16)

    sums.greet()
    gain_grad[...] = jnp.zeros_like(gain_grad)
    slots[...] = gain_parts[...]
    for k in range(CHUNKS):
        first.produce(k, False)
        if k == 0:
            meet(sums.n_dp + sums.n_mp - 2)
        first.begin(k)
    for k in range(CHUNKS):
        first.produce(k, True)
        first.first(k)
    for copy in swaps:
        copy.start()
    for k in range(CHUNKS):
        first.release(k)
        second.produce(k, False)
        second.begin(k)
    for k in range(CHUNKS):
        first.second(k)
    for k in range(CHUNKS):
        second.produce(k, True)
        second.first(k)
    for k in range(CHUNKS):
        first.arrive(k)
        tiles(k * first.rows, first.rows, step_grad)
    owned = gain_grad.shape[1] // sums.n_dp
    for i in range(sums.n_dp):
        for j in range(-(-owned // 128)):
            size = min(128, owned - j * 128)
            at = i * owned + j * 128
            slots[i, j : j + 1, :size] = gain_grad[:, at : at + size]
    sums.begin()
    place(gate_up_grad.at[mine], down_grad.at[mine], y)
    for k in range(CHUNKS):
        second.second(k)
    sums.pass_on()
    for copy in swaps:
        copy.wait_recv()
    place(gate_up_other, down_other, 1 - y)
    for k in range(CHUNKS):
        second.arrive(k)
        tiles(k * second.rows, second.rows, step_output)
    sums.finish()
    for k in range(CHUNKS):
        second.release(k)
    for copy in swaps:
        copy.wait_send()
    first.finish()
    second.finish()


ANY = pl.BlockSpec(memory_space=pl.ANY)
VM = pl.BlockSpec(memory_space=pltpu.VMEM)


def call_leg(kernel, ident, name, in_specs, out_shape, out_specs, scratch, bytes_moved):
    return pl.pallas_call(
        kernel,
        out_shape=out_shape,
        in_specs=in_specs,
        out_specs=out_specs,
        scratch_shapes=scratch,
        name=name,
        cost_estimate=pl.CostEstimate(flops=0, bytes_accessed=bytes_moved, transcendentals=0),
        compiler_params=pltpu.CompilerParams(
            collective_id=ident, has_side_effects=True, vmem_limit_bytes=60 * MIB
        ),
    )


class Spread:
    STAGES = 4

    def __init__(self, mine, other, send, recv):
        self.refs = (mine, other, send, recv)
        self.rows = mine.shape[0] // 4 // CHUNKS

    @staticmethod
    def scratch():
        return [
            pltpu.SemaphoreType.DMA((Spread.STAGES, CHUNKS)),
            pltpu.SemaphoreType.DMA((Spread.STAGES, CHUNKS)),
        ]

    def copy(self, k, i):
        mine, other, send, recv = self.refs
        x, c, core_peer, x_peer, y_peer = neighbours()

        def rows(at_x):
            start = (at_x * 2 + c) * (mine.shape[0] // 4) + k * self.rows
            return pl.ds(pl.multiple_of(start, self.rows), self.rows)

        at = rows(1 - x) if i == 3 else rows(x)
        peer = (y_peer, x_peer, core_peer, core_peer)[i]
        source = mine if i == 0 else other
        return remote(source.at[at], other.at[at], send.at[i, k], recv.at[i, k], peer)

    def pass_on(self, k):
        self.copy(k, 0).wait_recv()
        self.copy(k, 1).start()
        self.copy(k, 2).start()

    def pass_last(self, k):
        self.copy(k, 1).wait_recv()
        self.copy(k, 3).start()

    def finish(self):
        for k in range(CHUNKS):
            for i in (2, 3):
                self.copy(k, i).wait_recv()
            for i in range(4):
                self.copy(k, i).wait_send()


def front(
    q,
    k,
    v,
    o,
    gain,
    docs,
    tokens,
    gate,
    up,
    down,
    full,
    gains,
    docs_other,
    normed,
    gate_up_mine,
    down_mine,
    stage,
    gate_up_stage,
    down_stage,
    tokens_mine,
    tokens_other,
    gate_in,
    up_in,
    down_in,
    local,
    swap,
    gain_send,
    gain_recv,
    ring_send,
    ring_recv,
    *scratch
):
    dp, mp = lax.axis_index("dp"), lax.axis_index("mp")
    _, _, core_peer, x_peer, y_peer = neighbours()
    n_dp = gains.shape[0]
    n_slabs = n_dp // 2
    y, z = dp % 2, dp // 2
    rows = q.shape[0]
    spread = Spread(tokens, tokens_other, *scratch)

    def peer(j):
        return (lax.rem(dp + j, n_dp), mp)

    def greet_one(j, carry):
        barrier = pltpu.get_barrier_semaphore()
        pl.semaphore_signal(barrier, inc=1, device_id=peer(j), device_id_type=MESH)
        return carry

    lax.fori_loop(1, n_dp, greet_one, 0)
    greet([core_peer, x_peer])
    loads = [
        pltpu.make_async_copy(source, target, local.at[i])
        for i, (source, target) in enumerate(
            ((tokens, tokens_mine), (gate, gate_in), (up, up_in), (down, down_in))
        )
    ]
    for load in loads:
        load.start()
    widths = [w.shape[1] // 2 for w in (q, k, v)]
    first = sum(widths)

    def fill(target, row, which):
        at = 0
        for w, size in zip((q, k, v), widths):
            cols = pl.ds(pl.multiple_of(which * size, 128), size)
            target[pl.ds(row, rows), at : at + size] = w[:, cols].astype(BF16)
            at += size
        size = o.shape[0] // 2
        part = o[pl.ds(pl.multiple_of(which * size, 128), size), :].astype(BF16)
        target[pl.ds(row, rows), first : first + size] = part.T

    def block(slab, pair):
        return pl.ds(pl.multiple_of((slab * 2 + pair) * rows, rows), rows)

    swapped = remote(stage, full.at[block(z, y)], swap.at[0, 0], swap.at[1, 0], y_peer)
    docs_swapped = remote(docs, docs_other, swap.at[0, 1], swap.at[1, 1], y_peer)
    mine = pl.ds(pl.multiple_of(y * rows, rows), rows)
    gate_up_swapped = remote(
        gate_up_stage, gate_up_mine.at[mine], swap.at[0, 2], swap.at[1, 2], y_peer
    )
    down_swapped = remote(down_stage, down_mine.at[mine], swap.at[0, 3], swap.at[1, 3], y_peer)

    def ring(step, i):
        slab = lax.rem(z - step + n_slabs, n_slabs)
        at = full.at[block(slab, y if i == 0 else 1 - y)]
        to = (lax.rem(dp + 2, n_dp), mp)
        return remote(at, at, ring_send.at[step, i], ring_recv.at[step, i], to)

    def ring_next(step, i):
        slab = lax.rem(z - step - 1 + 2 * n_slabs, n_slabs)
        at = full.at[block(slab, y if i == 0 else 1 - y)]
        to = (lax.rem(dp + 2, n_dp), mp)
        came = remote(at, at, ring_send.at[step, i], ring_recv.at[step, i], to)
        came.wait_recv()
        if isinstance(step, int) and step + 1 >= n_slabs - 1:
            return
        ring(step + 1, i).start()

    def gain_to(j):
        return remote(gain, gains.at[dp], gain_send.at[j], gain_recv.at[j], peer(j))

    def share(j, carry):
        gain_to(j).start()
        return carry

    def settle(j, carry):
        gain_to(j).wait()
        return carry

    def fill_mlp(gate_up_to, down_to, row, which):
        size = gate.shape[1] // 2
        cols = pl.ds(pl.multiple_of(which * size, 128), size)
        gate_up_to[pl.ds(row, rows), :size] = gate_in[:, cols].astype(BF16)
        gate_up_to[pl.ds(row, rows), size:] = up_in[:, cols].astype(BF16)
        down_to[pl.ds(row, rows), :] = down_in[cols, :].astype(BF16).T

    fill(stage, 0, 1 - y)
    meet(n_dp - 1 + 2)
    swapped.start()
    fill(full, block(z, y).start, y)
    ring(0, 0).start()
    docs_swapped.start()
    lax.fori_loop(1, n_dp, share, 0)
    for c in range(CHUNKS):
        spread.copy(c, 0).start()
    gains[dp] = gain[...]
    for load in loads[1:]:
        load.wait()
    fill_mlp(gate_up_stage, down_stage, 0, 1 - y)
    gate_up_swapped.start()
    down_swapped.start()
    swapped.wait_recv()
    ring(0, 1).start()
    lax.fori_loop(1, n_dp, settle, 0)
    owned = gain_rows_of(full.shape[0] // n_dp)
    gain_row = jnp.concatenate(
        [gains[i, j : j + 1, :size] for i in range(n_dp) for j, size in owned], -1
    )

    def norm(source, base, start, count):
        def step(at):
            hat = norm_parts(source[at].astype(F32))[0]
            to = pl.ds(pl.multiple_of(base + at.start, TILE), TILE)
            normed[to] = (hat * gain_row).astype(BF16)

        tiles(start, count, step)

    total = tokens.shape[0]
    quarter = total // 4
    loads[0].wait()
    work = [functools.partial(norm, tokens_mine, 0, i * quarter, quarter) for i in range(4)]
    work[0:0] = [functools.partial(fill_mlp, gate_up_mine, down_mine, mine.start, y)]
    for c in range(CHUNKS):
        work.append(functools.partial(spread.pass_on, c))
    for c in range(CHUNKS):
        work.append(functools.partial(spread.pass_last, c))
    events = [(step, i) for step in range(n_slabs - 1) for i in range(2)]
    if len(events) <= len(work):
        for n, event in enumerate(events):
            ring_next(*event)
            if n < 2:
                work.pop(0)()
                work.pop(0)()
            elif n < 4:
                for _ in range(2):
                    if work:
                        work.pop(0)()
        for job in work:
            job()
    else:
        for job in work:
            job()

        def turn(step, carry):
            for i in range(2):
                ring_next(step, i)
            return carry

        lax.fori_loop(0, n_slabs - 2, turn, 0)
        for i in range(2):
            ring_next(n_slabs - 2, i)
    spread.finish()
    norm(tokens_other, total, 0, total)
    docs_swapped.wait()
    swapped.wait_send()
    gate_up_swapped.wait()
    down_swapped.wait()

    def sent(step, carry):
        for i in range(2):
            ring(step, i).wait_send()
        return carry

    lax.fori_loop(0, n_slabs - 1, sent, 0)


def gain_rows_of(size):
    return [(j, min(128, size - j * 128)) for j in range(-(-size // 128))]


def finish_attention(grads, q, k, v, o, other, send, recv):
    dp, mp = lax.axis_index("dp"), lax.axis_index("mp")
    y, y_peer = dp % 2, (dp + 1 - 2 * (dp % 2), mp)
    rows = q.shape[0]
    greet([y_peer])
    meet(1)
    theirs = pl.multiple_of((1 - y) * rows, rows)
    swapped = remote(grads.at[pl.ds(theirs, rows)], other, send, recv, y_peer)
    swapped.start()

    def place(source, row, which):
        at = 0
        for w in (q, k, v):
            size = w.shape[1] // 2
            cols = pl.ds(pl.multiple_of(which * size, 128), size)
            w[:, cols] = source[pl.ds(row, rows), at : at + size].astype(F32)
            at += size
        size = o.shape[0] // 2
        part = source[pl.ds(row, rows), at : at + size].astype(F32).T
        o[pl.ds(pl.multiple_of(which * size, 128), size), :] = part

    place(grads, pl.multiple_of(y * rows, rows), y)
    swapped.wait_recv()
    place(other, 0, 1 - y)
    swapped.wait_send()


QUERY_BLOCK = 256
LONGEST = 512


def rolled(values):
    return pltpu.roll(values, HEAD_WIDTH // 2, 1)


def head_norm(raw, h):
    return norm_parts(raw[:, h * HEAD_WIDTH : (h + 1) * HEAD_WIDTH])


def rope_into(target, at, normed, cosine, sine):
    target[:, at : at + HEAD_WIDTH] = (normed * cosine[...] + rolled(normed) * sine[...]).astype(
        BF16
    )


def blocks_of(length):
    for start in range(0, length, QUERY_BLOCK):
        first = max(0, start - LONGEST)
        yield slice(start, start + QUERY_BLOCK), slice(first, start + QUERY_BLOCK)


def weights_of(query, key, starts, rows, cols):
    scores = dot(query, key, 1, 1) * HEAD_WIDTH ** (-0.5)
    query_index = rows.start + lax.broadcasted_iota(jnp.int32, scores.shape, 0)
    key_index = cols.start + lax.broadcasted_iota(jnp.int32, scores.shape, 1)
    allowed = (key_index <= query_index) & (key_index >= starts[rows])
    scores = jnp.where(allowed, scores, MASKED)
    exponent = jnp.exp(scores - jnp.max(scores, -1, keepdims=True))
    return exponent / jnp.sum(exponent, -1, keepdims=True)


def attend_forward(raw, cosine, sine, starts, gain_query, gain_key, out, q, k):
    for h in range(GROUP):
        rope_into(q, h * HEAD_WIDTH, head_norm(raw, h)[0] * gain_query[...], cosine, sine)
    rope_into(k, 0, head_norm(raw, GROUP)[0] * gain_key[...], cosine, sine)
    at = (GROUP + 1) * HEAD_WIDTH
    for rows, cols in blocks_of(raw.shape[0]):
        for h in range(GROUP):
            lanes = slice(h * HEAD_WIDTH, (h + 1) * HEAD_WIDTH)
            weights = weights_of(q[rows, lanes], k[cols], starts, rows, cols).astype(BF16)
            value = raw[cols, at : at + HEAD_WIDTH].astype(BF16)
            out[rows, lanes] = dot(weights, value).astype(BF16)


def attend_backward(
    raw, cosine, sine, starts, gain_query, gain_key, grad, out, gains, q, k, v, dq, dk, dv
):
    factor = HEAD_WIDTH ** (-0.5)
    at = (GROUP + 1) * HEAD_WIDTH
    for h in range(GROUP):
        rope_into(q, h * HEAD_WIDTH, head_norm(raw, h)[0] * gain_query[...], cosine, sine)
    rope_into(k, 0, head_norm(raw, GROUP)[0] * gain_key[...], cosine, sine)
    v[...] = raw[:, at : at + HEAD_WIDTH].astype(BF16)
    dk[...] = jnp.zeros_like(dk)
    dv[...] = jnp.zeros_like(dv)
    for rows, cols in blocks_of(raw.shape[0]):
        for h in range(GROUP):
            lanes = slice(h * HEAD_WIDTH, (h + 1) * HEAD_WIDTH)
            weights = weights_of(q[rows, lanes], k[cols], starts, rows, cols)
            grad_weights = dot(grad[rows, lanes], v[cols], 1, 1)
            inner = jnp.sum(weights * grad_weights, -1, keepdims=True)
            grad_scores = (weights * (grad_weights - inner)).astype(BF16)
            dq[rows, lanes] = dot(grad_scores, k[cols]) * factor
            dk[cols] += dot(grad_scores, q[rows, lanes], 0, 0) * factor
            dv[cols] += dot(weights.astype(BF16), grad[rows, lanes], 0, 0)
    gains[...] = jnp.zeros_like(gains)

    def undo(rot_grad, h, gain, row):
        normed_grad = rot_grad * cosine[...] - rolled(rot_grad) * sine[...]
        hat, inv = head_norm(raw, h)
        gains[0, row : row + 1] += jnp.sum(normed_grad * hat, 0, keepdims=True)
        lanes = slice(h * HEAD_WIDTH, (h + 1) * HEAD_WIDTH)
        out[:, lanes] = norm_back(normed_grad, hat, inv, gain[...]).astype(BF16)

    for h in range(GROUP):
        undo(dq[:, h * HEAD_WIDTH : (h + 1) * HEAD_WIDTH], h, gain_query, 0)
    undo(dk[...], GROUP, gain_key, 1)
    out[:, at : at + HEAD_WIDTH] = dv[...].astype(BF16)


def call_attention(kernel, length, rows, out_shape, out_specs, scratch, flops):
    def seq(cols):
        return pl.BlockSpec((length, cols), lambda i: (i, 0))

    gain = pl.BlockSpec((1, HEAD_WIDTH), lambda i: (0, 0))
    specs = [seq((GROUP + 2) * HEAD_WIDTH), seq(HEAD_WIDTH), seq(HEAD_WIDTH), seq(1), gain, gain]
    if len(scratch) > 2:
        specs.append(seq(GROUP * HEAD_WIDTH))
    return pl.pallas_call(
        kernel,
        out_shape=out_shape,
        grid=(rows // length,),
        in_specs=specs,
        out_specs=out_specs,
        scratch_shapes=scratch,
        name=kernel.__name__,
        cost_estimate=pl.CostEstimate(
            flops=flops, bytes_accessed=8 * MIB, transcendentals=rows * length * GROUP // 2
        ),
        compiler_params=pltpu.CompilerParams(
            dimension_semantics=("arbitrary",), vmem_limit_bytes=56 * MIB
        ),
    )


def on_device(
    tokens,
    documents,
    cotangent,
    attn_gain,
    query_gain,
    key_norm_scale,
    query_weight,
    key_projection,
    value_projection,
    output_weight,
    mlp_gain,
    gate_weight,
    up_weight,
    down_weight,
):
    n_dp = lax.axis_size("dp")
    dp, mp = lax.axis_index("dp"), lax.axis_index("mp")
    y = dp % 2
    slabs = [[i + 2 * k for k in range(n_dp // 2)] for i in range(2)]
    rows, width = tokens.shape
    seq_length = documents.shape[1]
    seqs = 2 * documents.shape[0]
    share = rows // 4
    head = HEAD_WIDTH
    query_cols, key_cols, hidden_cols = (
        query_weight.shape[1] // 2,
        key_projection.shape[1] // 2,
        gate_weight.shape[1] // 2,
    )
    attn_cols = query_cols + 2 * key_cols

    def y_swap(values):
        return lax.ppermute(values, "dp", [(i, i ^ 1) for i in range(n_dp)])

    def mp_swap(values, bit):
        return lax.ppermute(values, "mp", [(i, i ^ bit) for i in range(4)])

    def in_order(where, mine, other, axis):
        return jnp.where(
            where == 0,
            jnp.concatenate([mine, other], axis),
            jnp.concatenate([other, mine], axis),
        )

    def half(values, which, axis):
        size = values.shape[axis] // 2
        return lax.dynamic_slice_in_dim(values, which * size, size, axis)

    def slab_gather(values):
        return lax.all_gather(values, "dp", axis=0, tiled=True, axis_index_groups=slabs)

    def slab_scatter(values):
        return lax.psum_scatter(
            values, "dp", scatter_dimension=0, tiled=True, axis_index_groups=slabs
        )

    n_gain, n_head = attn_gain.shape[0], query_gain.shape[0]

    def gain_rows(*parts):
        lead = parts[0].shape[:-1]
        pad = [(0, 0)] * len(lead)
        rows_of = jnp.concatenate(
            [
                jnp.pad(part, pad + [(0, -part.shape[-1] % 128)]).reshape(*lead, -1, 128)
                for part in parts
            ],
            -2,
        )
        return jnp.pad(rows_of, pad + [(0, 8 - rows_of.shape[-2]), (0, 0)])

    def gain_parts_of(rows_of):
        lead, parts, at = rows_of.shape[:-2], [], 0
        for size in (n_gain, n_gain, n_head, n_head):
            n = -(-size // 128)
            part = rows_of[..., at : at + n, :].reshape(*lead, n * 128)
            parts.append(part[..., :size])
            at += n
        return parts

    my_gains = gain_rows(
        *(g.astype(BF16).astype(F32) for g in (attn_gain, mlp_gain, query_gain, key_norm_scale))
    )
    model_rows = query_weight.shape[0]
    pack_cols = attn_cols + query_cols
    pair_rows = 2 * rows
    n_slabs = n_dp // 2
    attn_full, gains, docs_other, normed_one, mlp_mine, down_mine = call_leg(
        front,
        3,
        "front",
        [VM] * 6 + [ANY] * 4,
        (
            jax.ShapeDtypeStruct((width, pack_cols), BF16),
            jax.ShapeDtypeStruct((n_dp, 8, 128), F32),
            jax.ShapeDtypeStruct(documents.shape, jnp.int32),
            jax.ShapeDtypeStruct((pair_rows, width), BF16),
            jax.ShapeDtypeStruct((2 * model_rows, 2 * hidden_cols), BF16),
            jax.ShapeDtypeStruct((2 * model_rows, hidden_cols), BF16),
        ),
        (VM,) * 6,
        [
            pltpu.VMEM((model_rows, pack_cols), BF16),
            pltpu.VMEM((model_rows, 2 * hidden_cols), BF16),
            pltpu.VMEM((model_rows, hidden_cols), BF16),
            pltpu.VMEM((rows, width), BF16),
            pltpu.VMEM((rows, width), BF16),
            pltpu.VMEM(gate_weight.shape, F32),
            pltpu.VMEM(up_weight.shape, F32),
            pltpu.VMEM(down_weight.shape, F32),
            pltpu.SemaphoreType.DMA((4,)),
            pltpu.SemaphoreType.DMA((2, 4)),
            pltpu.SemaphoreType.DMA((n_dp,)),
            pltpu.SemaphoreType.DMA((n_dp,)),
            pltpu.SemaphoreType.DMA((n_slabs, 2)),
            pltpu.SemaphoreType.DMA((n_slabs, 2)),
        ]
        + Spread.scratch(),
        250 * MIB,
    )(
        query_weight,
        key_projection,
        value_projection,
        output_weight,
        my_gains,
        documents,
        tokens,
        gate_weight,
        up_weight,
        down_weight,
    )

    cot_part = lax.dynamic_slice_in_dim(cotangent, mp * share, share, 0)
    cot_part, _ = lax.optimization_barrier((cot_part, docs_other))
    cot_part = y_swap(cot_part)
    gate_up_full = slab_gather(mlp_mine)
    down_full = slab_gather(down_mine)
    gain_one, gain_two, gain_query, gain_key = (g.reshape(1, -1) for g in gain_parts_of(gains))
    docs = jnp.concatenate([documents, docs_other], 0)
    tokens_share = lax.dynamic_slice_in_dim(tokens, mp * share, share, 0)
    cot_share = lax.dynamic_slice_in_dim(cotangent, mp * share, share, 0)

    raw = dot(normed_one, attn_full[:, :attn_cols])
    starts = sum((docs < i).sum(1, keepdims=True) * (docs == i) for i in range(1, 4))
    positions = (jnp.arange(seq_length, dtype=jnp.int32)[None] - starts).reshape(pair_rows)
    cosine, sine = rope_tables(positions, head)
    starts = starts.reshape(pair_rows, 1).astype(jnp.int32)
    raw, cot_part = lax.optimization_barrier((raw, cot_part))
    cot_across = mp_swap(cot_part, 2)
    attention_args = (raw, cosine, sine, starts, gain_query, gain_key)
    pair_flops = pair_rows * seq_length * query_cols
    attended = call_attention(
        attend_forward,
        seq_length,
        pair_rows,
        jax.ShapeDtypeStruct((pair_rows, query_cols), BF16),
        pl.BlockSpec((seq_length, query_cols), lambda i: (i, 0)),
        [pltpu.VMEM((seq_length, query_cols), BF16), pltpu.VMEM((seq_length, head), BF16)],
        2 * pair_flops,
    )(*attention_args)
    attended, cot_across = lax.optimization_barrier((attended, cot_across))

    def grouped(cols):
        return (2, 2, 2, share, cols)

    half_width = width // 2
    leg_scratch = Reduce.scratch(share, width, half_width) + Gather.scratch(share, width)
    hidden, normed_two, cot_pair = call_leg(
        attention_leg,
        0,
        "attention_leg",
        [VM] * 4 + [ANY] * 3,
        (
            jax.ShapeDtypeStruct((share, width), F32),
            jax.ShapeDtypeStruct(grouped(width), BF16),
            jax.ShapeDtypeStruct((pair_rows, width), BF16),
        ),
        (VM, ANY, ANY),
        [
            pltpu.VMEM((rows + 2 * share, width), BF16),
            pltpu.SemaphoreType.DMA((3,)),
            pltpu.SemaphoreType.DMA((3,)),
            pltpu.SemaphoreType.DMA((2,)),
            pltpu.SemaphoreType.DMA((2,)),
        ]
        + leg_scratch,
        200 * MIB,
    )(
        attended.reshape(grouped(query_cols)),
        attn_full,
        tokens_share,
        gain_two,
        cotangent,
        cot_part,
        cot_across,
    )
    normed_two = normed_two.reshape(pair_rows, width)

    gate_up = dot(normed_two, gate_up_full)
    gate_pre, up_pre = gate_up[:, :hidden_cols], gate_up[:, hidden_cols:]
    sigmoid = jax.nn.sigmoid(gate_pre)
    swish = gate_pre * sigmoid
    active = (swish * up_pre).astype(BF16)
    down_part = dot(cot_pair, active, 0, 0).astype(BF16)
    down_grad = slab_scatter(down_part)
    cot_late, _ = lax.optimization_barrier((cot_pair, down_part))
    grad_active = dot(cot_late, down_full)
    grad_gate = (grad_active * up_pre * sigmoid * (1.0 + gate_pre * (1.0 - sigmoid))).astype(BF16)
    grad_up = (grad_active * swish).astype(BF16)
    grad_gate_up = jnp.concatenate([grad_gate, grad_up], 1)
    gate_up_part = dot(normed_two, grad_gate_up, 0, 0).astype(BF16)
    gate_up_grad = slab_scatter(gate_up_part)
    grad_gate_up, _, _ = lax.optimization_barrier((grad_gate_up, gate_up_part, down_part))
    grad_hidden, mlp_gain_part, grad_hidden_low = call_leg(
        hidden_leg,
        1,
        "hidden_leg",
        [VM] * 5,
        (
            jax.ShapeDtypeStruct((share, width), F32),
            jax.ShapeDtypeStruct((1, width), F32),
            jax.ShapeDtypeStruct(grouped(width), BF16),
        ),
        (VM, VM, ANY),
        leg_scratch,
        200 * MIB,
    )(
        grad_gate_up.reshape(grouped(2 * hidden_cols)),
        gate_up_full,
        hidden,
        cot_share,
        gain_two,
    )
    grad_hidden_low = grad_hidden_low.reshape(pair_rows, width)

    output_grad = dot(grad_hidden_low, attended, 0, 0).astype(BF16)
    grad_attended = dot(grad_hidden_low, attn_full[:, attn_cols:]).astype(BF16)
    raw_grad, head_gain_parts = call_attention(
        attend_backward,
        seq_length,
        pair_rows,
        (
            jax.ShapeDtypeStruct((pair_rows, attn_cols), BF16),
            jax.ShapeDtypeStruct((seqs, 8, head), F32),
        ),
        (
            pl.BlockSpec((seq_length, attn_cols), lambda i: (i, 0)),
            pl.BlockSpec((1, 8, head), lambda i: (i, 0, 0)),
        ),
        [
            pltpu.VMEM((seq_length, query_cols), BF16),
            pltpu.VMEM((seq_length, head), BF16),
            pltpu.VMEM((seq_length, head), BF16),
            pltpu.VMEM((seq_length, query_cols), F32),
            pltpu.VMEM((seq_length, head), F32),
            pltpu.VMEM((seq_length, head), F32),
        ],
        5 * pair_flops,
    )(*attention_args, grad_attended)
    head_gain_parts = head_gain_parts.sum(0)
    attn_grad = jnp.concatenate([dot(normed_one, raw_grad, 0, 0).astype(BF16), output_grad], 1)
    attn_grad, raw_grad, gate_up_grad, down_grad = lax.optimization_barrier(
        (attn_grad, raw_grad, gate_up_grad, down_grad)
    )
    attn_grad = slab_scatter(attn_grad)

    gain_parts = gain_rows(
        jnp.zeros((n_dp, n_gain), F32),
        mlp_gain_part.reshape(n_dp, n_gain),
        head_gain_parts[0].reshape(n_dp, n_head),
        head_gain_parts[1].reshape(n_dp, n_head),
    )
    low = 3 * width // 4
    input_grad, layer_output, gain_sums, gate_grad, up_grad, down_grad = call_leg(
        output_leg,
        2,
        "output_leg",
        [VM] * 11,
        (
            jax.ShapeDtypeStruct((share, width), F32),
            jax.ShapeDtypeStruct((share, width), BF16),
            jax.ShapeDtypeStruct((8, 128), F32),
            jax.ShapeDtypeStruct(gate_weight.shape, F32),
            jax.ShapeDtypeStruct(up_weight.shape, F32),
            jax.ShapeDtypeStruct(down_weight.shape, F32),
        ),
        (VM,) * 6,
        [
            pltpu.VMEM((2, 2, share, width), BF16),
            pltpu.VMEM((1, width), F32),
            pltpu.VMEM((n_dp, 8, 128), F32),
            pltpu.VMEM((model_rows, 2 * hidden_cols), BF16),
            pltpu.VMEM((model_rows, hidden_cols), BF16),
            pltpu.SemaphoreType.DMA((2,)),
            pltpu.SemaphoreType.DMA((2,)),
        ]
        + Reduce.scratch(share, width, low, False) * 2
        + SumGains.scratch(n_dp, 4),
        200 * MIB,
    )(
        raw_grad.reshape(grouped(attn_cols)),
        attn_full,
        active.reshape(grouped(hidden_cols)),
        down_full,
        tokens_share,
        hidden,
        grad_hidden,
        gain_one,
        gain_parts,
        gate_up_grad,
        down_grad,
    )

    query_grad, key_grad, value_grad, output_grad = call_leg(
        finish_attention,
        5,
        "finish_attention",
        [VM],
        tuple(
            jax.ShapeDtypeStruct(w.shape, F32)
            for w in (query_weight, key_projection, value_projection, output_weight)
        ),
        (VM,) * 4,
        [
            pltpu.VMEM((model_rows, pack_cols), BF16),
            pltpu.SemaphoreType.DMA,
            pltpu.SemaphoreType.DMA,
        ],
        3 * MIB,
    )(attn_grad)
    attn_gain_grad, mlp_gain_grad, query_gain_grad, key_gain_grad = gain_parts_of(gain_sums)
    return (
        layer_output,
        input_grad,
        attn_gain_grad,
        query_gain_grad,
        key_gain_grad,
        query_grad,
        key_grad,
        value_grad,
        output_grad,
        mlp_gain_grad,
        gate_grad,
        up_grad,
        down_grad,
    )


def solution(mesh):
    in_specs = (
        P("dp", None),
        P("dp", None),
        P("dp", None),
        P("dp"),
        P("dp"),
        P("dp"),
        P("dp", "mp"),
        P("dp", "mp"),
        P("dp", "mp"),
        P("mp", "dp"),
        P("dp"),
        P("dp", "mp"),
        P("dp", "mp"),
        P("mp", "dp"),
    )
    out_specs = (
        P(("dp", "mp"), None),
        P(("dp", "mp"), None),
        P("dp"),
        P("dp"),
        P("dp"),
        P("dp", "mp"),
        P("dp", "mp"),
        P("dp", "mp"),
        P("mp", "dp"),
        P("dp"),
        P("dp", "mp"),
        P("dp", "mp"),
        P("mp", "dp"),
    )
    return jax.shard_map(
        on_device, mesh=mesh, in_specs=in_specs, out_specs=out_specs, check_vma=False
    )
```

```python
import functools

import jax
import jax.numpy as jnp
from jax import lax
from jax.experimental import pallas as pl
from jax.experimental.pallas import tpu as pltpu
from jax.sharding import PartitionSpec as P

QUERY_HEADS = 16
KEY_VALUE_HEADS = 8
HEAD_WIDTH = 128
GROUP = QUERY_HEADS // KEY_VALUE_HEADS

EPSILON = 1e-06
MASKED = -1e30
MESH = pl.DeviceIdType.MESH
F32 = jnp.float32
BF16 = jnp.bfloat16
MIB = 2**20


def rope_tables(positions, head_size):
    middle = head_size // 2
    frequency = jnp.power(1000000.0, -2.0 * jnp.arange(middle, dtype=F32) / head_size)
    angles = positions.astype(F32)[:, None] * frequency[None, :]
    cosine_table = jnp.cos(angles)
    sine_table = jnp.sin(angles)
    return (
        jnp.concatenate([cosine_table, cosine_table], -1),
        jnp.concatenate([-sine_table, sine_table], -1),
    )


def norm_parts(values):
    scaling = lax.rsqrt(jnp.mean(values * values, -1, keepdims=True) + EPSILON)
    return (values * scaling, scaling)


def norm_back(grad_normed, normed_hat, scaling, gains):
    scaled = grad_normed * gains
    return scaling * (scaled - normed_hat * jnp.mean(scaled * normed_hat, -1, keepdims=True))


def dot(left, right, left_dim=1, right_dim=0):
    return lax.dot_general(
        left, right, (((left_dim,), (right_dim,)), ((), ())), preferred_element_type=F32
    )


CHUNKS = 4
FEW = 2
TILE = 32
COLUMNS = 512


def neighbours():
    dp, mp = lax.axis_index("dp"), lax.axis_index("mp")
    x, c = mp // 2, mp % 2
    return (
        x,
        c,
        (dp, x * 2 + 1 - c),
        (dp, (1 - x) * 2 + c),
        (dp + 1 - 2 * (dp % 2), mp),
    )


def greet(peers):
    barrier = pltpu.get_barrier_semaphore()
    for peer in peers:
        pl.semaphore_signal(barrier, inc=1, device_id=peer, device_id_type=MESH)


def meet(count):
    pl.semaphore_wait(pltpu.get_barrier_semaphore(), count)


def remote(src, dst, send, recv, peer):
    return pltpu.make_async_remote_copy(
        src_ref=src, dst_ref=dst, send_sem=send, recv_sem=recv, device_id=peer, device_id_type=MESH
    )


def tiles(start, rows, step):
    def body(i, carry):
        step(pl.ds(pl.multiple_of(start + i * TILE, TILE), TILE))
        return carry

    lax.fori_loop(0, rows // TILE, body, 0)


class Reduce:
    STAGES = 5

    def __init__(self, left, right, low, part, mine, got, gx, gy, fx, fy, send, recv, load=None):
        self.left, self.right, self.low, self.load = left, right, low, load
        self.refs = (part, mine, got, gx, gy, fx, fy, send, recv)
        self.chunks = send.shape[1]
        self.rows = mine.shape[2] // self.chunks
        self.width = mine.shape[3]

    @staticmethod
    def scratch(rows, width, low, chunks=CHUNKS):
        high = width - low
        return [
            pltpu.VMEM((2, 2, rows, width), BF16),
            pltpu.VMEM((2, 2, rows, width), BF16),
            pltpu.VMEM((2, 2, rows, width), BF16),
            pltpu.VMEM((2, rows, low), BF16),
            pltpu.VMEM((2, rows, high), BF16),
            pltpu.VMEM((rows, high), BF16),
            pltpu.VMEM((rows, low), BF16),
            pltpu.SemaphoreType.DMA((Reduce.STAGES, chunks)),
            pltpu.SemaphoreType.DMA((Reduce.STAGES, chunks)),
        ]

    def lanes(self):
        return pl.ds(0, self.low), pl.ds(self.low, self.width - self.low)

    def load_left(self, k, own):
        source, _, sems, _ = self.load
        core = neighbours()[1]
        at = (slice(None), slice(None), core if own else 1 - core, pl.ds(k * self.rows, self.rows))
        return pltpu.make_async_copy(source.at[at], self.left.at[at], sems.at[int(own), k])

    def load_right(self, j):
        _, source, _, sems = self.load
        at = pl.ds(pl.multiple_of(j * COLUMNS, COLUMNS), COLUMNS)
        return pltpu.make_async_copy(source.at[at], self.right.at[at], sems.at[j])

    def start_loads(self):
        self.load_left(0, False).start()
        for j in range(self.width // COLUMNS):
            self.load_right(j).start()
        self.load_left(0, True).start()
        for k in range(1, self.chunks):
            for own in (False, True):
                self.load_left(k, own).start()

    def copy(self, k, i):
        part, mine, got, gx, gy, fx, fy, send, recv = self.refs
        x, _, core_peer, x_peer, y_peer = neighbours()
        rows = pl.ds(k * self.rows, self.rows)
        low, high = self.lanes()
        s = [send.at[j, k] for j in range(self.STAGES)]
        r = [recv.at[j, k] for j in range(self.STAGES)]
        all_copies = (
            lambda: remote(part.at[:, :, rows], got.at[:, :, rows], s[0], r[0], core_peer),
            lambda: remote(mine.at[:, 1 - x, rows, low], gx.at[:, rows], s[1], r[1], x_peer),
            lambda: remote(mine.at[1, :, rows, high], gy.at[:, rows], s[2], r[2], y_peer),
            lambda: remote(mine.at[1, x, rows, low], fy.at[rows], s[3], r[3], y_peer),
            lambda: remote(mine.at[0, 1 - x, rows, high], fx.at[rows], s[4], r[4], x_peer),
        )
        return all_copies[i]()

    def produce(self, k, own):
        target = self.refs[1] if own else self.refs[0]
        core = neighbours()[1]
        core = core if own else 1 - core
        rows = pl.ds(k * self.rows, self.rows)
        depth = self.left.shape[4]
        if self.load is not None:
            self.load_left(k, own).wait()

        def tile(j, carry):
            if self.load is not None and k == 0 and not own:
                self.load_right(j).wait()
            cols = pl.ds(pl.multiple_of(j * COLUMNS, COLUMNS), COLUMNS)
            left = self.left[:, :, core, rows, :].reshape(4 * self.rows, depth)
            product = dot(left, self.right[cols, :], 1, 1).astype(BF16)
            target[:, :, rows, cols] = product.reshape(2, 2, self.rows, COLUMNS)
            return carry

        lax.fori_loop(0, self.width // COLUMNS, tile, 0)

    def begin(self, k):
        self.copy(k, 0).start()

    def release(self, k):
        self.copy(k, 0).wait_send()

    def first(self, k):
        mine, got = self.refs[1:3]
        self.copy(k, 0).wait_recv()

        def add(i, carry):
            def step(rows):
                at = (i // 2, i % 2, rows)
                mine[at] = mine[at] + got[at]

            tiles(k * self.rows, self.rows, step)
            return carry

        lax.fori_loop(0, 4, add, 0)
        self.copy(k, 1).start()
        self.copy(k, 2).start()

    def second(self, k):
        mine, _, gx, gy = self.refs[1:5]
        x = neighbours()[0]
        low, high = self.lanes()
        self.copy(k, 1).wait_recv()

        def step_low(rows):
            for i in range(2):
                at = (i, x, rows, low)
                mine[at] = mine[at] + gx[i, rows]

        tiles(k * self.rows, self.rows, step_low)
        self.copy(k, 3).start()
        self.copy(k, 2).wait_recv()

        def step_high(rows):
            for i in range(2):
                at = (0, i, rows, high)
                mine[at] = mine[at] + gy[i, rows]

        tiles(k * self.rows, self.rows, step_high)
        self.copy(k, 4).start()

    def arrive(self, k):
        self.copy(k, 3).wait_recv()
        self.copy(k, 4).wait_recv()

    def take(self, rows):
        mine, fx, fy = self.refs[1], *self.refs[5:7]
        x = neighbours()[0]
        low, high = self.lanes()
        return jnp.concatenate(
            [
                mine[0, x, rows, low].astype(F32) + fy[rows].astype(F32),
                mine[0, x, rows, high].astype(F32) + fx[rows].astype(F32),
            ],
            -1,
        )

    def finish(self):
        for k in range(self.chunks):
            for i in range(1, 5):
                self.copy(k, i).wait_send()


class Gather:
    STAGES = 9

    def __init__(self, mine, full, local, send, recv):
        self.refs = (mine, full, local, send, recv)
        self.rows = mine.shape[0] // CHUNKS
        self.half = mine.shape[1] // 2

    @staticmethod
    def scratch(rows, width):
        return [
            pltpu.VMEM((rows, width), BF16),
            pltpu.SemaphoreType.DMA((CHUNKS,)),
            pltpu.SemaphoreType.DMA((Gather.STAGES, CHUNKS)),
            pltpu.SemaphoreType.DMA((Gather.STAGES, CHUNKS)),
        ]

    def copy(self, k, i):
        mine, full, local, send, recv = self.refs
        x, c, core_peer, x_peer, y_peer = neighbours()
        rows = pl.ds(k * self.rows, self.rows)
        low, high = pl.ds(0, self.half), pl.ds(self.half, self.half)
        s = [send.at[j, k] for j in range(self.STAGES)]
        r = [recv.at[j, k] for j in range(self.STAGES)]

        def pass_on(j, at, peer):
            return lambda: remote(full.at[at], full.at[at], s[j], r[j], peer)

        all_copies = (
            lambda: pltpu.make_async_copy(mine.at[rows], full.at[0, x, c, rows], local.at[k]),
            lambda: remote(mine.at[rows, low], full.at[1, x, c, rows, low], s[0], r[0], y_peer),
            lambda: remote(mine.at[rows, high], full.at[0, x, c, rows, high], s[1], r[1], x_peer),
            lambda: remote(mine.at[rows], full.at[0, x, c, rows], s[2], r[2], core_peer),
            pass_on(3, (slice(None), x, c, rows, low), x_peer),
            lambda: remote(
                full.at[0, :, c, rows, high], full.at[1, :, c, rows, high], s[4], r[4], y_peer
            ),
            pass_on(5, (1, x, c, rows, low), core_peer),
            pass_on(6, (0, 1 - x, c, rows, high), core_peer),
            pass_on(7, (slice(None), 1 - x, c, rows, low), core_peer),
            pass_on(8, (1, slice(None), c, rows, high), core_peer),
        )
        return all_copies[i]()

    def begin(self, k):
        for i in (1, 2, 0, 3):
            self.copy(k, i).start()

    def second(self, k):
        self.copy(k, 0).wait()
        self.copy(k, 1).wait_recv()
        self.copy(k, 4).start()
        self.copy(k, 2).wait_recv()
        for i in (5, 6, 7):
            self.copy(k, i).start()

    def third(self, k):
        for i in (4, 5):
            self.copy(k, i).wait_recv()
            self.copy(k, i + 4).start()

    def finish(self):
        for k in range(CHUNKS):
            for i in (3, 6, 7, 8, 9):
                self.copy(k, i).wait_recv()
            for i in range(1, 10):
                self.copy(k, i).wait_send()


N_REDUCE = len(Reduce.scratch(32, 256, 128))


def nothing():
    pass


def leg(left, right, low, full, step, scratch, at_start=nothing, at_middle=nothing, load=None):
    reduce = Reduce(left, right, low, *scratch[:N_REDUCE], load=load)
    if load is not None:
        reduce.start_loads()
    gather = Gather(scratch[N_REDUCE], full, *scratch[N_REDUCE + 1 :])
    mine = scratch[N_REDUCE]
    greet(neighbours()[2:])
    for k in range(CHUNKS):
        reduce.produce(k, False)
        if k == 0:
            meet(3)
        reduce.begin(k)
        reduce.produce(k, True)
        reduce.first(k)
    at_start()
    for k in range(CHUNKS):
        reduce.second(k)
    at_middle()

    def step_at(rows):
        mine[rows] = step(rows, reduce.take(rows)).astype(BF16)

    for k in range(CHUNKS):
        reduce.arrive(k)
        tiles(k * reduce.rows, reduce.rows, step_at)
        gather.begin(k)
    for k in range(CHUNKS):
        gather.second(k)
    for k in range(CHUNKS):
        gather.third(k)
    gather.finish()
    for k in range(CHUNKS):
        reduce.release(k)
    reduce.finish()


def attention_leg(
    left,
    packed,
    tokens,
    gain,
    cotangent,
    cot_part,
    cot_across,
    hidden,
    normed,
    cot_pair,
    cot_buffer,
    cot_in,
    cot_out,
    cot_send,
    cot_recv,
    *scratch
):
    def step(rows, total):
        h = tokens[rows].astype(F32) + total
        hidden[rows] = h
        return norm_parts(h)[0] * gain[...]

    x, core, core_peer = neighbours()[:3]
    own, share = cotangent.shape[0], cot_part.shape[0]

    def place(at_x, at_core):
        start = own + (at_x * 2 + at_core) * share
        return pl.ds(pl.multiple_of(start, share), share)

    sources = (cotangent, cot_part, cot_across)
    starts = (0, own, own + share)
    places = (pl.ds(0, own), place(x, core), place(1 - x, core))
    loads, stores, sends = [], [], []
    for i in range(3):
        held = cot_buffer.at[pl.ds(starts[i], sources[i].shape[0])]
        loads.append(pltpu.make_async_copy(sources[i], held, cot_in.at[i]))
        stores.append(pltpu.make_async_copy(held, cot_pair.at[places[i]], cot_out.at[i]))
        if i > 0:
            to = cot_pair.at[places[i]]
            sends.append(remote(sources[i], to, cot_send.at[i - 1], cot_recv.at[i - 1], core_peer))

    def at_start():
        for copy in loads + sends:
            copy.start()

    def at_middle():
        for load, store in zip(loads, stores):
            load.wait()
            store.start()

    depth = left.shape[4]
    right = packed.at[:, pl.ds(packed.shape[1] - depth, depth)]
    leg(left, right, right.shape[0] // 2, normed, step, scratch, at_start, at_middle)
    for copy in stores + sends:
        copy.wait()


def hidden_leg(
    left,
    right,
    hidden,
    cotangent,
    gain,
    grad_hidden,
    gain_grad,
    full,
    left_held,
    right_held,
    left_sems,
    right_sems,
    *scratch
):
    def step(rows, grad):
        hat, inv = norm_parts(hidden[rows])
        gain_grad[...] += jnp.sum(grad * hat, 0, keepdims=True)
        grad = cotangent[rows].astype(F32) + norm_back(grad, hat, inv, gain[...])
        grad_hidden[rows] = grad
        return grad

    gain_grad[...] = jnp.zeros_like(gain_grad)
    load = (left, right, left_sems, right_sems)
    leg(left_held, right_held, right.shape[0] // 2, full, step, scratch, load=load)


class SumGains:
    def __init__(self, parts, total, got, mid, others, send, recv, send_mp, recv_mp):
        self.refs = (parts, total, got, mid, others, send, recv, send_mp, recv_mp)
        self.n_dp, self.n_mp = parts.shape[0], others.shape[0] + 1

    @staticmethod
    def scratch(n_dp, n_mp):
        return [
            pltpu.VMEM((n_dp, 8, 128), F32),
            pltpu.VMEM((8, 128), F32),
            pltpu.VMEM((n_mp - 1, 8, 128), F32),
            pltpu.SemaphoreType.DMA((n_dp,)),
            pltpu.SemaphoreType.DMA((n_dp,)),
            pltpu.SemaphoreType.DMA((n_mp,)),
            pltpu.SemaphoreType.DMA((n_mp,)),
        ]

    def across(self, j):
        return (lax.rem(lax.axis_index("dp") + j, self.n_dp), lax.axis_index("mp"))

    def along(self, j):
        return (lax.axis_index("dp"), lax.rem(lax.axis_index("mp") + j, self.n_mp))

    def greet(self):
        barrier = pltpu.get_barrier_semaphore()

        def one(j, carry):
            pl.semaphore_signal(barrier, inc=1, device_id=self.across(j), device_id_type=MESH)
            return carry

        lax.fori_loop(1, self.n_dp, one, 0)
        greet([self.along(j) for j in range(1, self.n_mp)])

    def first(self, j):
        parts, _, got, _, _, send, recv = self.refs[:7]
        to = self.across(j)
        return remote(parts.at[to[0]], got.at[j], send.at[j], recv.at[j], to)

    def second(self, j):
        mid, others = self.refs[3:5]
        send, recv = self.refs[7:]
        return remote(mid, others.at[j - 1], send.at[j], recv.at[j], self.along(j))

    def begin(self):
        def start(j, carry):
            self.first(j).start()
            return carry

        lax.fori_loop(1, self.n_dp, start, 0)

    def pass_on(self):
        parts, _, got, mid = self.refs[:4]
        mid[...] = parts[lax.axis_index("dp")]

        def add(j, carry):
            self.first(j).wait()
            mid[...] += got[j]
            return carry

        lax.fori_loop(1, self.n_dp, add, 0)
        for j in range(1, self.n_mp):
            self.second(j).start()

    def finish(self):
        _, total, _, mid, others = self.refs[:5]
        result = mid[...]
        for j in range(1, self.n_mp):
            self.second(j).wait()
            result += others[j - 1]
        total[...] = result


def output_leg(
    left,
    packed,
    tokens,
    gain,
    gain_parts,
    weight_grads,
    grad_hidden,
    gate_up_grad,
    input_grad,
    gain_total,
    gate_up_other,
    slots,
    swap_send,
    swap_recv,
    *scratch
):
    low = scratch[3].shape[2]
    depth = left.shape[4]
    right = packed.at[:, pl.ds(0, depth)]
    reduce = Reduce(left, right, low, *scratch[:N_REDUCE])
    sums = SumGains(slots, gain_total, *scratch[N_REDUCE:])
    y, y_peer = lax.axis_index("dp") % 2, neighbours()[4]
    half = gate_up_other.shape[0]
    theirs = pl.ds(pl.multiple_of((1 - y) * half, half), half)
    swap = remote(gate_up_grad.at[theirs], gate_up_other, swap_send, swap_recv, y_peer)

    def step(rows):
        grad = reduce.take(rows)
        hat, inv = norm_parts(tokens[rows].astype(F32))
        input_grad[rows] = grad_hidden[rows] + norm_back(grad, hat, inv, gain[...])

    sums.greet()
    slots[...] = gain_parts[...]
    meet(sums.n_dp + sums.n_mp - 2)
    swap.start()
    for k in range(reduce.chunks):
        reduce.produce(k, False)
        reduce.begin(k)
        reduce.produce(k, True)
        reduce.first(k)
    owned = weight_grads.shape[2]
    diagonal = lax.broadcasted_iota(jnp.int32, (owned, owned), 0) == lax.broadcasted_iota(
        jnp.int32, (owned, owned), 1
    )
    for i in range(sums.n_dp):
        product = dot(right[i * owned : (i + 1) * owned, :], weight_grads[i, :depth, :])
        sums_of = jnp.sum(jnp.where(diagonal, product, 0.0), 0, keepdims=True)
        sums_of = sums_of / gain[:, i * owned : (i + 1) * owned]
        for j, size in gain_rows_of(owned):
            slots[i, j : j + 1, :size] = sums_of[:, j * 128 : j * 128 + size]
    sums.begin()
    for k in range(reduce.chunks):
        reduce.second(k)
    sums.pass_on()
    for k in range(reduce.chunks):
        reduce.arrive(k)
        tiles(k * reduce.rows, reduce.rows, step)
    sums.finish()
    for k in range(reduce.chunks):
        reduce.release(k)
    swap.wait()
    reduce.finish()


ANY = pl.BlockSpec(memory_space=pl.ANY)
VM = pl.BlockSpec(memory_space=pltpu.VMEM)


def call_leg(kernel, ident, name, in_specs, out_shape, out_specs, scratch, bytes_moved):
    return pl.pallas_call(
        kernel,
        out_shape=out_shape,
        in_specs=in_specs,
        out_specs=out_specs,
        scratch_shapes=scratch,
        name=name,
        cost_estimate=pl.CostEstimate(flops=0, bytes_accessed=bytes_moved, transcendentals=0),
        compiler_params=pltpu.CompilerParams(
            collective_id=ident, has_side_effects=True, vmem_limit_bytes=60 * MIB
        ),
    )


class Spread:
    STAGES = 4

    def __init__(self, mine, other, send, recv):
        self.refs = (mine, other, send, recv)
        self.rows = mine.shape[0] // 4 // FEW

    @staticmethod
    def scratch():
        return [
            pltpu.SemaphoreType.DMA((Spread.STAGES, FEW)),
            pltpu.SemaphoreType.DMA((Spread.STAGES, FEW)),
        ]

    def copy(self, k, i):
        mine, other, send, recv = self.refs
        x, c, core_peer, x_peer, y_peer = neighbours()

        def rows(at_x):
            start = (at_x * 2 + c) * (mine.shape[0] // 4) + k * self.rows
            return pl.ds(pl.multiple_of(start, self.rows), self.rows)

        at = rows(1 - x) if i == 3 else rows(x)
        peer = (y_peer, x_peer, core_peer, core_peer)[i]
        source = mine if i == 0 else other
        return remote(source.at[at], other.at[at], send.at[i, k], recv.at[i, k], peer)

    def pass_on(self, k):
        self.copy(k, 0).wait_recv()
        self.copy(k, 1).start()
        self.copy(k, 2).start()

    def pass_last(self, k):
        self.copy(k, 1).wait_recv()
        self.copy(k, 3).start()

    def finish(self):
        for k in range(FEW):
            for i in range(4):
                self.copy(k, i).wait_send()


def front(
    q,
    k,
    v,
    o,
    attn_gain,
    mlp_gain,
    query_gain,
    key_gain,
    docs,
    tokens,
    gate,
    up,
    down,
    full,
    gains,
    docs_other,
    normed_out,
    gate_up_mine,
    down_mine,
    stage,
    gain,
    normed,
    gate_up_stage,
    down_stage,
    tokens_mine,
    tokens_other,
    gate_in,
    up_in,
    down_in,
    local,
    stores,
    swap,
    gain_send,
    gain_recv,
    ring_send,
    ring_recv,
    *scratch
):
    dp, mp = lax.axis_index("dp"), lax.axis_index("mp")
    _, _, core_peer, x_peer, y_peer = neighbours()
    n_dp = gains.shape[0]
    n_slabs = n_dp // 2
    y, z = dp % 2, dp // 2
    rows = q.shape[0]
    spread = Spread(tokens, tokens_other, *scratch)

    def peer(j):
        return (lax.rem(dp + j, n_dp), mp)

    def greet_one(j, carry):
        barrier = pltpu.get_barrier_semaphore()
        pl.semaphore_signal(barrier, inc=1, device_id=peer(j), device_id_type=MESH)
        return carry

    lax.fori_loop(1, n_dp, greet_one, 0)
    greet([core_peer, x_peer])
    loads = [
        pltpu.make_async_copy(source, target, local.at[i])
        for i, (source, target) in enumerate(
            ((tokens, tokens_mine), (gate, gate_in), (up, up_in), (down, down_in))
        )
    ]
    for load in loads:
        load.start()
    widths = [w.shape[1] // 2 for w in (q, k, v)]
    first = sum(widths)

    def fill(target, row, which):
        at = 0
        for w, size in zip((q, k, v), widths):
            cols = pl.ds(pl.multiple_of(which * size, 128), size)
            target[pl.ds(row, rows), at : at + size] = w[:, cols].astype(BF16)
            at += size
        size = o.shape[0] // 2
        part = o[pl.ds(pl.multiple_of(which * size, 128), size), :].astype(BF16)
        target[pl.ds(row, rows), first : first + size] = part.T

    def block(slab, pair):
        return pl.ds(pl.multiple_of((slab * 2 + pair) * rows, rows), rows)

    swapped = remote(stage, full.at[block(z, y)], swap.at[0, 0], swap.at[1, 0], y_peer)
    docs_swapped = remote(docs, docs_other, swap.at[0, 1], swap.at[1, 1], y_peer)
    mine = pl.ds(pl.multiple_of(y * rows, rows), rows)
    gate_up_swapped = remote(
        gate_up_stage, gate_up_mine.at[mine], swap.at[0, 2], swap.at[1, 2], y_peer
    )
    down_swapped = remote(down_stage, down_mine.at[mine], swap.at[0, 3], swap.at[1, 3], y_peer)

    def ring(step, i):
        slab = lax.rem(z - step + n_slabs, n_slabs)
        at = full.at[block(slab, y if i == 0 else 1 - y)]
        to = (lax.rem(dp + 2, n_dp), mp)
        return remote(at, at, ring_send.at[step, i], ring_recv.at[step, i], to)

    def ring_next(step, i):
        slab = lax.rem(z - step - 1 + 2 * n_slabs, n_slabs)
        at = full.at[block(slab, y if i == 0 else 1 - y)]
        to = (lax.rem(dp + 2, n_dp), mp)
        came = remote(at, at, ring_send.at[step, i], ring_recv.at[step, i], to)
        came.wait_recv()
        if isinstance(step, int) and step + 1 >= n_slabs - 1:
            return
        ring(step + 1, i).start()

    def gain_to(j):
        return remote(gain, gains.at[dp], gain_send.at[j], gain_recv.at[j], peer(j))

    def share(j, carry):
        gain_to(j).start()
        return carry

    def settle(j, carry):
        gain_to(j).wait()
        return carry

    def fill_mlp(gate_up_to, down_to, row, which):
        size = gate.shape[1] // 2
        cols = pl.ds(pl.multiple_of(which * size, 128), size)
        gate_up_to[pl.ds(row, rows), :size] = gate_in[:, cols].astype(BF16)
        gate_up_to[pl.ds(row, rows), size:] = up_in[:, cols].astype(BF16)
        down_to[pl.ds(row, rows), :] = down_in[cols, :].astype(BF16).T

    fill(stage, 0, 1 - y)
    row = 0
    for values in (attn_gain, mlp_gain, query_gain, key_gain):
        for j, size in gain_rows_of(values.shape[1]):
            part = values[:, j * 128 : j * 128 + size]
            gain[row : row + 1, :size] = part.astype(BF16).astype(F32)
            row += 1
    meet(n_dp - 1 + 2)
    swapped.start()
    fill(full, block(z, y).start, y)
    ring(0, 0).start()
    docs_swapped.start()
    lax.fori_loop(1, n_dp, share, 0)
    for c in range(FEW):
        spread.copy(c, 0).start()
    gains[dp] = gain[...]
    for load in loads[1:]:
        load.wait()
    fill_mlp(gate_up_stage, down_stage, 0, 1 - y)
    gate_up_swapped.start()
    down_swapped.start()
    swapped.wait_recv()
    ring(0, 1).start()
    lax.fori_loop(1, n_dp, settle, 0)
    owned = gain_rows_of(full.shape[0] // n_dp)
    gain_row = jnp.concatenate(
        [gains[i, j : j + 1, :size] for i in range(n_dp) for j, size in owned], -1
    )

    def norm(source, base, start, count):
        def step(at):
            hat = norm_parts(source[at].astype(F32))[0]
            to = pl.ds(pl.multiple_of(base + at.start, TILE), TILE)
            normed[to] = (hat * gain_row).astype(BF16)

        tiles(start, count, step)

    total = tokens.shape[0]
    quarter = total // 4

    def store(i):
        at = pl.ds(i * quarter, quarter)
        return pltpu.make_async_copy(normed.at[at], normed_out.at[at], stores.at[i])

    def norm_mine(i):
        norm(tokens_mine, 0, i * quarter, quarter)
        store(i).start()

    def norm_other():
        for c in range(FEW):
            for i in (2, 3):
                spread.copy(c, i).wait_recv()
        for i in range(4):
            norm(tokens_other, total, i * quarter, quarter)
            store(4 + i).start()

    loads[0].wait()
    early = [functools.partial(fill_mlp, gate_up_mine, down_mine, mine.start, y)]
    early += [functools.partial(norm_mine, i) for i in range(4)]
    late = [functools.partial(spread.pass_on, c) for c in range(FEW)]
    late += [functools.partial(spread.pass_last, c) for c in range(FEW)]

    def run(jobs):
        for job in jobs:
            job()

    if n_slabs == 4:
        ring_next(0, 0)
        run(early[:3])
        ring_next(0, 1)
        run(early[3:])
        spread.pass_on(0)
        ring_next(1, 0)
        spread.pass_on(1)
        spread.pass_last(0)
        ring_next(1, 1)
        spread.pass_last(1)
        norm_other()
        ring_next(2, 0)
        ring_next(2, 1)
    else:
        run(early)
        run(late)

        def turn(step, carry):
            for i in range(2):
                ring_next(step, i)
            return carry

        lax.fori_loop(0, n_slabs - 2, turn, 0)
        for i in range(2):
            ring_next(n_slabs - 2, i)
        norm_other()
    spread.finish()
    for i in range(8):
        store(i).wait()
    docs_swapped.wait()
    swapped.wait_send()
    gate_up_swapped.wait()
    down_swapped.wait()

    def sent(step, carry):
        for i in range(2):
            ring(step, i).wait_send()
        return carry

    lax.fori_loop(0, n_slabs - 1, sent, 0)


def gain_rows_of(size):
    return [(j, min(128, size - j * 128)) for j in range(-(-size // 128))]


QUERY_BLOCK = 256
LONGEST = 512


def rolled(values):
    return pltpu.roll(values, HEAD_WIDTH // 2, 1)


def lane_mean(values):
    high = values.astype(BF16)
    low = (values - high.astype(F32)).astype(BF16)
    share = jnp.full((HEAD_WIDTH, HEAD_WIDTH), 1.0 / HEAD_WIDTH, BF16)
    return dot(high, share) + dot(low, share)


def head_norm(raw, h):
    values = raw[:, h * HEAD_WIDTH : (h + 1) * HEAD_WIDTH]
    scaling = lax.rsqrt(lane_mean(values * values) + EPSILON)
    return (values * scaling, scaling)


def rope_of(normed, cosine, sine):
    return (normed * cosine[...] + rolled(normed) * sine[...]).astype(BF16)


def blocks_of(length):
    for start in range(0, length, QUERY_BLOCK):
        first = max(0, start - LONGEST)
        yield slice(start, start + QUERY_BLOCK), slice(first, start + QUERY_BLOCK)


def together(values, rows):
    return values[:, rows].reshape(GROUP * QUERY_BLOCK, HEAD_WIDTH)


def weights_of(query, key, starts, rows, cols):
    size = cols.stop - cols.start
    scores = dot(query, key, 1, 1).reshape(GROUP, QUERY_BLOCK, size)
    shape = (QUERY_BLOCK, size)
    query_index = rows.start + lax.broadcasted_iota(jnp.int32, shape, 0)
    key_index = cols.start + lax.broadcasted_iota(jnp.int32, shape, 1)
    allowed = (key_index <= query_index) & (key_index >= starts[rows])
    scores = jnp.where(allowed[None], scores, MASKED)
    highest = jnp.max(scores, -1, keepdims=True)
    exponent = jnp.exp((scores - highest) * HEAD_WIDTH ** (-0.5))
    weights = exponent * (1.0 / jnp.sum(exponent, -1, keepdims=True))
    return weights.reshape(GROUP * QUERY_BLOCK, size)


def prepare_heads(raw, cosine, sine, gain_query, gain_key, q, k):
    for h in range(GROUP):
        q[h] = rope_of(head_norm(raw, h)[0] * gain_query[...], cosine, sine)
    k[...] = rope_of(head_norm(raw, GROUP)[0] * gain_key[...], cosine, sine)


def attend_forward(raw, cosine, sine, starts, gain_query, gain_key, out, q, k):
    prepare_heads(raw, cosine, sine, gain_query, gain_key, q, k)
    at = (GROUP + 1) * HEAD_WIDTH
    for rows, cols in blocks_of(raw.shape[0]):
        weights = weights_of(together(q, rows), k[cols], starts, rows, cols).astype(BF16)
        value = raw[cols, at : at + HEAD_WIDTH].astype(BF16)
        result = dot(weights, value).astype(BF16).reshape(GROUP, QUERY_BLOCK, HEAD_WIDTH)
        for h in range(GROUP):
            out[rows, h * HEAD_WIDTH : (h + 1) * HEAD_WIDTH] = result[h]


def attend_backward(
    raw,
    cosine,
    sine,
    starts,
    gain_query,
    gain_key,
    grad_hidden,
    normed,
    attended,
    packed,
    mlp_left,
    mlp_right,
    hidden,
    down_grad,
    out,
    gains,
    weight_grads,
    output,
    down_other,
    q,
    k,
    v,
    dq,
    dk,
    dv,
    grad,
    total,
    normed_held,
    mlp_left_held,
    mlp_right_held,
    hidden_held,
    loads,
    swap,
    *scratch
):
    factor = HEAD_WIDTH ** (-0.5)
    at = (GROUP + 1) * HEAD_WIDTH
    inputs = (GROUP + 2) * HEAD_WIDTH
    mlp = Reduce(mlp_left_held, mlp_right_held, mlp_right.shape[0] // 2, *scratch)
    length = raw.shape[0]
    here = pl.ds(pl.multiple_of(pl.program_id(0) * length, length), length)
    normed_load = pltpu.make_async_copy(normed.at[here], normed_held, loads.at[0])
    mlp_loads = [
        pltpu.make_async_copy(source, target, loads.at[i + 1])
        for i, (source, target) in enumerate(
            ((mlp_left, mlp_left_held), (mlp_right, mlp_right_held), (hidden, hidden_held))
        )
    ]

    theirs = pl.ds(
        pl.multiple_of((1 - lax.axis_index("dp") % 2) * down_other.shape[0], down_other.shape[0]),
        down_other.shape[0],
    )
    swapped = remote(down_grad.at[theirs], down_other, swap.at[0], swap.at[1], neighbours()[4])

    def mlp_load():
        greet(neighbours()[2:])
        for load in mlp_loads:
            load.start()

    def mlp_begin():
        for load in mlp_loads[:2]:
            load.wait()
        for c in range(FEW):
            mlp.produce(c, False)
            if c == 0:
                meet(3)
            mlp.begin(c)
        swapped.start()

    def mlp_first():
        for c in range(FEW):
            mlp.produce(c, True)
            mlp.first(c)

    def mlp_second():
        for c in range(FEW):
            mlp.second(c)

    def mlp_end():
        def step(rows):
            output[rows] = (hidden_held[rows] + mlp.take(rows)).astype(BF16)

        mlp_loads[2].wait()

        for c in range(FEW):
            mlp.arrive(c)
            tiles(c * mlp.rows, mlp.rows, step)
        for c in range(FEW):
            mlp.release(c)
        mlp.finish()
        swapped.wait()

    def at_step(step, job):
        pl.when(pl.program_id(0) == step)(job)

    at_step(0, mlp_load)
    normed_load.start()
    prepare_heads(raw, cosine, sine, gain_query, gain_key, q, k)
    v[...] = raw[:, at : at + HEAD_WIDTH].astype(BF16)
    dk[...] = jnp.zeros_like(dk)
    dv[...] = jnp.zeros_like(dv)
    for h in range(GROUP):
        lanes = slice(inputs + h * HEAD_WIDTH, inputs + (h + 1) * HEAD_WIDTH)
        grad[h] = dot(grad_hidden[...], packed[:, lanes]).astype(BF16)
    at_step(0, mlp_begin)
    for n, (rows, cols) in enumerate(blocks_of(length)):
        query, block_grad = together(q, rows), together(grad, rows)
        weights = weights_of(query, k[cols], starts, rows, cols)
        grad_weights = dot(block_grad, v[cols], 1, 1)
        inner = jnp.sum(weights * grad_weights, -1, keepdims=True)
        grad_scores = (weights * (grad_weights - inner)).astype(BF16)
        dq[:, rows] = (dot(grad_scores, k[cols]) * factor).reshape(GROUP, QUERY_BLOCK, HEAD_WIDTH)
        dk[cols] += dot(grad_scores, query, 0, 0) * factor
        dv[cols] += dot(weights.astype(BF16), block_grad, 0, 0)
        if n == 0:
            at_step(0, mlp_first)
        if n == 1:
            at_step(1, mlp_second)
    gains[...] = jnp.zeros_like(gains)

    def undo(rot_grad, h, gain, row):
        normed_grad = rot_grad * cosine[...] - rolled(rot_grad) * sine[...]
        hat, inv = head_norm(raw, h)
        gains[0, row : row + 1] += jnp.sum(normed_grad * hat, 0, keepdims=True)
        lanes = slice(h * HEAD_WIDTH, (h + 1) * HEAD_WIDTH)
        scaled = normed_grad * gain[...]
        out[:, lanes] = (inv * (scaled - hat * lane_mean(scaled * hat))).astype(BF16)

    for h in range(GROUP):
        undo(dq[h], h, gain_query, 0)
    undo(dk[...], GROUP, gain_key, 1)
    out[:, at : at + HEAD_WIDTH] = dv[...].astype(BF16)

    @pl.when(pl.program_id(0) == 0)
    def _():
        total[...] = jnp.zeros_like(total)

    out_turned, attended_turned = out[...].T, attended[...].T
    normed_load.wait()
    for start in range(0, normed.shape[1], COLUMNS):
        cols = slice(start, start + COLUMNS)
        total[:inputs, cols] += dot(out_turned, normed_held[:, cols])
        total[inputs:, cols] += dot(attended_turned, grad_hidden[:, cols])

    @pl.when(pl.program_id(0) == pl.num_programs(0) - 1)
    def _():
        size = weight_grads.shape[2]
        for i in range(weight_grads.shape[0]):
            weight_grads[i] = total[:, i * size : (i + 1) * size].astype(BF16)

    at_step(1, mlp_end)


def once(spec):
    return pl.BlockSpec(spec.block_shape, spec.index_map, pipeline_mode=pl.Buffered(1))


def by_rows(rows, cols):
    return pl.BlockSpec((rows, cols), lambda i: (i, 0))


def whole(*shape):
    return pl.BlockSpec(shape, lambda i: (0,) * len(shape))


def call_blocks(
    kernel, steps, in_specs, out_shape, out_specs, scratch, flops, bytes_accessed, **remote_params
):
    return pl.pallas_call(
        kernel,
        out_shape=out_shape,
        grid=(steps,),
        in_specs=in_specs,
        out_specs=out_specs,
        scratch_shapes=scratch,
        name=kernel.__name__,
        cost_estimate=pl.CostEstimate(
            flops=flops, bytes_accessed=bytes_accessed, transcendentals=0
        ),
        compiler_params=pltpu.CompilerParams(
            dimension_semantics=("arbitrary",), vmem_limit_bytes=60 * MIB, **remote_params
        ),
    )


TOKEN_BLOCK = 512
HIDDEN_BLOCK = 256


def mlp_forward(normed, weights, active, gate_slope, up_slope):
    size = active.shape[1]
    for start in range(0, size, HIDDEN_BLOCK):
        cols = slice(start, start + HIDDEN_BLOCK)
        gate = dot(normed[...], weights[:, cols])
        up = dot(normed[...], weights[:, size + start : size + start + HIDDEN_BLOCK])
        sigmoid = jax.nn.sigmoid(gate)
        swish = gate * sigmoid
        active[:, cols] = (swish * up).astype(BF16)
        gate_slope[:, cols] = up * sigmoid * (1.0 + gate * (1.0 - sigmoid))
        up_slope[:, cols] = swish


def mlp_backward(cotangent, weights, gate_slope, up_slope, grads):
    size = gate_slope.shape[1]
    for start in range(0, size, HIDDEN_BLOCK):
        cols = slice(start, start + HIDDEN_BLOCK)
        grad = dot(cotangent[...], weights[:, cols])
        grads[:, cols] = (grad * gate_slope[:, cols]).astype(BF16)
        up_cols = slice(size + start, size + start + HIDDEN_BLOCK)
        grads[:, up_cols] = (grad * up_slope[:, cols]).astype(BF16)


def on_device(
    tokens,
    documents,
    cotangent,
    attn_gain,
    query_gain,
    key_norm_scale,
    query_weight,
    key_projection,
    value_projection,
    output_weight,
    mlp_gain,
    gate_weight,
    up_weight,
    down_weight,
):
    n_dp = lax.axis_size("dp")
    dp, mp = lax.axis_index("dp"), lax.axis_index("mp")
    y = dp % 2
    slabs = [[i + 2 * k for k in range(n_dp // 2)] for i in range(2)]
    rows, width = tokens.shape
    seq_length = documents.shape[1]
    seqs = 2 * documents.shape[0]
    share = rows // 4
    head = HEAD_WIDTH
    query_cols, key_cols, hidden_cols = (
        query_weight.shape[1] // 2,
        key_projection.shape[1] // 2,
        gate_weight.shape[1] // 2,
    )
    attn_cols = query_cols + 2 * key_cols

    def y_swap(values):
        return lax.ppermute(values, "dp", [(i, i ^ 1) for i in range(n_dp)])

    def mp_swap(values, bit):
        return lax.ppermute(values, "mp", [(i, i ^ bit) for i in range(4)])

    def in_order(where, mine, other, axis):
        return jnp.where(
            where == 0,
            jnp.concatenate([mine, other], axis),
            jnp.concatenate([other, mine], axis),
        )

    def half(values, which, axis):
        size = values.shape[axis] // 2
        return lax.dynamic_slice_in_dim(values, which * size, size, axis)

    def slab_gather(values):
        return lax.all_gather(values, "dp", axis=0, tiled=True, axis_index_groups=slabs)

    def slab_scatter(values):
        return lax.psum_scatter(
            values, "dp", scatter_dimension=0, tiled=True, axis_index_groups=slabs
        )

    n_gain, n_head = attn_gain.shape[0], query_gain.shape[0]

    def gain_rows(*parts):
        lead = parts[0].shape[:-1]
        pad = [(0, 0)] * len(lead)
        rows_of = jnp.concatenate(
            [
                jnp.pad(part, pad + [(0, -part.shape[-1] % 128)]).reshape(*lead, -1, 128)
                for part in parts
            ],
            -2,
        )
        return jnp.pad(rows_of, pad + [(0, 8 - rows_of.shape[-2]), (0, 0)])

    def gain_parts_of(rows_of):
        lead, parts, at = rows_of.shape[:-2], [], 0
        for size in (n_gain, n_gain, n_head, n_head):
            n = -(-size // 128)
            part = rows_of[..., at : at + n, :].reshape(*lead, n * 128)
            parts.append(part[..., :size])
            at += n
        return parts

    model_rows = query_weight.shape[0]
    pack_cols = attn_cols + query_cols
    pair_rows = 2 * rows
    n_slabs = n_dp // 2
    attn_full, gains, docs_other, normed_one, mlp_mine, down_mine = call_leg(
        front,
        3,
        "front",
        [VM] * 9 + [ANY] * 4,
        (
            jax.ShapeDtypeStruct((width, pack_cols), BF16),
            jax.ShapeDtypeStruct((n_dp, 8, 128), F32),
            jax.ShapeDtypeStruct(documents.shape, jnp.int32),
            jax.ShapeDtypeStruct((pair_rows, width), BF16),
            jax.ShapeDtypeStruct((2 * model_rows, 2 * hidden_cols), BF16),
            jax.ShapeDtypeStruct((2 * model_rows, hidden_cols), BF16),
        ),
        (VM, VM, VM, ANY, VM, VM),
        [
            pltpu.VMEM((model_rows, pack_cols), BF16),
            pltpu.VMEM((8, 128), F32),
            pltpu.VMEM((pair_rows, width), BF16),
            pltpu.VMEM((model_rows, 2 * hidden_cols), BF16),
            pltpu.VMEM((model_rows, hidden_cols), BF16),
            pltpu.VMEM((rows, width), BF16),
            pltpu.VMEM((rows, width), BF16),
            pltpu.VMEM(gate_weight.shape, F32),
            pltpu.VMEM(up_weight.shape, F32),
            pltpu.VMEM(down_weight.shape, F32),
            pltpu.SemaphoreType.DMA((4,)),
            pltpu.SemaphoreType.DMA((8,)),
            pltpu.SemaphoreType.DMA((2, 4)),
            pltpu.SemaphoreType.DMA((n_dp,)),
            pltpu.SemaphoreType.DMA((n_dp,)),
            pltpu.SemaphoreType.DMA((n_slabs, 2)),
            pltpu.SemaphoreType.DMA((n_slabs, 2)),
        ]
        + Spread.scratch(),
        250 * MIB,
    )(
        query_weight,
        key_projection,
        value_projection,
        output_weight,
        attn_gain.reshape(1, -1),
        mlp_gain.reshape(1, -1),
        query_gain.reshape(1, -1),
        key_norm_scale.reshape(1, -1),
        documents,
        tokens,
        gate_weight,
        up_weight,
        down_weight,
    )

    cot_part = lax.dynamic_slice_in_dim(cotangent, mp * share, share, 0)
    cot_part, _ = lax.optimization_barrier((cot_part, docs_other))
    cot_part = y_swap(cot_part)
    gate_up_full = slab_gather(mlp_mine)
    down_full = slab_gather(down_mine)
    gain_one, gain_two, gain_query, gain_key = (g.reshape(1, -1) for g in gain_parts_of(gains))
    docs = jnp.concatenate([documents, docs_other], 0)
    tokens_share = lax.dynamic_slice_in_dim(tokens, mp * share, share, 0)
    cot_share = lax.dynamic_slice_in_dim(cotangent, mp * share, share, 0)

    raw = dot(normed_one, attn_full[:, :attn_cols])
    starts = sum((docs < i).sum(1, keepdims=True) * (docs == i) for i in range(1, 4))
    positions = (jnp.arange(seq_length, dtype=jnp.int32)[None] - starts).reshape(pair_rows)
    cosine, sine = rope_tables(positions, head)
    starts = starts.reshape(pair_rows, 1).astype(jnp.int32)
    raw, sine, cot_part = lax.optimization_barrier((raw, sine, cot_part))
    cot_across = mp_swap(cot_part, 2)
    attention_args = (raw, cosine, sine, starts, gain_query, gain_key)
    attention_specs = [
        by_rows(seq_length, attn_cols),
        by_rows(seq_length, head),
        by_rows(seq_length, head),
        by_rows(seq_length, 1),
        whole(1, head),
        whole(1, head),
    ]
    pair_flops = pair_rows * seq_length * query_cols
    attended = call_blocks(
        attend_forward,
        seqs,
        attention_specs,
        jax.ShapeDtypeStruct((pair_rows, query_cols), BF16),
        by_rows(seq_length, query_cols),
        [pltpu.VMEM((GROUP, seq_length, head), BF16), pltpu.VMEM((seq_length, head), BF16)],
        2 * pair_flops,
        20 * MIB,
    )(*attention_args)
    attended, cot_across = lax.optimization_barrier((attended, cot_across))

    def grouped(cols):
        return (2, 2, 2, share, cols)

    half_width = width // 2
    leg_scratch = Reduce.scratch(share, width, half_width) + Gather.scratch(share, width)
    hidden, normed_two, cot_pair = call_leg(
        attention_leg,
        0,
        "attention_leg",
        [VM] * 4 + [ANY] * 3,
        (
            jax.ShapeDtypeStruct((share, width), F32),
            jax.ShapeDtypeStruct(grouped(width), BF16),
            jax.ShapeDtypeStruct((pair_rows, width), BF16),
        ),
        (VM, ANY, ANY),
        [
            pltpu.VMEM((rows + 2 * share, width), BF16),
            pltpu.SemaphoreType.DMA((3,)),
            pltpu.SemaphoreType.DMA((3,)),
            pltpu.SemaphoreType.DMA((2,)),
            pltpu.SemaphoreType.DMA((2,)),
        ]
        + leg_scratch,
        200 * MIB,
    )(
        attended.reshape(grouped(query_cols)),
        attn_full,
        tokens_share,
        gain_two,
        cotangent,
        cot_part,
        cot_across,
    )
    normed_two = normed_two.reshape(pair_rows, width)

    blocks = pair_rows // TOKEN_BLOCK
    hidden_block = by_rows(TOKEN_BLOCK, hidden_cols)
    hidden_shape = (pair_rows, hidden_cols)
    mlp_flops = 2 * pair_rows * width * hidden_cols
    active, gate_slope, up_slope = call_blocks(
        mlp_forward,
        blocks,
        [by_rows(TOKEN_BLOCK, width), whole(width, 2 * hidden_cols)],
        (
            jax.ShapeDtypeStruct(hidden_shape, BF16),
            jax.ShapeDtypeStruct(hidden_shape, F32),
            jax.ShapeDtypeStruct(hidden_shape, F32),
        ),
        (hidden_block,) * 3,
        [],
        2 * mlp_flops,
        30 * MIB,
    )(normed_two, gate_up_full)
    down_part = dot(cot_pair, active, 0, 0).astype(BF16)
    down_grad = slab_scatter(down_part)
    cot_late, _ = lax.optimization_barrier((cot_pair, down_part))
    grad_gate_up = call_blocks(
        mlp_backward,
        blocks,
        [by_rows(TOKEN_BLOCK, width), whole(width, hidden_cols), hidden_block, hidden_block],
        jax.ShapeDtypeStruct((pair_rows, 2 * hidden_cols), BF16),
        by_rows(TOKEN_BLOCK, 2 * hidden_cols),
        [],
        mlp_flops,
        30 * MIB,
    )(cot_late, down_full, gate_slope, up_slope)
    gate_up_part = dot(normed_two, grad_gate_up, 0, 0).astype(BF16)
    gate_up_grad = slab_scatter(gate_up_part)
    grad_gate_up, _, _ = lax.optimization_barrier((grad_gate_up, gate_up_part, down_part))
    grad_hidden, mlp_gain_part, grad_hidden_low = call_leg(
        hidden_leg,
        1,
        "hidden_leg",
        [ANY] * 2 + [VM] * 3,
        (
            jax.ShapeDtypeStruct((share, width), F32),
            jax.ShapeDtypeStruct((1, width), F32),
            jax.ShapeDtypeStruct(grouped(width), BF16),
        ),
        (VM, VM, ANY),
        [
            pltpu.VMEM(grouped(2 * hidden_cols), BF16),
            pltpu.VMEM((width, 2 * hidden_cols), BF16),
            pltpu.SemaphoreType.DMA((2, CHUNKS)),
            pltpu.SemaphoreType.DMA((width // COLUMNS,)),
        ]
        + leg_scratch,
        200 * MIB,
    )(
        grad_gate_up.reshape(grouped(2 * hidden_cols)),
        gate_up_full,
        hidden,
        cot_share,
        gain_two,
    )
    grad_hidden_low = grad_hidden_low.reshape(pair_rows, width)

    raw_grad, head_gain_parts, attn_grad, layer_output, down_other = call_blocks(
        attend_backward,
        seqs,
        [once(spec) for spec in attention_specs]
        + [
            once(by_rows(seq_length, width)),
            ANY,
            once(by_rows(seq_length, query_cols)),
            once(whole(width, pack_cols)),
            ANY,
            ANY,
            ANY,
            ANY,
        ],
        (
            jax.ShapeDtypeStruct((pair_rows, attn_cols), BF16),
            jax.ShapeDtypeStruct((seqs, 8, head), F32),
            jax.ShapeDtypeStruct((n_dp, pack_cols, model_rows), BF16),
            jax.ShapeDtypeStruct((share, width), BF16),
            jax.ShapeDtypeStruct((model_rows, hidden_cols), BF16),
        ),
        (
            once(by_rows(seq_length, attn_cols)),
            pl.BlockSpec((1, 8, head), lambda i: (i, 0, 0)),
            once(whole(n_dp, pack_cols, model_rows)),
            once(whole(share, width)),
            ANY,
        ),
        [
            pltpu.VMEM((GROUP, seq_length, head), BF16),
            pltpu.VMEM((seq_length, head), BF16),
            pltpu.VMEM((seq_length, head), BF16),
            pltpu.VMEM((GROUP, seq_length, head), F32),
            pltpu.VMEM((seq_length, head), F32),
            pltpu.VMEM((seq_length, head), F32),
            pltpu.VMEM((GROUP, seq_length, head), BF16),
            pltpu.VMEM((pack_cols, width), F32),
            pltpu.VMEM((seq_length, width), BF16),
            pltpu.VMEM(grouped(hidden_cols), BF16),
            pltpu.VMEM((width, hidden_cols), BF16),
            pltpu.VMEM((share, width), F32),
            pltpu.SemaphoreType.DMA((4,)),
            pltpu.SemaphoreType.DMA((2,)),
        ]
        + Reduce.scratch(share, width, half_width, FEW),
        5 * pair_flops + 2 * pair_rows * width * (pack_cols + query_cols + hidden_cols),
        80 * MIB,
        collective_id=4,
        has_side_effects=True,
    )(
        *attention_args,
        grad_hidden_low,
        normed_one,
        attended,
        attn_full,
        active.reshape(grouped(hidden_cols)),
        down_full,
        hidden,
        down_grad,
    )
    head_gain_parts = head_gain_parts.sum(0)
    attn_grad = attn_grad.reshape(n_dp * pack_cols, model_rows)
    attn_grad, raw_grad, gate_up_grad, down_grad = lax.optimization_barrier(
        (attn_grad, raw_grad, gate_up_grad, down_grad)
    )
    attn_parts = attn_grad.reshape(n_dp, pack_cols, model_rows)
    attn_grad = slab_scatter(attn_grad).reshape(2, pack_cols, model_rows)
    gain_parts = gain_rows(
        jnp.zeros((n_dp, n_gain), F32),
        mlp_gain_part.reshape(n_dp, n_gain),
        head_gain_parts[0].reshape(n_dp, n_head),
        head_gain_parts[1].reshape(n_dp, n_head),
    )

    low = 3 * width // 4
    input_grad, gain_sums, gate_up_other = call_leg(
        output_leg,
        2,
        "output_leg",
        [VM] * 7 + [ANY],
        (
            jax.ShapeDtypeStruct((share, width), F32),
            jax.ShapeDtypeStruct((8, 128), F32),
            jax.ShapeDtypeStruct((model_rows, 2 * hidden_cols), BF16),
        ),
        (VM, VM, ANY),
        [
            pltpu.VMEM((n_dp, 8, 128), F32),
            pltpu.SemaphoreType.DMA,
            pltpu.SemaphoreType.DMA,
        ]
        + Reduce.scratch(share, width, low)
        + SumGains.scratch(n_dp, 4),
        200 * MIB,
    )(
        raw_grad.reshape(grouped(attn_cols)),
        attn_full,
        tokens_share,
        gain_one,
        gain_parts,
        attn_parts,
        grad_hidden,
        gate_up_grad,
    )
    attn_given = lax.dynamic_index_in_dim(attn_grad, 1 - y, 0, False)
    attn_given, gate_up_other, down_other = lax.optimization_barrier(
        (attn_given, gate_up_other, down_other)
    )

    def columns(own, other, start, axis=1):
        own = half(own, y, 0)[:, start : start + hidden_cols]
        other = other[:, start : start + hidden_cols]
        if axis == 0:
            own, other = own.T, other.T
        return in_order(y, own, other, axis).astype(F32)

    gate_grad = columns(gate_up_grad, gate_up_other, 0)
    up_grad = columns(gate_up_grad, gate_up_other, hidden_cols)
    down_grad = columns(down_grad, down_other, 0, 0)

    attn_other = y_swap(attn_given)
    attn_own = lax.dynamic_index_in_dim(attn_grad, y, 0, False)

    def attn_columns(start, size, turn=True):
        own, other = attn_own[start : start + size], attn_other[start : start + size]
        if turn:
            own, other = own.T, other.T
        return in_order(y, own, other, int(turn)).astype(F32)

    query_grad = attn_columns(0, query_cols)
    key_grad = attn_columns(query_cols, key_cols)
    value_grad = attn_columns(query_cols + key_cols, key_cols)
    output_grad = attn_columns(attn_cols, query_cols, False)
    attn_gain_grad, mlp_gain_grad, query_gain_grad, key_gain_grad = gain_parts_of(gain_sums)
    return (
        layer_output,
        input_grad,
        attn_gain_grad,
        query_gain_grad,
        key_gain_grad,
        query_grad,
        key_grad,
        value_grad,
        output_grad,
        mlp_gain_grad,
        gate_grad,
        up_grad,
        down_grad,
    )


def solution(mesh):
    in_specs = (
        P("dp", None),
        P("dp", None),
        P("dp", None),
        P("dp"),
        P("dp"),
        P("dp"),
        P("dp", "mp"),
        P("dp", "mp"),
        P("dp", "mp"),
        P("mp", "dp"),
        P("dp"),
        P("dp", "mp"),
        P("dp", "mp"),
        P("mp", "dp"),
    )
    out_specs = (
        P(("dp", "mp"), None),
        P(("dp", "mp"), None),
        P("dp"),
        P("dp"),
        P("dp"),
        P("dp", "mp"),
        P("dp", "mp"),
        P("dp", "mp"),
        P("mp", "dp"),
        P("dp"),
        P("dp", "mp"),
        P("dp", "mp"),
        P("mp", "dp"),
    )
    return jax.shard_map(
        on_device, mesh=mesh, in_specs=in_specs, out_specs=out_specs, check_vma=False
    )
```

```python
import functools

import jax
import jax.numpy as jnp
from jax import lax
from jax.experimental import pallas as pl
from jax.experimental.pallas import tpu as pltpu
from jax.sharding import PartitionSpec as P

QUERY_HEADS = 16
KEY_VALUE_HEADS = 8
HEAD_WIDTH = 128
GROUP = QUERY_HEADS // KEY_VALUE_HEADS

EPSILON = 1e-06
MASKED = -1e30
MESH = pl.DeviceIdType.MESH
F32 = jnp.float32
BF16 = jnp.bfloat16
MIB = 2**20


def rope_tables(positions, head_size):
    middle = head_size // 2
    frequency = jnp.power(1000000.0, -2.0 * jnp.arange(middle, dtype=F32) / head_size)
    angles = positions.astype(F32)[:, None] * frequency[None, :]
    cosine_table = jnp.cos(angles)
    sine_table = jnp.sin(angles)
    return (
        jnp.concatenate([cosine_table, cosine_table], -1),
        jnp.concatenate([-sine_table, sine_table], -1),
    )


def norm_parts(values):
    scaling = lax.rsqrt(jnp.mean(values * values, -1, keepdims=True) + EPSILON)
    return (values * scaling, scaling)


def norm_back(grad_normed, normed_hat, scaling, gains):
    scaled = grad_normed * gains
    return scaling * (scaled - normed_hat * jnp.mean(scaled * normed_hat, -1, keepdims=True))


def dot(left, right, left_dim=1, right_dim=0):
    return lax.dot_general(
        left, right, (((left_dim,), (right_dim,)), ((), ())), preferred_element_type=F32
    )


CHUNKS = 4
FEW = 2
TILE = 32
COLUMNS = 512


def neighbours():
    dp, mp = lax.axis_index("dp"), lax.axis_index("mp")
    x, c = mp // 2, mp % 2
    return (
        x,
        c,
        (dp, x * 2 + 1 - c),
        (dp, (1 - x) * 2 + c),
        (dp + 1 - 2 * (dp % 2), mp),
    )


def greet(peers):
    barrier = pltpu.get_barrier_semaphore()
    for peer in peers:
        pl.semaphore_signal(barrier, inc=1, device_id=peer, device_id_type=MESH)


def meet(count):
    pl.semaphore_wait(pltpu.get_barrier_semaphore(), count)


def remote(src, dst, send, recv, peer):
    return pltpu.make_async_remote_copy(
        src_ref=src, dst_ref=dst, send_sem=send, recv_sem=recv, device_id=peer, device_id_type=MESH
    )


def tiles(start, rows, step):
    def body(i, carry):
        step(pl.ds(pl.multiple_of(start + i * TILE, TILE), TILE))
        return carry

    lax.fori_loop(0, rows // TILE, body, 0)


class Reduce:
    STAGES = 5

    def __init__(self, left, right, low, part, mine, got, gx, gy, fx, fy, send, recv, load=None):
        self.left, self.right, self.low, self.load = left, right, low, load
        self.refs = (part, mine, got, gx, gy, fx, fy, send, recv)
        self.chunks = send.shape[1]
        self.rows = mine.shape[2] // self.chunks
        self.width = mine.shape[3]

    @staticmethod
    def scratch(rows, width, low, chunks=CHUNKS):
        high = width - low
        return [
            pltpu.VMEM((2, 2, rows, width), BF16),
            pltpu.VMEM((2, 2, rows, width), BF16),
            pltpu.VMEM((2, 2, rows, width), BF16),
            pltpu.VMEM((2, rows, low), BF16),
            pltpu.VMEM((2, rows, high), BF16),
            pltpu.VMEM((rows, high), BF16),
            pltpu.VMEM((rows, low), BF16),
            pltpu.SemaphoreType.DMA((Reduce.STAGES, chunks)),
            pltpu.SemaphoreType.DMA((Reduce.STAGES, chunks)),
        ]

    def lanes(self):
        return pl.ds(0, self.low), pl.ds(self.low, self.width - self.low)

    def load_left(self, k, own):
        source, _, sems, _ = self.load
        core = neighbours()[1]
        at = (slice(None), slice(None), core if own else 1 - core, pl.ds(k * self.rows, self.rows))
        return pltpu.make_async_copy(source.at[at], self.left.at[at], sems.at[int(own), k])

    def load_right(self, j):
        _, source, _, sems = self.load
        at = pl.ds(pl.multiple_of(j * COLUMNS, COLUMNS), COLUMNS)
        return pltpu.make_async_copy(source.at[at], self.right.at[at], sems.at[j])

    def start_loads(self):
        self.load_left(0, False).start()
        for j in range(self.width // COLUMNS):
            self.load_right(j).start()
        self.load_left(0, True).start()
        for k in range(1, self.chunks):
            for own in (False, True):
                self.load_left(k, own).start()

    def copy(self, k, i):
        part, mine, got, gx, gy, fx, fy, send, recv = self.refs
        x, _, core_peer, x_peer, y_peer = neighbours()
        rows = pl.ds(k * self.rows, self.rows)
        low, high = self.lanes()
        s = [send.at[j, k] for j in range(self.STAGES)]
        r = [recv.at[j, k] for j in range(self.STAGES)]
        all_copies = (
            lambda: remote(part.at[:, :, rows], got.at[:, :, rows], s[0], r[0], core_peer),
            lambda: remote(mine.at[:, 1 - x, rows, low], gx.at[:, rows], s[1], r[1], x_peer),
            lambda: remote(mine.at[1, :, rows, high], gy.at[:, rows], s[2], r[2], y_peer),
            lambda: remote(mine.at[1, x, rows, low], fy.at[rows], s[3], r[3], y_peer),
            lambda: remote(mine.at[0, 1 - x, rows, high], fx.at[rows], s[4], r[4], x_peer),
        )
        return all_copies[i]()

    def produce(self, k, own):
        target = self.refs[1] if own else self.refs[0]
        core = neighbours()[1]
        core = core if own else 1 - core
        rows = pl.ds(k * self.rows, self.rows)
        depth = self.left.shape[4]
        if self.load is not None:
            self.load_left(k, own).wait()

        def tile(j, carry):
            if self.load is not None and k == 0 and not own:
                self.load_right(j).wait()
            cols = pl.ds(pl.multiple_of(j * COLUMNS, COLUMNS), COLUMNS)
            left = self.left[:, :, core, rows, :].reshape(4 * self.rows, depth)
            product = dot(left, self.right[cols, :], 1, 1).astype(BF16)
            target[:, :, rows, cols] = product.reshape(2, 2, self.rows, COLUMNS)
            return carry

        lax.fori_loop(0, self.width // COLUMNS, tile, 0)

    def begin(self, k):
        self.copy(k, 0).start()

    def release(self, k):
        self.copy(k, 0).wait_send()

    def first(self, k):
        mine, got = self.refs[1:3]
        self.copy(k, 0).wait_recv()

        def add(i, carry):
            def step(rows):
                at = (i // 2, i % 2, rows)
                mine[at] = mine[at] + got[at]

            tiles(k * self.rows, self.rows, step)
            return carry

        lax.fori_loop(0, 4, add, 0)
        self.copy(k, 1).start()
        self.copy(k, 2).start()

    def second(self, k):
        mine, _, gx, gy = self.refs[1:5]
        x = neighbours()[0]
        low, high = self.lanes()
        self.copy(k, 1).wait_recv()

        def step_low(rows):
            for i in range(2):
                at = (i, x, rows, low)
                mine[at] = mine[at] + gx[i, rows]

        tiles(k * self.rows, self.rows, step_low)
        self.copy(k, 3).start()
        self.copy(k, 2).wait_recv()

        def step_high(rows):
            for i in range(2):
                at = (0, i, rows, high)
                mine[at] = mine[at] + gy[i, rows]

        tiles(k * self.rows, self.rows, step_high)
        self.copy(k, 4).start()

    def arrive(self, k):
        self.copy(k, 3).wait_recv()
        self.copy(k, 4).wait_recv()

    def take(self, rows):
        mine, fx, fy = self.refs[1], *self.refs[5:7]
        x = neighbours()[0]
        low, high = self.lanes()
        return jnp.concatenate(
            [
                mine[0, x, rows, low].astype(F32) + fy[rows].astype(F32),
                mine[0, x, rows, high].astype(F32) + fx[rows].astype(F32),
            ],
            -1,
        )

    def finish(self):
        for k in range(self.chunks):
            for i in range(1, 5):
                self.copy(k, i).wait_send()


class Gather:
    STAGES = 9

    def __init__(self, mine, full, local, send, recv):
        self.refs = (mine, full, local, send, recv)
        self.rows = mine.shape[0] // CHUNKS
        self.half = mine.shape[1] // 2

    @staticmethod
    def scratch(rows, width):
        return [
            pltpu.VMEM((rows, width), BF16),
            pltpu.SemaphoreType.DMA((CHUNKS,)),
            pltpu.SemaphoreType.DMA((Gather.STAGES, CHUNKS)),
            pltpu.SemaphoreType.DMA((Gather.STAGES, CHUNKS)),
        ]

    def copy(self, k, i):
        mine, full, local, send, recv = self.refs
        x, c, core_peer, x_peer, y_peer = neighbours()
        rows = pl.ds(k * self.rows, self.rows)
        low, high = pl.ds(0, self.half), pl.ds(self.half, self.half)
        s = [send.at[j, k] for j in range(self.STAGES)]
        r = [recv.at[j, k] for j in range(self.STAGES)]

        def pass_on(j, at, peer):
            return lambda: remote(full.at[at], full.at[at], s[j], r[j], peer)

        all_copies = (
            lambda: pltpu.make_async_copy(mine.at[rows], full.at[0, x, c, rows], local.at[k]),
            lambda: remote(mine.at[rows, low], full.at[1, x, c, rows, low], s[0], r[0], y_peer),
            lambda: remote(mine.at[rows, high], full.at[0, x, c, rows, high], s[1], r[1], x_peer),
            lambda: remote(mine.at[rows], full.at[0, x, c, rows], s[2], r[2], core_peer),
            pass_on(3, (slice(None), x, c, rows, low), x_peer),
            lambda: remote(
                full.at[0, :, c, rows, high], full.at[1, :, c, rows, high], s[4], r[4], y_peer
            ),
            pass_on(5, (1, x, c, rows, low), core_peer),
            pass_on(6, (0, 1 - x, c, rows, high), core_peer),
            pass_on(7, (slice(None), 1 - x, c, rows, low), core_peer),
            pass_on(8, (1, slice(None), c, rows, high), core_peer),
        )
        return all_copies[i]()

    def begin(self, k):
        for i in (1, 2, 0, 3):
            self.copy(k, i).start()

    def second(self, k):
        self.copy(k, 0).wait()
        self.copy(k, 1).wait_recv()
        self.copy(k, 4).start()
        self.copy(k, 2).wait_recv()
        for i in (5, 6, 7):
            self.copy(k, i).start()

    def third(self, k):
        for i in (4, 5):
            self.copy(k, i).wait_recv()
            self.copy(k, i + 4).start()

    def finish(self):
        for k in range(CHUNKS):
            for i in (3, 6, 7, 8, 9):
                self.copy(k, i).wait_recv()
            for i in range(1, 10):
                self.copy(k, i).wait_send()


N_REDUCE = len(Reduce.scratch(32, 256, 128))


def nothing():
    pass


def leg(left, right, low, full, step, scratch, at_start=nothing, at_middle=nothing, load=None):
    reduce = Reduce(left, right, low, *scratch[:N_REDUCE], load=load)
    if load is not None:
        reduce.start_loads()
    gather = Gather(scratch[N_REDUCE], full, *scratch[N_REDUCE + 1 :])
    mine = scratch[N_REDUCE]
    greet(neighbours()[2:])
    for k in range(CHUNKS):
        reduce.produce(k, False)
        if k == 0:
            meet(3)
        reduce.begin(k)
        reduce.produce(k, True)
        reduce.first(k)
    at_start()
    for k in range(CHUNKS):
        reduce.second(k)
    at_middle()

    def step_at(rows):
        mine[rows] = step(rows, reduce.take(rows)).astype(BF16)

    for k in range(CHUNKS):
        reduce.arrive(k)
        tiles(k * reduce.rows, reduce.rows, step_at)
        gather.begin(k)
    for k in range(CHUNKS):
        gather.second(k)
    for k in range(CHUNKS):
        gather.third(k)
    gather.finish()
    for k in range(CHUNKS):
        reduce.release(k)
    reduce.finish()


def attention_leg(
    left,
    packed,
    tokens,
    gain,
    cotangent,
    cot_part,
    cot_across,
    hidden,
    normed,
    cot_pair,
    cot_buffer,
    cot_in,
    cot_out,
    cot_send,
    cot_recv,
    *scratch
):
    def step(rows, total):
        h = tokens[rows].astype(F32) + total
        hidden[rows] = h
        return norm_parts(h)[0] * gain[...]

    x, core, core_peer = neighbours()[:3]
    own, share = cotangent.shape[0], cot_part.shape[0]

    def place(at_x, at_core):
        start = own + (at_x * 2 + at_core) * share
        return pl.ds(pl.multiple_of(start, share), share)

    sources = (cotangent, cot_part, cot_across)
    starts = (0, own, own + share)
    places = (pl.ds(0, own), place(x, core), place(1 - x, core))
    loads, stores, sends = [], [], []
    for i in range(3):
        held = cot_buffer.at[pl.ds(starts[i], sources[i].shape[0])]
        loads.append(pltpu.make_async_copy(sources[i], held, cot_in.at[i]))
        stores.append(pltpu.make_async_copy(held, cot_pair.at[places[i]], cot_out.at[i]))
        if i > 0:
            to = cot_pair.at[places[i]]
            sends.append(remote(sources[i], to, cot_send.at[i - 1], cot_recv.at[i - 1], core_peer))

    def at_start():
        for copy in loads + sends:
            copy.start()

    def at_middle():
        for load, store in zip(loads, stores):
            load.wait()
            store.start()

    depth = left.shape[4]
    right = packed.at[:, pl.ds(packed.shape[1] - depth, depth)]
    leg(left, right, right.shape[0] // 2, normed, step, scratch, at_start, at_middle)
    for copy in stores + sends:
        copy.wait()


def hidden_leg(
    left,
    right,
    hidden,
    cotangent,
    gain,
    grad_hidden,
    gain_grad,
    full,
    left_held,
    right_held,
    left_sems,
    right_sems,
    *scratch
):
    def step(rows, grad):
        hat, inv = norm_parts(hidden[rows])
        gain_grad[...] += jnp.sum(grad * hat, 0, keepdims=True)
        grad = cotangent[rows].astype(F32) + norm_back(grad, hat, inv, gain[...])
        grad_hidden[rows] = grad
        return grad

    gain_grad[...] = jnp.zeros_like(gain_grad)
    load = (left, right, left_sems, right_sems)
    leg(left_held, right_held, right.shape[0] // 2, full, step, scratch, load=load)


class SumGains:
    def __init__(self, parts, total, got, mid, others, send, recv, send_mp, recv_mp):
        self.refs = (parts, total, got, mid, others, send, recv, send_mp, recv_mp)
        self.n_dp, self.n_mp = parts.shape[0], others.shape[0] + 1

    @staticmethod
    def scratch(n_dp, n_mp):
        return [
            pltpu.VMEM((n_dp, 8, 128), F32),
            pltpu.VMEM((8, 128), F32),
            pltpu.VMEM((n_mp - 1, 8, 128), F32),
            pltpu.SemaphoreType.DMA((n_dp,)),
            pltpu.SemaphoreType.DMA((n_dp,)),
            pltpu.SemaphoreType.DMA((n_mp,)),
            pltpu.SemaphoreType.DMA((n_mp,)),
        ]

    def across(self, j):
        return (lax.rem(lax.axis_index("dp") + j, self.n_dp), lax.axis_index("mp"))

    def along(self, j):
        return (lax.axis_index("dp"), lax.rem(lax.axis_index("mp") + j, self.n_mp))

    def greet(self):
        barrier = pltpu.get_barrier_semaphore()

        def one(j, carry):
            pl.semaphore_signal(barrier, inc=1, device_id=self.across(j), device_id_type=MESH)
            return carry

        lax.fori_loop(1, self.n_dp, one, 0)
        greet([self.along(j) for j in range(1, self.n_mp)])

    def first(self, j):
        parts, _, got, _, _, send, recv = self.refs[:7]
        to = self.across(j)
        return remote(parts.at[to[0]], got.at[j], send.at[j], recv.at[j], to)

    def second(self, j):
        mid, others = self.refs[3:5]
        send, recv = self.refs[7:]
        return remote(mid, others.at[j - 1], send.at[j], recv.at[j], self.along(j))

    def begin(self):
        def start(j, carry):
            self.first(j).start()
            return carry

        lax.fori_loop(1, self.n_dp, start, 0)

    def pass_on(self):
        parts, _, got, mid = self.refs[:4]
        mid[...] = parts[lax.axis_index("dp")]

        def add(j, carry):
            self.first(j).wait()
            mid[...] += got[j]
            return carry

        lax.fori_loop(1, self.n_dp, add, 0)
        for j in range(1, self.n_mp):
            self.second(j).start()

    def finish(self):
        _, total, _, mid, others = self.refs[:5]
        result = mid[...]
        for j in range(1, self.n_mp):
            self.second(j).wait()
            result += others[j - 1]
        total[...] = result


def output_leg(
    left,
    packed,
    tokens,
    gain,
    gain_parts,
    weight_grads,
    grad_hidden,
    gate_up_grad,
    down_grad,
    input_grad,
    gain_total,
    gate_up_other,
    down_other,
    slots,
    swap_send,
    swap_recv,
    *scratch
):
    low = scratch[3].shape[2]
    depth = left.shape[4]
    right = packed.at[:, pl.ds(0, depth)]
    reduce = Reduce(left, right, low, *scratch[:N_REDUCE])
    sums = SumGains(slots, gain_total, *scratch[N_REDUCE:])
    y, y_peer = lax.axis_index("dp") % 2, neighbours()[4]
    half = gate_up_other.shape[0]
    theirs = pl.ds(pl.multiple_of((1 - y) * half, half), half)
    swaps = [
        remote(gate_up_grad.at[theirs], gate_up_other, swap_send.at[0], swap_recv.at[0], y_peer),
        remote(down_grad.at[theirs], down_other, swap_send.at[1], swap_recv.at[1], y_peer),
    ]

    def step(rows):
        grad = reduce.take(rows)
        hat, inv = norm_parts(tokens[rows].astype(F32))
        input_grad[rows] = grad_hidden[rows] + norm_back(grad, hat, inv, gain[...])

    sums.greet()
    slots[...] = gain_parts[...]
    meet(sums.n_dp + sums.n_mp - 2)
    swaps[0].start()
    for k in range(reduce.chunks):
        reduce.produce(k, False)
        reduce.begin(k)
        reduce.produce(k, True)
        reduce.first(k)
    swaps[1].start()
    owned = weight_grads.shape[2]
    diagonal = lax.broadcasted_iota(jnp.int32, (owned, owned), 0) == lax.broadcasted_iota(
        jnp.int32, (owned, owned), 1
    )
    for i in range(sums.n_dp):
        product = dot(right[i * owned : (i + 1) * owned, :], weight_grads[i, :depth, :])
        sums_of = jnp.sum(jnp.where(diagonal, product, 0.0), 0, keepdims=True)
        sums_of = sums_of / gain[:, i * owned : (i + 1) * owned]
        for j, size in gain_rows_of(owned):
            slots[i, j : j + 1, :size] = sums_of[:, j * 128 : j * 128 + size]
    sums.begin()
    for k in range(reduce.chunks):
        reduce.second(k)
    sums.pass_on()
    for k in range(reduce.chunks):
        reduce.arrive(k)
        tiles(k * reduce.rows, reduce.rows, step)
    sums.finish()
    for k in range(reduce.chunks):
        reduce.release(k)
    for copy in swaps:
        copy.wait()
    reduce.finish()


ANY = pl.BlockSpec(memory_space=pl.ANY)
VM = pl.BlockSpec(memory_space=pltpu.VMEM)


def call_leg(kernel, ident, name, in_specs, out_shape, out_specs, scratch, bytes_moved):
    return pl.pallas_call(
        kernel,
        out_shape=out_shape,
        in_specs=in_specs,
        out_specs=out_specs,
        scratch_shapes=scratch,
        name=name,
        cost_estimate=pl.CostEstimate(flops=0, bytes_accessed=bytes_moved, transcendentals=0),
        compiler_params=pltpu.CompilerParams(
            collective_id=ident, has_side_effects=True, vmem_limit_bytes=60 * MIB
        ),
    )


class Spread:
    STAGES = 4

    def __init__(self, mine, other, send, recv):
        self.refs = (mine, other, send, recv)
        self.rows = mine.shape[0] // 4 // FEW

    @staticmethod
    def scratch():
        return [
            pltpu.SemaphoreType.DMA((Spread.STAGES, FEW)),
            pltpu.SemaphoreType.DMA((Spread.STAGES, FEW)),
        ]

    def copy(self, k, i):
        mine, other, send, recv = self.refs
        x, c, core_peer, x_peer, y_peer = neighbours()

        def rows(at_x):
            start = (at_x * 2 + c) * (mine.shape[0] // 4) + k * self.rows
            return pl.ds(pl.multiple_of(start, self.rows), self.rows)

        at = rows(1 - x) if i == 3 else rows(x)
        peer = (y_peer, x_peer, core_peer, core_peer)[i]
        source = mine if i == 0 else other
        return remote(source.at[at], other.at[at], send.at[i, k], recv.at[i, k], peer)

    def pass_on(self, k):
        self.copy(k, 0).wait_recv()
        self.copy(k, 1).start()
        self.copy(k, 2).start()

    def pass_last(self, k):
        self.copy(k, 1).wait_recv()
        self.copy(k, 3).start()

    def finish(self):
        for k in range(FEW):
            for i in range(4):
                self.copy(k, i).wait_send()


def front(
    q,
    k,
    v,
    o,
    attn_gain,
    mlp_gain,
    query_gain,
    key_gain,
    docs,
    tokens,
    gate,
    up,
    full,
    gains,
    docs_other,
    normed_out,
    gate_up_mine,
    stage,
    gain,
    normed,
    gate_up_stage,
    tokens_mine,
    tokens_other,
    gate_in,
    up_in,
    local,
    stores,
    swap,
    gain_send,
    gain_recv,
    ring_send,
    ring_recv,
    *scratch
):
    dp, mp = lax.axis_index("dp"), lax.axis_index("mp")
    _, _, core_peer, x_peer, y_peer = neighbours()
    n_dp = gains.shape[0]
    n_slabs = n_dp // 2
    y, z = dp % 2, dp // 2
    rows = q.shape[0]
    spread = Spread(tokens, tokens_other, *scratch)

    def peer(j):
        return (lax.rem(dp + j, n_dp), mp)

    def greet_one(j, carry):
        barrier = pltpu.get_barrier_semaphore()
        pl.semaphore_signal(barrier, inc=1, device_id=peer(j), device_id_type=MESH)
        return carry

    lax.fori_loop(1, n_dp, greet_one, 0)
    greet([core_peer, x_peer])
    loads = [
        pltpu.make_async_copy(source, target, local.at[i])
        for i, (source, target) in enumerate(
            ((tokens, tokens_mine), (gate, gate_in), (up, up_in))
        )
    ]
    for load in loads:
        load.start()
    widths = [w.shape[1] // 2 for w in (q, k, v)]
    first = sum(widths)

    def fill(target, row, which):
        at = 0
        for w, size in zip((q, k, v), widths):
            cols = pl.ds(pl.multiple_of(which * size, 128), size)
            target[pl.ds(row, rows), at : at + size] = w[:, cols].astype(BF16)
            at += size
        size = o.shape[0] // 2
        part = o[pl.ds(pl.multiple_of(which * size, 128), size), :].astype(BF16)
        target[pl.ds(row, rows), first : first + size] = part.T

    def block(slab, pair):
        return pl.ds(pl.multiple_of((slab * 2 + pair) * rows, rows), rows)

    swapped = remote(stage, full.at[block(z, y)], swap.at[0, 0], swap.at[1, 0], y_peer)
    docs_swapped = remote(docs, docs_other, swap.at[0, 1], swap.at[1, 1], y_peer)
    mine = pl.ds(pl.multiple_of(y * rows, rows), rows)
    gate_up_swapped = remote(
        gate_up_stage, gate_up_mine.at[mine], swap.at[0, 2], swap.at[1, 2], y_peer
    )

    def ring(step, i):
        slab = lax.rem(z - step + n_slabs, n_slabs)
        at = full.at[block(slab, y if i == 0 else 1 - y)]
        to = (lax.rem(dp + 2, n_dp), mp)
        return remote(at, at, ring_send.at[step, i], ring_recv.at[step, i], to)

    def ring_next(step, i):
        slab = lax.rem(z - step - 1 + 2 * n_slabs, n_slabs)
        at = full.at[block(slab, y if i == 0 else 1 - y)]
        to = (lax.rem(dp + 2, n_dp), mp)
        came = remote(at, at, ring_send.at[step, i], ring_recv.at[step, i], to)
        came.wait_recv()
        if isinstance(step, int) and step + 1 >= n_slabs - 1:
            return
        ring(step + 1, i).start()

    def gain_to(j):
        return remote(gain, gains.at[dp], gain_send.at[j], gain_recv.at[j], peer(j))

    def share(j, carry):
        gain_to(j).start()
        return carry

    def settle(j, carry):
        gain_to(j).wait()
        return carry

    def fill_mlp(gate_up_to, row, which):
        size = gate.shape[1] // 2
        cols = pl.ds(pl.multiple_of(which * size, 128), size)
        gate_up_to[pl.ds(row, rows), :size] = gate_in[:, cols].astype(BF16)
        gate_up_to[pl.ds(row, rows), size:] = up_in[:, cols].astype(BF16)

    fill(stage, 0, 1 - y)
    row = 0
    for values in (attn_gain, mlp_gain, query_gain, key_gain):
        for j, size in gain_rows_of(values.shape[1]):
            part = values[:, j * 128 : j * 128 + size]
            gain[row : row + 1, :size] = part.astype(BF16).astype(F32)
            row += 1
    meet(n_dp - 1 + 2)
    swapped.start()
    fill(full, block(z, y).start, y)
    ring(0, 0).start()
    docs_swapped.start()
    lax.fori_loop(1, n_dp, share, 0)
    for c in range(FEW):
        spread.copy(c, 0).start()
    gains[dp] = gain[...]
    for load in loads[1:]:
        load.wait()
    fill_mlp(gate_up_stage, 0, 1 - y)
    gate_up_swapped.start()
    swapped.wait_recv()
    ring(0, 1).start()
    lax.fori_loop(1, n_dp, settle, 0)
    owned = gain_rows_of(full.shape[0] // n_dp)
    gain_row = jnp.concatenate(
        [gains[i, j : j + 1, :size] for i in range(n_dp) for j, size in owned], -1
    )

    def norm(source, base, start, count):
        def step(at):
            hat = norm_parts(source[at].astype(F32))[0]
            to = pl.ds(pl.multiple_of(base + at.start, TILE), TILE)
            normed[to] = (hat * gain_row).astype(BF16)

        tiles(start, count, step)

    total = tokens.shape[0]
    quarter = total // 4

    def store(i):
        at = pl.ds(i * quarter, quarter)
        return pltpu.make_async_copy(normed.at[at], normed_out.at[at], stores.at[i])

    def norm_mine(i):
        norm(tokens_mine, 0, i * quarter, quarter)
        store(i).start()

    def norm_other():
        for c in range(FEW):
            for i in (2, 3):
                spread.copy(c, i).wait_recv()
        for i in range(4):
            norm(tokens_other, total, i * quarter, quarter)
            store(4 + i).start()

    loads[0].wait()
    early = [functools.partial(fill_mlp, gate_up_mine, mine.start, y)]
    early += [functools.partial(norm_mine, i) for i in range(4)]
    late = [functools.partial(spread.pass_on, c) for c in range(FEW)]
    late += [functools.partial(spread.pass_last, c) for c in range(FEW)]

    def run(jobs):
        for job in jobs:
            job()

    if n_slabs == 4:
        ring_next(0, 0)
        run(early[:3])
        ring_next(0, 1)
        run(early[3:])
        spread.pass_on(0)
        ring_next(1, 0)
        spread.pass_on(1)
        spread.pass_last(0)
        ring_next(1, 1)
        spread.pass_last(1)
        norm_other()
        ring_next(2, 0)
        ring_next(2, 1)
    else:
        run(early)
        run(late)

        def turn(step, carry):
            for i in range(2):
                ring_next(step, i)
            return carry

        lax.fori_loop(0, n_slabs - 2, turn, 0)
        for i in range(2):
            ring_next(n_slabs - 2, i)
        norm_other()
    spread.finish()
    for i in range(8):
        store(i).wait()
    docs_swapped.wait()
    swapped.wait_send()
    gate_up_swapped.wait()

    def sent(step, carry):
        for i in range(2):
            ring(step, i).wait_send()
        return carry

    lax.fori_loop(0, n_slabs - 1, sent, 0)


def gain_rows_of(size):
    return [(j, min(128, size - j * 128)) for j in range(-(-size // 128))]


QUERY_BLOCK = 256
LONGEST = 512


def rolled(values):
    return pltpu.roll(values, HEAD_WIDTH // 2, 1)


def lane_mean(values):
    high = values.astype(BF16)
    low = (values - high.astype(F32)).astype(BF16)
    share = jnp.full((HEAD_WIDTH, HEAD_WIDTH), 1.0 / HEAD_WIDTH, BF16)
    return dot(high, share) + dot(low, share)


def head_norm(raw, h):
    values = raw[:, h * HEAD_WIDTH : (h + 1) * HEAD_WIDTH]
    scaling = lax.rsqrt(lane_mean(values * values) + EPSILON)
    return (values * scaling, scaling)


def rope_of(normed, cosine, sine):
    return (normed * cosine[...] + rolled(normed) * sine[...]).astype(BF16)


def blocks_of(length):
    for start in range(0, length, QUERY_BLOCK):
        first = max(0, start - LONGEST)
        yield slice(start, start + QUERY_BLOCK), slice(first, start + QUERY_BLOCK)


def together(values, rows):
    return values[:, rows].reshape(GROUP * QUERY_BLOCK, HEAD_WIDTH)


def weights_of(query, key, starts, rows, cols):
    size = cols.stop - cols.start
    scores = dot(query, key, 1, 1).reshape(GROUP, QUERY_BLOCK, size)
    shape = (QUERY_BLOCK, size)
    query_index = rows.start + lax.broadcasted_iota(jnp.int32, shape, 0)
    key_index = cols.start + lax.broadcasted_iota(jnp.int32, shape, 1)
    allowed = (key_index <= query_index) & (key_index >= starts[rows])
    scores = jnp.where(allowed[None], scores, MASKED)
    highest = jnp.max(scores, -1, keepdims=True)
    exponent = jnp.exp((scores - highest) * HEAD_WIDTH ** (-0.5))
    weights = exponent * (1.0 / jnp.sum(exponent, -1, keepdims=True))
    return weights.reshape(GROUP * QUERY_BLOCK, size)


def prepare_heads(raw, cosine, sine, gain_query, gain_key, q, k):
    for h in range(GROUP):
        q[h] = rope_of(head_norm(raw, h)[0] * gain_query[...], cosine, sine)
    k[...] = rope_of(head_norm(raw, GROUP)[0] * gain_key[...], cosine, sine)


def attend_forward(raw, cosine, sine, starts, gain_query, gain_key, out, q, k):
    prepare_heads(raw, cosine, sine, gain_query, gain_key, q, k)
    at = (GROUP + 1) * HEAD_WIDTH
    for rows, cols in blocks_of(raw.shape[0]):
        weights = weights_of(together(q, rows), k[cols], starts, rows, cols).astype(BF16)
        value = raw[cols, at : at + HEAD_WIDTH].astype(BF16)
        result = dot(weights, value).astype(BF16).reshape(GROUP, QUERY_BLOCK, HEAD_WIDTH)
        for h in range(GROUP):
            out[rows, h * HEAD_WIDTH : (h + 1) * HEAD_WIDTH] = result[h]


def attend_backward(
    raw,
    cosine,
    sine,
    starts,
    gain_query,
    gain_key,
    grad_hidden,
    normed,
    attended,
    packed,
    mlp_left,
    mlp_right,
    hidden,
    out,
    gains,
    weight_grads,
    output,
    q,
    k,
    v,
    dq,
    dk,
    dv,
    grad,
    total,
    normed_held,
    mlp_left_held,
    mlp_right_held,
    hidden_held,
    loads,
    *scratch
):
    factor = HEAD_WIDTH ** (-0.5)
    at = (GROUP + 1) * HEAD_WIDTH
    inputs = (GROUP + 2) * HEAD_WIDTH
    mlp = Reduce(mlp_left_held, mlp_right_held, mlp_right.shape[0] // 2, *scratch)
    length = raw.shape[0]
    here = pl.ds(pl.multiple_of(pl.program_id(0) * length, length), length)
    normed_load = pltpu.make_async_copy(normed.at[here], normed_held, loads.at[0])
    mlp_loads = [
        pltpu.make_async_copy(source, target, loads.at[i + 1])
        for i, (source, target) in enumerate(
            ((mlp_left, mlp_left_held), (mlp_right, mlp_right_held), (hidden, hidden_held))
        )
    ]

    def mlp_load():
        greet(neighbours()[2:])
        for load in mlp_loads:
            load.start()

    def mlp_begin():
        for load in mlp_loads[:2]:
            load.wait()
        for c in range(FEW):
            mlp.produce(c, False)
            if c == 0:
                meet(3)
            mlp.begin(c)
        for c in range(FEW):
            mlp.produce(c, True)
            mlp.first(c)

    def mlp_second():
        for c in range(FEW):
            mlp.second(c)

    def mlp_end():
        def step(rows):
            output[rows] = (hidden_held[rows] + mlp.take(rows)).astype(BF16)

        mlp_loads[2].wait()

        for c in range(FEW):
            mlp.arrive(c)
            tiles(c * mlp.rows, mlp.rows, step)
        for c in range(FEW):
            mlp.release(c)
        mlp.finish()

    def at_step(step, job):
        pl.when(pl.program_id(0) == step)(job)

    at_step(0, mlp_load)
    normed_load.start()
    prepare_heads(raw, cosine, sine, gain_query, gain_key, q, k)
    v[...] = raw[:, at : at + HEAD_WIDTH].astype(BF16)
    dk[...] = jnp.zeros_like(dk)
    dv[...] = jnp.zeros_like(dv)
    for h in range(GROUP):
        lanes = slice(inputs + h * HEAD_WIDTH, inputs + (h + 1) * HEAD_WIDTH)
        grad[h] = dot(grad_hidden[...], packed[:, lanes]).astype(BF16)
    at_step(0, mlp_begin)
    for n, (rows, cols) in enumerate(blocks_of(length)):
        query, block_grad = together(q, rows), together(grad, rows)
        weights = weights_of(query, k[cols], starts, rows, cols)
        grad_weights = dot(block_grad, v[cols], 1, 1)
        inner = jnp.sum(weights * grad_weights, -1, keepdims=True)
        grad_scores = (weights * (grad_weights - inner)).astype(BF16)
        dq[:, rows] = (dot(grad_scores, k[cols]) * factor).reshape(GROUP, QUERY_BLOCK, HEAD_WIDTH)
        dk[cols] += dot(grad_scores, query, 0, 0) * factor
        dv[cols] += dot(weights.astype(BF16), block_grad, 0, 0)
        if n == 0:
            at_step(1, mlp_second)
    gains[...] = jnp.zeros_like(gains)

    def undo(rot_grad, h, gain, row):
        normed_grad = rot_grad * cosine[...] - rolled(rot_grad) * sine[...]
        hat, inv = head_norm(raw, h)
        gains[0, row : row + 1] += jnp.sum(normed_grad * hat, 0, keepdims=True)
        lanes = slice(h * HEAD_WIDTH, (h + 1) * HEAD_WIDTH)
        scaled = normed_grad * gain[...]
        out[:, lanes] = (inv * (scaled - hat * lane_mean(scaled * hat))).astype(BF16)

    for h in range(GROUP):
        undo(dq[h], h, gain_query, 0)
    undo(dk[...], GROUP, gain_key, 1)
    out[:, at : at + HEAD_WIDTH] = dv[...].astype(BF16)

    @pl.when(pl.program_id(0) == 0)
    def _():
        total[...] = jnp.zeros_like(total)

    out_turned, attended_turned = out[...].T, attended[...].T
    normed_load.wait()
    for start in range(0, normed.shape[1], COLUMNS):
        cols = slice(start, start + COLUMNS)
        total[:inputs, cols] += dot(out_turned, normed_held[:, cols])
        total[inputs:, cols] += dot(attended_turned, grad_hidden[:, cols])

    @pl.when(pl.program_id(0) == pl.num_programs(0) - 1)
    def _():
        size = weight_grads.shape[2]
        for i in range(weight_grads.shape[0]):
            weight_grads[i] = total[:, i * size : (i + 1) * size].astype(BF16)

    at_step(1, mlp_end)


def once(spec):
    return pl.BlockSpec(spec.block_shape, spec.index_map, pipeline_mode=pl.Buffered(1))


def by_rows(rows, cols):
    return pl.BlockSpec((rows, cols), lambda i: (i, 0))


def whole(*shape):
    return pl.BlockSpec(shape, lambda i: (0,) * len(shape))


def call_blocks(
    kernel, steps, in_specs, out_shape, out_specs, scratch, flops, bytes_accessed, **remote_params
):
    return pl.pallas_call(
        kernel,
        out_shape=out_shape,
        grid=(steps,),
        in_specs=in_specs,
        out_specs=out_specs,
        scratch_shapes=scratch,
        name=kernel.__name__,
        cost_estimate=pl.CostEstimate(
            flops=flops, bytes_accessed=bytes_accessed, transcendentals=0
        ),
        compiler_params=pltpu.CompilerParams(
            dimension_semantics=("arbitrary",), vmem_limit_bytes=60 * MIB, **remote_params
        ),
    )


TOKEN_BLOCK = 512
HIDDEN_BLOCK = 256


def mlp_forward(normed, weights, active, gate_slope, up_slope):
    size = active.shape[1]
    for start in range(0, size, HIDDEN_BLOCK):
        cols = slice(start, start + HIDDEN_BLOCK)
        gate = dot(normed[...], weights[:, cols])
        up = dot(normed[...], weights[:, size + start : size + start + HIDDEN_BLOCK])
        sigmoid = jax.nn.sigmoid(gate)
        swish = gate * sigmoid
        active[:, cols] = (swish * up).astype(BF16)
        gate_slope[:, cols] = up * sigmoid * (1.0 + gate * (1.0 - sigmoid))
        up_slope[:, cols] = swish


def mlp_backward(cotangent, weights, gate_slope, up_slope, grads):
    size = gate_slope.shape[1]
    for start in range(0, size, HIDDEN_BLOCK):
        cols = slice(start, start + HIDDEN_BLOCK)
        grad = dot(cotangent[...], weights[:, cols])
        grads[:, cols] = (grad * gate_slope[:, cols]).astype(BF16)
        up_cols = slice(size + start, size + start + HIDDEN_BLOCK)
        grads[:, up_cols] = (grad * up_slope[:, cols]).astype(BF16)


def on_device(
    tokens,
    documents,
    cotangent,
    attn_gain,
    query_gain,
    key_norm_scale,
    query_weight,
    key_projection,
    value_projection,
    output_weight,
    mlp_gain,
    gate_weight,
    up_weight,
    down_weight,
):
    n_dp = lax.axis_size("dp")
    dp, mp = lax.axis_index("dp"), lax.axis_index("mp")
    y = dp % 2
    slabs = [[i + 2 * k for k in range(n_dp // 2)] for i in range(2)]
    rows, width = tokens.shape
    seq_length = documents.shape[1]
    seqs = 2 * documents.shape[0]
    share = rows // 4
    head = HEAD_WIDTH
    query_cols, key_cols, hidden_cols = (
        query_weight.shape[1] // 2,
        key_projection.shape[1] // 2,
        gate_weight.shape[1] // 2,
    )
    attn_cols = query_cols + 2 * key_cols

    def y_swap(values):
        return lax.ppermute(values, "dp", [(i, i ^ 1) for i in range(n_dp)])

    def mp_swap(values, bit):
        return lax.ppermute(values, "mp", [(i, i ^ bit) for i in range(4)])

    def in_order(where, mine, other, axis):
        return jnp.where(
            where == 0,
            jnp.concatenate([mine, other], axis),
            jnp.concatenate([other, mine], axis),
        )

    def half(values, which, axis):
        size = values.shape[axis] // 2
        return lax.dynamic_slice_in_dim(values, which * size, size, axis)

    def slab_gather(values):
        return lax.all_gather(values, "dp", axis=0, tiled=True, axis_index_groups=slabs)

    def slab_scatter(values):
        return lax.psum_scatter(
            values, "dp", scatter_dimension=0, tiled=True, axis_index_groups=slabs
        )

    n_gain, n_head = attn_gain.shape[0], query_gain.shape[0]

    def gain_rows(*parts):
        lead = parts[0].shape[:-1]
        pad = [(0, 0)] * len(lead)
        rows_of = jnp.concatenate(
            [
                jnp.pad(part, pad + [(0, -part.shape[-1] % 128)]).reshape(*lead, -1, 128)
                for part in parts
            ],
            -2,
        )
        return jnp.pad(rows_of, pad + [(0, 8 - rows_of.shape[-2]), (0, 0)])

    def gain_parts_of(rows_of):
        lead, parts, at = rows_of.shape[:-2], [], 0
        for size in (n_gain, n_gain, n_head, n_head):
            n = -(-size // 128)
            part = rows_of[..., at : at + n, :].reshape(*lead, n * 128)
            parts.append(part[..., :size])
            at += n
        return parts

    model_rows = query_weight.shape[0]
    pack_cols = attn_cols + query_cols
    pair_rows = 2 * rows
    n_slabs = n_dp // 2
    attn_full, gains, docs_other, normed_one, mlp_mine = call_leg(
        front,
        3,
        "front",
        [VM] * 9 + [ANY] * 3,
        (
            jax.ShapeDtypeStruct((width, pack_cols), BF16),
            jax.ShapeDtypeStruct((n_dp, 8, 128), F32),
            jax.ShapeDtypeStruct(documents.shape, jnp.int32),
            jax.ShapeDtypeStruct((pair_rows, width), BF16),
            jax.ShapeDtypeStruct((2 * model_rows, 2 * hidden_cols), BF16),
        ),
        (VM, VM, VM, ANY, VM),
        [
            pltpu.VMEM((model_rows, pack_cols), BF16),
            pltpu.VMEM((8, 128), F32),
            pltpu.VMEM((pair_rows, width), BF16),
            pltpu.VMEM((model_rows, 2 * hidden_cols), BF16),
            pltpu.VMEM((rows, width), BF16),
            pltpu.VMEM((rows, width), BF16),
            pltpu.VMEM(gate_weight.shape, F32),
            pltpu.VMEM(up_weight.shape, F32),
            pltpu.SemaphoreType.DMA((3,)),
            pltpu.SemaphoreType.DMA((8,)),
            pltpu.SemaphoreType.DMA((2, 4)),
            pltpu.SemaphoreType.DMA((n_dp,)),
            pltpu.SemaphoreType.DMA((n_dp,)),
            pltpu.SemaphoreType.DMA((n_slabs, 2)),
            pltpu.SemaphoreType.DMA((n_slabs, 2)),
        ]
        + Spread.scratch(),
        250 * MIB,
    )(
        query_weight,
        key_projection,
        value_projection,
        output_weight,
        attn_gain.reshape(1, -1),
        mlp_gain.reshape(1, -1),
        query_gain.reshape(1, -1),
        key_norm_scale.reshape(1, -1),
        documents,
        tokens,
        gate_weight,
        up_weight,
    )
    down_low = down_weight.astype(BF16)
    down_given, _ = lax.optimization_barrier((half(down_low, 1 - y, 0).T, docs_other))
    down_got = y_swap(down_given)

    cot_part = lax.dynamic_slice_in_dim(cotangent, mp * share, share, 0)
    cot_part, _ = lax.optimization_barrier((cot_part, docs_other))
    cot_part = y_swap(cot_part)
    gate_up_full = slab_gather(mlp_mine)
    gain_one, gain_two, gain_query, gain_key = (g.reshape(1, -1) for g in gain_parts_of(gains))
    docs = jnp.concatenate([documents, docs_other], 0)
    tokens_share = lax.dynamic_slice_in_dim(tokens, mp * share, share, 0)
    cot_share = lax.dynamic_slice_in_dim(cotangent, mp * share, share, 0)

    raw = dot(normed_one, attn_full[:, :attn_cols])
    starts = sum((docs < i).sum(1, keepdims=True) * (docs == i) for i in range(1, 4))
    positions = (jnp.arange(seq_length, dtype=jnp.int32)[None] - starts).reshape(pair_rows)
    cosine, sine = rope_tables(positions, head)
    starts = starts.reshape(pair_rows, 1).astype(jnp.int32)
    raw, sine, cot_part = lax.optimization_barrier((raw, sine, cot_part))
    cot_across = mp_swap(cot_part, 2)
    attention_args = (raw, cosine, sine, starts, gain_query, gain_key)
    attention_specs = [
        by_rows(seq_length, attn_cols),
        by_rows(seq_length, head),
        by_rows(seq_length, head),
        by_rows(seq_length, 1),
        whole(1, head),
        whole(1, head),
    ]
    pair_flops = pair_rows * seq_length * query_cols
    attended = call_blocks(
        attend_forward,
        seqs,
        attention_specs,
        jax.ShapeDtypeStruct((pair_rows, query_cols), BF16),
        by_rows(seq_length, query_cols),
        [pltpu.VMEM((GROUP, seq_length, head), BF16), pltpu.VMEM((seq_length, head), BF16)],
        2 * pair_flops,
        20 * MIB,
    )(*attention_args)
    attended, cot_across, down_got = lax.optimization_barrier((attended, cot_across, down_got))
    down_full = slab_gather(in_order(y, half(down_low, y, 0).T, down_got, 0))

    def grouped(cols):
        return (2, 2, 2, share, cols)

    half_width = width // 2
    leg_scratch = Reduce.scratch(share, width, half_width) + Gather.scratch(share, width)
    hidden, normed_two, cot_pair = call_leg(
        attention_leg,
        0,
        "attention_leg",
        [VM] * 4 + [ANY] * 3,
        (
            jax.ShapeDtypeStruct((share, width), F32),
            jax.ShapeDtypeStruct(grouped(width), BF16),
            jax.ShapeDtypeStruct((pair_rows, width), BF16),
        ),
        (VM, ANY, ANY),
        [
            pltpu.VMEM((rows + 2 * share, width), BF16),
            pltpu.SemaphoreType.DMA((3,)),
            pltpu.SemaphoreType.DMA((3,)),
            pltpu.SemaphoreType.DMA((2,)),
            pltpu.SemaphoreType.DMA((2,)),
        ]
        + leg_scratch,
        200 * MIB,
    )(
        attended.reshape(grouped(query_cols)),
        attn_full,
        tokens_share,
        gain_two,
        cotangent,
        cot_part,
        cot_across,
    )
    normed_two = normed_two.reshape(pair_rows, width)

    blocks = pair_rows // TOKEN_BLOCK
    hidden_block = by_rows(TOKEN_BLOCK, hidden_cols)
    hidden_shape = (pair_rows, hidden_cols)
    mlp_flops = 2 * pair_rows * width * hidden_cols
    active, gate_slope, up_slope = call_blocks(
        mlp_forward,
        blocks,
        [by_rows(TOKEN_BLOCK, width), whole(width, 2 * hidden_cols)],
        (
            jax.ShapeDtypeStruct(hidden_shape, BF16),
            jax.ShapeDtypeStruct(hidden_shape, F32),
            jax.ShapeDtypeStruct(hidden_shape, F32),
        ),
        (hidden_block,) * 3,
        [],
        2 * mlp_flops,
        30 * MIB,
    )(normed_two, gate_up_full)
    down_part = dot(cot_pair, active, 0, 0).astype(BF16)
    down_grad = slab_scatter(down_part)
    cot_late, _ = lax.optimization_barrier((cot_pair, down_part))
    grad_gate_up = call_blocks(
        mlp_backward,
        blocks,
        [by_rows(TOKEN_BLOCK, width), whole(width, hidden_cols), hidden_block, hidden_block],
        jax.ShapeDtypeStruct((pair_rows, 2 * hidden_cols), BF16),
        by_rows(TOKEN_BLOCK, 2 * hidden_cols),
        [],
        mlp_flops,
        30 * MIB,
    )(cot_late, down_full, gate_slope, up_slope)
    gate_up_part = dot(normed_two, grad_gate_up, 0, 0).astype(BF16)
    gate_up_grad = slab_scatter(gate_up_part)
    grad_gate_up, _, _ = lax.optimization_barrier((grad_gate_up, gate_up_part, down_part))
    grad_hidden, mlp_gain_part, grad_hidden_low = call_leg(
        hidden_leg,
        1,
        "hidden_leg",
        [ANY] * 2 + [VM] * 3,
        (
            jax.ShapeDtypeStruct((share, width), F32),
            jax.ShapeDtypeStruct((1, width), F32),
            jax.ShapeDtypeStruct(grouped(width), BF16),
        ),
        (VM, VM, ANY),
        [
            pltpu.VMEM(grouped(2 * hidden_cols), BF16),
            pltpu.VMEM((width, 2 * hidden_cols), BF16),
            pltpu.SemaphoreType.DMA((2, CHUNKS)),
            pltpu.SemaphoreType.DMA((width // COLUMNS,)),
        ]
        + leg_scratch,
        200 * MIB,
    )(
        grad_gate_up.reshape(grouped(2 * hidden_cols)),
        gate_up_full,
        hidden,
        cot_share,
        gain_two,
    )
    grad_hidden_low = grad_hidden_low.reshape(pair_rows, width)

    raw_grad, head_gain_parts, attn_grad, layer_output = call_blocks(
        attend_backward,
        seqs,
        [once(spec) for spec in attention_specs]
        + [
            once(by_rows(seq_length, width)),
            ANY,
            once(by_rows(seq_length, query_cols)),
            once(whole(width, pack_cols)),
            ANY,
            ANY,
            ANY,
        ],
        (
            jax.ShapeDtypeStruct((pair_rows, attn_cols), BF16),
            jax.ShapeDtypeStruct((seqs, 8, head), F32),
            jax.ShapeDtypeStruct((n_dp, pack_cols, model_rows), BF16),
            jax.ShapeDtypeStruct((share, width), BF16),
        ),
        (
            once(by_rows(seq_length, attn_cols)),
            pl.BlockSpec((1, 8, head), lambda i: (i, 0, 0)),
            once(whole(n_dp, pack_cols, model_rows)),
            once(whole(share, width)),
        ),
        [
            pltpu.VMEM((GROUP, seq_length, head), BF16),
            pltpu.VMEM((seq_length, head), BF16),
            pltpu.VMEM((seq_length, head), BF16),
            pltpu.VMEM((GROUP, seq_length, head), F32),
            pltpu.VMEM((seq_length, head), F32),
            pltpu.VMEM((seq_length, head), F32),
            pltpu.VMEM((GROUP, seq_length, head), BF16),
            pltpu.VMEM((pack_cols, width), F32),
            pltpu.VMEM((seq_length, width), BF16),
            pltpu.VMEM(grouped(hidden_cols), BF16),
            pltpu.VMEM((width, hidden_cols), BF16),
            pltpu.VMEM((share, width), F32),
            pltpu.SemaphoreType.DMA((4,)),
        ]
        + Reduce.scratch(share, width, half_width, FEW),
        5 * pair_flops + 2 * pair_rows * width * (pack_cols + query_cols + hidden_cols),
        80 * MIB,
        collective_id=4,
        has_side_effects=True,
    )(
        *attention_args,
        grad_hidden_low,
        normed_one,
        attended,
        attn_full,
        active.reshape(grouped(hidden_cols)),
        down_full,
        hidden,
    )
    head_gain_parts = head_gain_parts.sum(0)
    attn_grad = attn_grad.reshape(n_dp * pack_cols, model_rows)
    attn_grad, raw_grad, gate_up_grad, down_grad = lax.optimization_barrier(
        (attn_grad, raw_grad, gate_up_grad, down_grad)
    )
    attn_parts = attn_grad.reshape(n_dp, pack_cols, model_rows)
    attn_grad = slab_scatter(attn_grad).reshape(2, pack_cols, model_rows)
    gain_parts = gain_rows(
        jnp.zeros((n_dp, n_gain), F32),
        mlp_gain_part.reshape(n_dp, n_gain),
        head_gain_parts[0].reshape(n_dp, n_head),
        head_gain_parts[1].reshape(n_dp, n_head),
    )

    low = 7 * width // 8
    input_grad, gain_sums, gate_up_other, down_other = call_leg(
        output_leg,
        2,
        "output_leg",
        [VM] * 7 + [ANY] * 2,
        (
            jax.ShapeDtypeStruct((share, width), F32),
            jax.ShapeDtypeStruct((8, 128), F32),
            jax.ShapeDtypeStruct((model_rows, 2 * hidden_cols), BF16),
            jax.ShapeDtypeStruct((model_rows, hidden_cols), BF16),
        ),
        (VM, VM, ANY, ANY),
        [
            pltpu.VMEM((n_dp, 8, 128), F32),
            pltpu.SemaphoreType.DMA((2,)),
            pltpu.SemaphoreType.DMA((2,)),
        ]
        + Reduce.scratch(share, width, low)
        + SumGains.scratch(n_dp, 4),
        200 * MIB,
    )(
        raw_grad.reshape(grouped(attn_cols)),
        attn_full,
        tokens_share,
        gain_one,
        gain_parts,
        attn_parts,
        grad_hidden,
        gate_up_grad,
        down_grad,
    )
    attn_given = lax.dynamic_index_in_dim(attn_grad, 1 - y, 0, False)
    attn_given, gate_up_other, down_other = lax.optimization_barrier(
        (attn_given, gate_up_other, down_other)
    )

    def columns(own, other, start, axis=1):
        own = half(own, y, 0)[:, start : start + hidden_cols]
        other = other[:, start : start + hidden_cols]
        if axis == 0:
            own, other = own.T, other.T
        return in_order(y, own, other, axis).astype(F32)

    gate_grad = columns(gate_up_grad, gate_up_other, 0)
    up_grad = columns(gate_up_grad, gate_up_other, hidden_cols)
    down_grad = columns(down_grad, down_other, 0, 0)

    attn_other = y_swap(attn_given)
    attn_own = lax.dynamic_index_in_dim(attn_grad, y, 0, False)

    def attn_columns(start, size, turn=True):
        own, other = attn_own[start : start + size], attn_other[start : start + size]
        if turn:
            own, other = own.T, other.T
        return in_order(y, own, other, int(turn)).astype(F32)

    query_grad = attn_columns(0, query_cols)
    key_grad = attn_columns(query_cols, key_cols)
    value_grad = attn_columns(query_cols + key_cols, key_cols)
    output_grad = attn_columns(attn_cols, query_cols, False)
    attn_gain_grad, mlp_gain_grad, query_gain_grad, key_gain_grad = gain_parts_of(gain_sums)
    return (
        layer_output,
        input_grad,
        attn_gain_grad,
        query_gain_grad,
        key_gain_grad,
        query_grad,
        key_grad,
        value_grad,
        output_grad,
        mlp_gain_grad,
        gate_grad,
        up_grad,
        down_grad,
    )


def solution(mesh):
    in_specs = (
        P("dp", None),
        P("dp", None),
        P("dp", None),
        P("dp"),
        P("dp"),
        P("dp"),
        P("dp", "mp"),
        P("dp", "mp"),
        P("dp", "mp"),
        P("mp", "dp"),
        P("dp"),
        P("dp", "mp"),
        P("dp", "mp"),
        P("mp", "dp"),
    )
    out_specs = (
        P(("dp", "mp"), None),
        P(("dp", "mp"), None),
        P("dp"),
        P("dp"),
        P("dp"),
        P("dp", "mp"),
        P("dp", "mp"),
        P("dp", "mp"),
        P("mp", "dp"),
        P("dp"),
        P("dp", "mp"),
        P("dp", "mp"),
        P("mp", "dp"),
    )
    return jax.shard_map(
        on_device, mesh=mesh, in_specs=in_specs, out_specs=out_specs, check_vma=False
    )
```

```python
import functools

import jax
import jax.numpy as jnp
from jax import lax
from jax.experimental import pallas as pl
from jax.experimental.pallas import tpu as pltpu
from jax.sharding import PartitionSpec as P

QUERY_HEADS = 16
KEY_VALUE_HEADS = 8
HEAD_WIDTH = 128
GROUP = QUERY_HEADS // KEY_VALUE_HEADS

EPSILON = 1e-06
MASKED = -1e30
MESH = pl.DeviceIdType.MESH
F32 = jnp.float32
BF16 = jnp.bfloat16
MIB = 2**20


def rope_tables(positions, head_size):
    middle = head_size // 2
    frequency = jnp.power(1000000.0, -2.0 * jnp.arange(middle, dtype=F32) / head_size)
    angles = positions.astype(F32)[:, None] * frequency[None, :]
    cosine_table = jnp.cos(angles)
    sine_table = jnp.sin(angles)
    return (
        jnp.concatenate([cosine_table, cosine_table], -1),
        jnp.concatenate([-sine_table, sine_table], -1),
    )


def norm_parts(values):
    scaling = lax.rsqrt(jnp.mean(values * values, -1, keepdims=True) + EPSILON)
    return (values * scaling, scaling)


def norm_back(grad_normed, normed_hat, scaling, gains):
    scaled = grad_normed * gains
    return scaling * (scaled - normed_hat * jnp.mean(scaled * normed_hat, -1, keepdims=True))


def dot(left, right, left_dim=1, right_dim=0):
    return lax.dot_general(
        left, right, (((left_dim,), (right_dim,)), ((), ())), preferred_element_type=F32
    )


CHUNKS = 4
FEW = 2
TILE = 32
COLUMNS = 512


def neighbours():
    dp, mp = lax.axis_index("dp"), lax.axis_index("mp")
    x, c = mp // 2, mp % 2
    return (
        x,
        c,
        (dp, x * 2 + 1 - c),
        (dp, (1 - x) * 2 + c),
        (dp + 1 - 2 * (dp % 2), mp),
    )


def greet(peers):
    barrier = pltpu.get_barrier_semaphore()
    for peer in peers:
        pl.semaphore_signal(barrier, inc=1, device_id=peer, device_id_type=MESH)


def meet(count):
    pl.semaphore_wait(pltpu.get_barrier_semaphore(), count)


def remote(src, dst, send, recv, peer):
    return pltpu.make_async_remote_copy(
        src_ref=src, dst_ref=dst, send_sem=send, recv_sem=recv, device_id=peer, device_id_type=MESH
    )


def tiles(start, rows, step):
    def body(i, carry):
        step(pl.ds(pl.multiple_of(start + i * TILE, TILE), TILE))
        return carry

    lax.fori_loop(0, rows // TILE, body, 0)


class Reduce:
    STAGES = 5

    def __init__(self, left, right, low, part, mine, got, gx, gy, fx, fy, send, recv, load=None):
        self.left, self.right, self.low, self.load = left, right, low, load
        self.refs = (part, mine, got, gx, gy, fx, fy, send, recv)
        self.chunks = send.shape[1]
        self.rows = mine.shape[2] // self.chunks
        self.width = mine.shape[3]

    @staticmethod
    def scratch(rows, width, low, chunks=CHUNKS):
        high = width - low
        return [
            pltpu.VMEM((2, 2, rows, width), BF16),
            pltpu.VMEM((2, 2, rows, width), BF16),
            pltpu.VMEM((2, 2, rows, width), BF16),
            pltpu.VMEM((2, rows, low), BF16),
            pltpu.VMEM((2, rows, high), BF16),
            pltpu.VMEM((rows, high), BF16),
            pltpu.VMEM((rows, low), BF16),
            pltpu.SemaphoreType.DMA((Reduce.STAGES, chunks)),
            pltpu.SemaphoreType.DMA((Reduce.STAGES, chunks)),
        ]

    def lanes(self):
        return pl.ds(0, self.low), pl.ds(self.low, self.width - self.low)

    def load_left(self, k, own):
        source, _, sems, _ = self.load
        core = neighbours()[1]
        at = (slice(None), slice(None), core if own else 1 - core, pl.ds(k * self.rows, self.rows))
        return pltpu.make_async_copy(source.at[at], self.left.at[at], sems.at[int(own), k])

    def load_right(self, j):
        _, source, _, sems = self.load
        at = pl.ds(pl.multiple_of(j * COLUMNS, COLUMNS), COLUMNS)
        return pltpu.make_async_copy(source.at[at], self.right.at[at], sems.at[j])

    def start_loads(self):
        self.load_left(0, False).start()
        for j in range(self.width // COLUMNS):
            self.load_right(j).start()
        self.load_left(0, True).start()
        for k in range(1, self.chunks):
            for own in (False, True):
                self.load_left(k, own).start()

    def copy(self, k, i):
        part, mine, got, gx, gy, fx, fy, send, recv = self.refs
        x, _, core_peer, x_peer, y_peer = neighbours()
        rows = pl.ds(k * self.rows, self.rows)
        low, high = self.lanes()
        s = [send.at[j, k] for j in range(self.STAGES)]
        r = [recv.at[j, k] for j in range(self.STAGES)]
        all_copies = (
            lambda: remote(part.at[:, :, rows], got.at[:, :, rows], s[0], r[0], core_peer),
            lambda: remote(mine.at[:, 1 - x, rows, low], gx.at[:, rows], s[1], r[1], x_peer),
            lambda: remote(mine.at[1, :, rows, high], gy.at[:, rows], s[2], r[2], y_peer),
            lambda: remote(mine.at[1, x, rows, low], fy.at[rows], s[3], r[3], y_peer),
            lambda: remote(mine.at[0, 1 - x, rows, high], fx.at[rows], s[4], r[4], x_peer),
        )
        return all_copies[i]()

    def produce(self, k, own):
        target = self.refs[1] if own else self.refs[0]
        core = neighbours()[1]
        core = core if own else 1 - core
        rows = pl.ds(k * self.rows, self.rows)
        depth = self.left.shape[4]
        if self.load is not None:
            self.load_left(k, own).wait()

        def tile(j, carry):
            if self.load is not None and k == 0 and not own:
                self.load_right(j).wait()
            cols = pl.ds(pl.multiple_of(j * COLUMNS, COLUMNS), COLUMNS)
            left = self.left[:, :, core, rows, :].reshape(4 * self.rows, depth)
            product = dot(left, self.right[cols, :], 1, 1).astype(BF16)
            target[:, :, rows, cols] = product.reshape(2, 2, self.rows, COLUMNS)
            return carry

        lax.fori_loop(0, self.width // COLUMNS, tile, 0)

    def begin(self, k):
        self.copy(k, 0).start()

    def release(self, k):
        self.copy(k, 0).wait_send()

    def first(self, k):
        mine, got = self.refs[1:3]
        self.copy(k, 0).wait_recv()

        def add(i, carry):
            def step(rows):
                at = (i // 2, i % 2, rows)
                mine[at] = mine[at] + got[at]

            tiles(k * self.rows, self.rows, step)
            return carry

        lax.fori_loop(0, 4, add, 0)
        self.copy(k, 1).start()
        self.copy(k, 2).start()

    def second(self, k):
        mine, _, gx, gy = self.refs[1:5]
        x = neighbours()[0]
        low, high = self.lanes()
        self.copy(k, 1).wait_recv()

        def step_low(rows):
            for i in range(2):
                at = (i, x, rows, low)
                mine[at] = mine[at] + gx[i, rows]

        tiles(k * self.rows, self.rows, step_low)
        self.copy(k, 3).start()
        self.copy(k, 2).wait_recv()

        def step_high(rows):
            for i in range(2):
                at = (0, i, rows, high)
                mine[at] = mine[at] + gy[i, rows]

        tiles(k * self.rows, self.rows, step_high)
        self.copy(k, 4).start()

    def arrive(self, k):
        self.copy(k, 3).wait_recv()
        self.copy(k, 4).wait_recv()

    def take(self, rows):
        mine, fx, fy = self.refs[1], *self.refs[5:7]
        x = neighbours()[0]
        low, high = self.lanes()
        return jnp.concatenate(
            [
                mine[0, x, rows, low].astype(F32) + fy[rows].astype(F32),
                mine[0, x, rows, high].astype(F32) + fx[rows].astype(F32),
            ],
            -1,
        )

    def finish(self):
        for k in range(self.chunks):
            for i in range(1, 5):
                self.copy(k, i).wait_send()


class Gather:
    STAGES = 9

    def __init__(self, mine, full, local, send, recv):
        self.refs = (mine, full, local, send, recv)
        self.rows = mine.shape[0] // CHUNKS
        self.half = mine.shape[1] // 2

    @staticmethod
    def scratch(rows, width):
        return [
            pltpu.VMEM((rows, width), BF16),
            pltpu.SemaphoreType.DMA((CHUNKS,)),
            pltpu.SemaphoreType.DMA((Gather.STAGES, CHUNKS)),
            pltpu.SemaphoreType.DMA((Gather.STAGES, CHUNKS)),
        ]

    def copy(self, k, i):
        mine, full, local, send, recv = self.refs
        x, c, core_peer, x_peer, y_peer = neighbours()
        rows = pl.ds(k * self.rows, self.rows)
        low, high = pl.ds(0, self.half), pl.ds(self.half, self.half)
        s = [send.at[j, k] for j in range(self.STAGES)]
        r = [recv.at[j, k] for j in range(self.STAGES)]

        def pass_on(j, at, peer):
            return lambda: remote(full.at[at], full.at[at], s[j], r[j], peer)

        all_copies = (
            lambda: pltpu.make_async_copy(mine.at[rows], full.at[0, x, c, rows], local.at[k]),
            lambda: remote(mine.at[rows, low], full.at[1, x, c, rows, low], s[0], r[0], y_peer),
            lambda: remote(mine.at[rows, high], full.at[0, x, c, rows, high], s[1], r[1], x_peer),
            lambda: remote(mine.at[rows], full.at[0, x, c, rows], s[2], r[2], core_peer),
            pass_on(3, (slice(None), x, c, rows, low), x_peer),
            lambda: remote(
                full.at[0, :, c, rows, high], full.at[1, :, c, rows, high], s[4], r[4], y_peer
            ),
            pass_on(5, (1, x, c, rows, low), core_peer),
            pass_on(6, (0, 1 - x, c, rows, high), core_peer),
            pass_on(7, (slice(None), 1 - x, c, rows, low), core_peer),
            pass_on(8, (1, slice(None), c, rows, high), core_peer),
        )
        return all_copies[i]()

    def begin(self, k):
        for i in (1, 2, 0, 3):
            self.copy(k, i).start()

    def second(self, k):
        self.copy(k, 0).wait()
        self.copy(k, 1).wait_recv()
        self.copy(k, 4).start()
        self.copy(k, 2).wait_recv()
        for i in (5, 6, 7):
            self.copy(k, i).start()

    def third(self, k):
        for i in (4, 5):
            self.copy(k, i).wait_recv()
            self.copy(k, i + 4).start()

    def finish(self):
        for k in range(CHUNKS):
            for i in (3, 6, 7, 8, 9):
                self.copy(k, i).wait_recv()
            for i in range(1, 10):
                self.copy(k, i).wait_send()


N_REDUCE = len(Reduce.scratch(32, 256, 128))


def nothing():
    pass


def leg(left, right, low, full, step, scratch, at_start=nothing, at_middle=nothing, load=None):
    reduce = Reduce(left, right, low, *scratch[:N_REDUCE], load=load)
    if load is not None:
        reduce.start_loads()
    gather = Gather(scratch[N_REDUCE], full, *scratch[N_REDUCE + 1 :])
    mine = scratch[N_REDUCE]
    greet(neighbours()[2:])
    for k in range(CHUNKS):
        reduce.produce(k, False)
        if k == 0:
            meet(3)
        reduce.begin(k)
        reduce.produce(k, True)
        reduce.first(k)
    at_start()
    for k in range(CHUNKS):
        reduce.second(k)
    at_middle()

    def step_at(rows):
        mine[rows] = step(rows, reduce.take(rows)).astype(BF16)

    for k in range(CHUNKS):
        reduce.arrive(k)
        tiles(k * reduce.rows, reduce.rows, step_at)
        gather.begin(k)
    for k in range(CHUNKS):
        gather.second(k)
    for k in range(CHUNKS):
        gather.third(k)
    gather.finish()
    for k in range(CHUNKS):
        reduce.release(k)
    reduce.finish()


def attention_leg(
    left,
    packed,
    tokens,
    gain,
    cotangent,
    cot_part,
    cot_across,
    hidden,
    normed,
    cot_pair,
    cot_buffer,
    cot_in,
    cot_out,
    cot_send,
    cot_recv,
    *scratch
):
    def step(rows, total):
        h = tokens[rows].astype(F32) + total
        hidden[rows] = h
        return norm_parts(h)[0] * gain[...]

    x, core, core_peer = neighbours()[:3]
    own, share = cotangent.shape[0], cot_part.shape[0]

    def place(at_x, at_core):
        start = own + (at_x * 2 + at_core) * share
        return pl.ds(pl.multiple_of(start, share), share)

    sources = (cotangent, cot_part, cot_across)
    starts = (0, own, own + share)
    places = (pl.ds(0, own), place(x, core), place(1 - x, core))
    loads, stores, sends = [], [], []
    for i in range(3):
        held = cot_buffer.at[pl.ds(starts[i], sources[i].shape[0])]
        loads.append(pltpu.make_async_copy(sources[i], held, cot_in.at[i]))
        stores.append(pltpu.make_async_copy(held, cot_pair.at[places[i]], cot_out.at[i]))
        if i > 0:
            to = cot_pair.at[places[i]]
            sends.append(remote(sources[i], to, cot_send.at[i - 1], cot_recv.at[i - 1], core_peer))

    def at_start():
        for copy in loads + sends:
            copy.start()

    def at_middle():
        for load, store in zip(loads, stores):
            load.wait()
            store.start()

    depth = left.shape[4]
    right = packed.at[:, pl.ds(packed.shape[1] - depth, depth)]
    leg(left, right, right.shape[0] // 2, normed, step, scratch, at_start, at_middle)
    for copy in stores + sends:
        copy.wait()


def hidden_leg(
    left,
    right,
    hidden,
    cotangent,
    gain,
    grad_hidden,
    gain_grad,
    full,
    left_held,
    right_held,
    left_sems,
    right_sems,
    *scratch
):
    def step(rows, grad):
        hat, inv = norm_parts(hidden[rows])
        gain_grad[...] += jnp.sum(grad * hat, 0, keepdims=True)
        grad = cotangent[rows].astype(F32) + norm_back(grad, hat, inv, gain[...])
        grad_hidden[rows] = grad
        return grad

    gain_grad[...] = jnp.zeros_like(gain_grad)
    load = (left, right, left_sems, right_sems)
    leg(left_held, right_held, right.shape[0] // 2, full, step, scratch, load=load)


class SumGains:
    def __init__(self, parts, total, got, mid, others, send, recv, send_mp, recv_mp):
        self.refs = (parts, total, got, mid, others, send, recv, send_mp, recv_mp)
        self.n_dp, self.n_mp = parts.shape[0], others.shape[0] + 1

    @staticmethod
    def scratch(n_dp, n_mp):
        return [
            pltpu.VMEM((n_dp, 8, 128), F32),
            pltpu.VMEM((8, 128), F32),
            pltpu.VMEM((n_mp - 1, 8, 128), F32),
            pltpu.SemaphoreType.DMA((n_dp,)),
            pltpu.SemaphoreType.DMA((n_dp,)),
            pltpu.SemaphoreType.DMA((n_mp,)),
            pltpu.SemaphoreType.DMA((n_mp,)),
        ]

    def across(self, j):
        return (lax.rem(lax.axis_index("dp") + j, self.n_dp), lax.axis_index("mp"))

    def along(self, j):
        return (lax.axis_index("dp"), lax.rem(lax.axis_index("mp") + j, self.n_mp))

    def greet(self):
        barrier = pltpu.get_barrier_semaphore()

        def one(j, carry):
            pl.semaphore_signal(barrier, inc=1, device_id=self.across(j), device_id_type=MESH)
            return carry

        lax.fori_loop(1, self.n_dp, one, 0)
        greet([self.along(j) for j in range(1, self.n_mp)])

    def first(self, j):
        parts, _, got, _, _, send, recv = self.refs[:7]
        to = self.across(j)
        return remote(parts.at[to[0]], got.at[j], send.at[j], recv.at[j], to)

    def second(self, j):
        mid, others = self.refs[3:5]
        send, recv = self.refs[7:]
        return remote(mid, others.at[j - 1], send.at[j], recv.at[j], self.along(j))

    def begin(self):
        def start(j, carry):
            self.first(j).start()
            return carry

        lax.fori_loop(1, self.n_dp, start, 0)

    def pass_on(self):
        parts, _, got, mid = self.refs[:4]
        mid[...] = parts[lax.axis_index("dp")]

        def add(j, carry):
            self.first(j).wait()
            mid[...] += got[j]
            return carry

        lax.fori_loop(1, self.n_dp, add, 0)
        for j in range(1, self.n_mp):
            self.second(j).start()

    def finish(self):
        _, total, _, mid, others = self.refs[:5]
        result = mid[...]
        for j in range(1, self.n_mp):
            self.second(j).wait()
            result += others[j - 1]
        total[...] = result


def output_leg(
    left,
    packed,
    tokens,
    gain,
    gain_parts,
    weight_grads,
    grad_hidden,
    gate_up_grad,
    down_grad,
    input_grad,
    gain_total,
    gate_up_other,
    down_other,
    slots,
    swap_send,
    swap_recv,
    *scratch
):
    low = scratch[3].shape[2]
    depth = left.shape[4]
    right = packed.at[:, pl.ds(0, depth)]
    reduce = Reduce(left, right, low, *scratch[:N_REDUCE])
    sums = SumGains(slots, gain_total, *scratch[N_REDUCE:])
    y, y_peer = lax.axis_index("dp") % 2, neighbours()[4]
    half = gate_up_other.shape[0]
    theirs = pl.ds(pl.multiple_of((1 - y) * half, half), half)
    swaps = [
        remote(gate_up_grad.at[theirs], gate_up_other, swap_send.at[0], swap_recv.at[0], y_peer),
        remote(down_grad.at[theirs], down_other, swap_send.at[1], swap_recv.at[1], y_peer),
    ]

    def step(rows):
        grad = reduce.take(rows)
        hat, inv = norm_parts(tokens[rows].astype(F32))
        input_grad[rows] = grad_hidden[rows] + norm_back(grad, hat, inv, gain[...])

    sums.greet()
    slots[...] = gain_parts[...]
    meet(sums.n_dp + sums.n_mp - 2)
    swaps[0].start()
    for k in range(reduce.chunks):
        reduce.produce(k, False)
        reduce.begin(k)
        reduce.produce(k, True)
        reduce.first(k)
    swaps[1].start()
    owned = weight_grads.shape[2]
    diagonal = lax.broadcasted_iota(jnp.int32, (owned, owned), 0) == lax.broadcasted_iota(
        jnp.int32, (owned, owned), 1
    )
    for i in range(sums.n_dp):
        product = dot(right[i * owned : (i + 1) * owned, :], weight_grads[i, :depth, :])
        sums_of = jnp.sum(jnp.where(diagonal, product, 0.0), 0, keepdims=True)
        sums_of = sums_of / gain[:, i * owned : (i + 1) * owned]
        for j, size in gain_rows_of(owned):
            slots[i, j : j + 1, :size] = sums_of[:, j * 128 : j * 128 + size]
    sums.begin()
    for k in range(reduce.chunks):
        reduce.second(k)
    sums.pass_on()
    for k in range(reduce.chunks):
        reduce.arrive(k)
        tiles(k * reduce.rows, reduce.rows, step)
    sums.finish()
    for k in range(reduce.chunks):
        reduce.release(k)
    for copy in swaps:
        copy.wait()
    reduce.finish()


ANY = pl.BlockSpec(memory_space=pl.ANY)
VM = pl.BlockSpec(memory_space=pltpu.VMEM)


def call_leg(kernel, ident, name, in_specs, out_shape, out_specs, scratch, bytes_moved):
    return pl.pallas_call(
        kernel,
        out_shape=out_shape,
        in_specs=in_specs,
        out_specs=out_specs,
        scratch_shapes=scratch,
        name=name,
        cost_estimate=pl.CostEstimate(flops=0, bytes_accessed=bytes_moved, transcendentals=0),
        compiler_params=pltpu.CompilerParams(
            collective_id=ident, has_side_effects=True, vmem_limit_bytes=60 * MIB
        ),
    )


class Spread:
    STAGES = 4

    def __init__(self, mine, other, send, recv):
        self.refs = (mine, other, send, recv)
        self.rows = mine.shape[0] // 4 // FEW

    @staticmethod
    def scratch():
        return [
            pltpu.SemaphoreType.DMA((Spread.STAGES, FEW)),
            pltpu.SemaphoreType.DMA((Spread.STAGES, FEW)),
        ]

    def copy(self, k, i):
        mine, other, send, recv = self.refs
        x, c, core_peer, x_peer, y_peer = neighbours()

        def rows(at_x):
            start = (at_x * 2 + c) * (mine.shape[0] // 4) + k * self.rows
            return pl.ds(pl.multiple_of(start, self.rows), self.rows)

        at = rows(1 - x) if i == 3 else rows(x)
        peer = (y_peer, x_peer, core_peer, core_peer)[i]
        source = mine if i == 0 else other
        return remote(source.at[at], other.at[at], send.at[i, k], recv.at[i, k], peer)

    def pass_on(self, k):
        self.copy(k, 0).wait_recv()
        self.copy(k, 1).start()
        self.copy(k, 2).start()

    def pass_last(self, k):
        self.copy(k, 1).wait_recv()
        self.copy(k, 3).start()

    def finish(self):
        for k in range(FEW):
            for i in range(4):
                self.copy(k, i).wait_send()


def front(
    q,
    k,
    v,
    o,
    attn_gain,
    mlp_gain,
    query_gain,
    key_gain,
    docs,
    tokens,
    gate,
    up,
    full,
    gains,
    docs_other,
    normed_out,
    gate_up_mine,
    stage,
    gain,
    normed,
    gate_up_stage,
    tokens_mine,
    tokens_other,
    gate_in,
    up_in,
    local,
    stores,
    swap,
    gain_send,
    gain_recv,
    ring_send,
    ring_recv,
    *scratch
):
    dp, mp = lax.axis_index("dp"), lax.axis_index("mp")
    _, _, core_peer, x_peer, y_peer = neighbours()
    n_dp = gains.shape[0]
    n_slabs = n_dp // 2
    y, z = dp % 2, dp // 2
    rows = q.shape[0]
    spread = Spread(tokens, tokens_other, *scratch)

    def peer(j):
        return (lax.rem(dp + j, n_dp), mp)

    def greet_one(j, carry):
        barrier = pltpu.get_barrier_semaphore()
        pl.semaphore_signal(barrier, inc=1, device_id=peer(j), device_id_type=MESH)
        return carry

    lax.fori_loop(1, n_dp, greet_one, 0)
    greet([core_peer, x_peer])
    loads = [
        pltpu.make_async_copy(source, target, local.at[i])
        for i, (source, target) in enumerate(
            ((tokens, tokens_mine), (gate, gate_in), (up, up_in))
        )
    ]
    for load in loads:
        load.start()
    widths = [w.shape[1] // 2 for w in (q, k, v)]
    first = sum(widths)

    def fill(target, row, which):
        at = 0
        for w, size in zip((q, k, v), widths):
            cols = pl.ds(pl.multiple_of(which * size, 128), size)
            target[pl.ds(row, rows), at : at + size] = w[:, cols].astype(BF16)
            at += size
        size = o.shape[0] // 2
        part = o[pl.ds(pl.multiple_of(which * size, 128), size), :].astype(BF16)
        target[pl.ds(row, rows), first : first + size] = part.T

    def block(slab, pair):
        return pl.ds(pl.multiple_of((slab * 2 + pair) * rows, rows), rows)

    swapped = remote(stage, full.at[block(z, y)], swap.at[0, 0], swap.at[1, 0], y_peer)
    docs_swapped = remote(docs, docs_other, swap.at[0, 1], swap.at[1, 1], y_peer)
    mine = pl.ds(pl.multiple_of(y * rows, rows), rows)
    gate_up_swapped = remote(
        gate_up_stage, gate_up_mine.at[mine], swap.at[0, 2], swap.at[1, 2], y_peer
    )

    def ring(step, i):
        slab = lax.rem(z - step + n_slabs, n_slabs)
        at = full.at[block(slab, y if i == 0 else 1 - y)]
        to = (lax.rem(dp + 2, n_dp), mp)
        return remote(at, at, ring_send.at[step, i], ring_recv.at[step, i], to)

    def ring_next(step, i):
        slab = lax.rem(z - step - 1 + 2 * n_slabs, n_slabs)
        at = full.at[block(slab, y if i == 0 else 1 - y)]
        to = (lax.rem(dp + 2, n_dp), mp)
        came = remote(at, at, ring_send.at[step, i], ring_recv.at[step, i], to)
        came.wait_recv()
        if isinstance(step, int) and step + 1 >= n_slabs - 1:
            return
        ring(step + 1, i).start()

    def gain_to(j):
        return remote(gain, gains.at[dp], gain_send.at[j], gain_recv.at[j], peer(j))

    def share(j, carry):
        gain_to(j).start()
        return carry

    def settle(j, carry):
        gain_to(j).wait()
        return carry

    def fill_mlp(gate_up_to, row, which):
        size = gate.shape[1] // 2
        cols = pl.ds(pl.multiple_of(which * size, 128), size)
        gate_up_to[pl.ds(row, rows), :size] = gate_in[:, cols].astype(BF16)
        gate_up_to[pl.ds(row, rows), size:] = up_in[:, cols].astype(BF16)

    fill(stage, 0, 1 - y)
    row = 0
    for values in (attn_gain, mlp_gain, query_gain, key_gain):
        for j, size in gain_rows_of(values.shape[1]):
            part = values[:, j * 128 : j * 128 + size]
            gain[row : row + 1, :size] = part.astype(BF16).astype(F32)
            row += 1
    meet(n_dp - 1 + 2)
    swapped.start()
    fill(full, block(z, y).start, y)
    ring(0, 0).start()
    docs_swapped.start()
    lax.fori_loop(1, n_dp, share, 0)
    for c in range(FEW):
        spread.copy(c, 0).start()
    gains[dp] = gain[...]
    for load in loads[1:]:
        load.wait()
    fill_mlp(gate_up_stage, 0, 1 - y)
    gate_up_swapped.start()
    swapped.wait_recv()
    ring(0, 1).start()
    lax.fori_loop(1, n_dp, settle, 0)
    owned = gain_rows_of(full.shape[0] // n_dp)
    gain_row = jnp.concatenate(
        [gains[i, j : j + 1, :size] for i in range(n_dp) for j, size in owned], -1
    )

    def norm(source, base, start, count):
        def step(at):
            hat = norm_parts(source[at].astype(F32))[0]
            to = pl.ds(pl.multiple_of(base + at.start, TILE), TILE)
            normed[to] = (hat * gain_row).astype(BF16)

        tiles(start, count, step)

    total = tokens.shape[0]
    quarter = total // 4

    def store(i):
        at = pl.ds(i * quarter, quarter)
        return pltpu.make_async_copy(normed.at[at], normed_out.at[at], stores.at[i])

    def norm_mine(i):
        norm(tokens_mine, 0, i * quarter, quarter)
        store(i).start()

    def norm_other():
        for c in range(FEW):
            for i in (2, 3):
                spread.copy(c, i).wait_recv()
        for i in range(4):
            norm(tokens_other, total, i * quarter, quarter)
            store(4 + i).start()

    loads[0].wait()
    early = [functools.partial(fill_mlp, gate_up_mine, mine.start, y)]
    early += [functools.partial(norm_mine, i) for i in range(4)]
    late = [functools.partial(spread.pass_on, c) for c in range(FEW)]
    late += [functools.partial(spread.pass_last, c) for c in range(FEW)]

    def run(jobs):
        for job in jobs:
            job()

    if n_slabs == 4:
        ring_next(0, 0)
        run(early[:3])
        ring_next(0, 1)
        run(early[3:])
        spread.pass_on(0)
        ring_next(1, 0)
        spread.pass_on(1)
        spread.pass_last(0)
        ring_next(1, 1)
        spread.pass_last(1)
        norm_other()
        ring_next(2, 0)
        ring_next(2, 1)
    else:
        run(early)
        run(late)

        def turn(step, carry):
            for i in range(2):
                ring_next(step, i)
            return carry

        lax.fori_loop(0, n_slabs - 2, turn, 0)
        for i in range(2):
            ring_next(n_slabs - 2, i)
        norm_other()
    spread.finish()
    for i in range(8):
        store(i).wait()
    docs_swapped.wait()
    swapped.wait_send()
    gate_up_swapped.wait()

    def sent(step, carry):
        for i in range(2):
            ring(step, i).wait_send()
        return carry

    lax.fori_loop(0, n_slabs - 1, sent, 0)


def gain_rows_of(size):
    return [(j, min(128, size - j * 128)) for j in range(-(-size // 128))]


def finish_attention(own, other, q, k, v, o):
    y = lax.axis_index("dp") % 2

    def place(source, which):
        at = 0
        for w in (q, k, v):
            size = w.shape[1] // 2
            cols = pl.ds(pl.multiple_of(which * size, 128), size)
            w[:, cols] = source[at : at + size, :].T.astype(F32)
            at += size
        size = o.shape[0] // 2
        rows = pl.ds(pl.multiple_of(which * size, size), size)
        o[rows, :] = source[at : at + size, :].astype(F32)

    place(own, y)
    place(other, 1 - y)


QUERY_BLOCK = 256
LONGEST = 512


def rolled(values):
    return pltpu.roll(values, HEAD_WIDTH // 2, 1)


def lane_mean(values):
    high = values.astype(BF16)
    low = (values - high.astype(F32)).astype(BF16)
    share = jnp.full((HEAD_WIDTH, HEAD_WIDTH), 1.0 / HEAD_WIDTH, BF16)
    return dot(high, share) + dot(low, share)


def head_norm(raw, h):
    values = raw[:, h * HEAD_WIDTH : (h + 1) * HEAD_WIDTH]
    scaling = lax.rsqrt(lane_mean(values * values) + EPSILON)
    return (values * scaling, scaling)


def rope_of(normed, cosine, sine):
    return (normed * cosine[...] + rolled(normed) * sine[...]).astype(BF16)


def blocks_of(length):
    for start in range(0, length, QUERY_BLOCK):
        first = max(0, start - LONGEST)
        yield slice(start, start + QUERY_BLOCK), slice(first, start + QUERY_BLOCK)


def together(values, rows):
    return values[:, rows].reshape(GROUP * QUERY_BLOCK, HEAD_WIDTH)


def weights_of(query, key, starts, rows, cols):
    size = cols.stop - cols.start
    scores = dot(query, key, 1, 1).reshape(GROUP, QUERY_BLOCK, size)
    shape = (QUERY_BLOCK, size)
    query_index = rows.start + lax.broadcasted_iota(jnp.int32, shape, 0)
    key_index = cols.start + lax.broadcasted_iota(jnp.int32, shape, 1)
    allowed = (key_index <= query_index) & (key_index >= starts[rows])
    scores = jnp.where(allowed[None], scores, MASKED)
    highest = jnp.max(scores, -1, keepdims=True)
    exponent = jnp.exp((scores - highest) * HEAD_WIDTH ** (-0.5))
    weights = exponent * (1.0 / jnp.sum(exponent, -1, keepdims=True))
    return weights.reshape(GROUP * QUERY_BLOCK, size)


def prepare_heads(raw, cosine, sine, gain_query, gain_key, q, k):
    for h in range(GROUP):
        q[h] = rope_of(head_norm(raw, h)[0] * gain_query[...], cosine, sine)
    k[...] = rope_of(head_norm(raw, GROUP)[0] * gain_key[...], cosine, sine)


def attend_forward(raw, cosine, sine, starts, gain_query, gain_key, out, q, k):
    prepare_heads(raw, cosine, sine, gain_query, gain_key, q, k)
    at = (GROUP + 1) * HEAD_WIDTH
    for rows, cols in blocks_of(raw.shape[0]):
        weights = weights_of(together(q, rows), k[cols], starts, rows, cols).astype(BF16)
        value = raw[cols, at : at + HEAD_WIDTH].astype(BF16)
        result = dot(weights, value).astype(BF16).reshape(GROUP, QUERY_BLOCK, HEAD_WIDTH)
        for h in range(GROUP):
            out[rows, h * HEAD_WIDTH : (h + 1) * HEAD_WIDTH] = result[h]


def attend_backward(
    raw,
    cosine,
    sine,
    starts,
    gain_query,
    gain_key,
    grad_hidden,
    normed,
    attended,
    packed,
    mlp_left,
    mlp_right,
    out,
    gains,
    weight_grads,
    output,
    q,
    k,
    v,
    dq,
    dk,
    dv,
    grad,
    total,
    normed_held,
    mlp_left_held,
    mlp_right_held,
    loads,
    *scratch
):
    factor = HEAD_WIDTH ** (-0.5)
    at = (GROUP + 1) * HEAD_WIDTH
    inputs = (GROUP + 2) * HEAD_WIDTH
    mlp = Reduce(mlp_left_held, mlp_right_held, mlp_right.shape[0] // 2, *scratch)
    length = raw.shape[0]
    here = pl.ds(pl.multiple_of(pl.program_id(0) * length, length), length)
    normed_load = pltpu.make_async_copy(normed.at[here], normed_held, loads.at[0])
    mlp_loads = [
        pltpu.make_async_copy(source, target, loads.at[i + 1])
        for i, (source, target) in enumerate(
            ((mlp_left, mlp_left_held), (mlp_right, mlp_right_held))
        )
    ]

    def mlp_load():
        greet(neighbours()[2:])
        for load in mlp_loads:
            load.start()

    def mlp_begin():
        for load in mlp_loads:
            load.wait()
        for c in range(FEW):
            mlp.produce(c, False)
            if c == 0:
                meet(3)
            mlp.begin(c)
        for c in range(FEW):
            mlp.produce(c, True)
            mlp.first(c)

    def mlp_second():
        for c in range(FEW):
            mlp.second(c)

    def mlp_end():
        def step(rows):
            output[rows] = mlp.take(rows)


        for c in range(FEW):
            mlp.arrive(c)
            tiles(c * mlp.rows, mlp.rows, step)
        for c in range(FEW):
            mlp.release(c)
        mlp.finish()

    def at_step(step, job):
        pl.when(pl.program_id(0) == step)(job)

    at_step(0, mlp_load)
    normed_load.start()
    prepare_heads(raw, cosine, sine, gain_query, gain_key, q, k)
    v[...] = raw[:, at : at + HEAD_WIDTH].astype(BF16)
    dk[...] = jnp.zeros_like(dk)
    dv[...] = jnp.zeros_like(dv)
    for h in range(GROUP):
        lanes = slice(inputs + h * HEAD_WIDTH, inputs + (h + 1) * HEAD_WIDTH)
        grad[h] = dot(grad_hidden[...], packed[:, lanes]).astype(BF16)
    at_step(0, mlp_begin)
    for n, (rows, cols) in enumerate(blocks_of(length)):
        query, block_grad = together(q, rows), together(grad, rows)
        weights = weights_of(query, k[cols], starts, rows, cols)
        grad_weights = dot(block_grad, v[cols], 1, 1)
        inner = jnp.sum(weights * grad_weights, -1, keepdims=True)
        grad_scores = (weights * (grad_weights - inner)).astype(BF16)
        dq[:, rows] = (dot(grad_scores, k[cols]) * factor).reshape(GROUP, QUERY_BLOCK, HEAD_WIDTH)
        dk[cols] += dot(grad_scores, query, 0, 0) * factor
        dv[cols] += dot(weights.astype(BF16), block_grad, 0, 0)
        if n == 0:
            at_step(1, mlp_second)
    gains[...] = jnp.zeros_like(gains)

    def undo(rot_grad, h, gain, row):
        normed_grad = rot_grad * cosine[...] - rolled(rot_grad) * sine[...]
        hat, inv = head_norm(raw, h)
        gains[0, row : row + 1] += jnp.sum(normed_grad * hat, 0, keepdims=True)
        lanes = slice(h * HEAD_WIDTH, (h + 1) * HEAD_WIDTH)
        scaled = normed_grad * gain[...]
        out[:, lanes] = (inv * (scaled - hat * lane_mean(scaled * hat))).astype(BF16)

    for h in range(GROUP):
        undo(dq[h], h, gain_query, 0)
    undo(dk[...], GROUP, gain_key, 1)
    out[:, at : at + HEAD_WIDTH] = dv[...].astype(BF16)

    @pl.when(pl.program_id(0) == 0)
    def _():
        total[...] = jnp.zeros_like(total)

    out_turned, attended_turned = out[...].T, attended[...].T
    normed_load.wait()
    for start in range(0, normed.shape[1], COLUMNS):
        cols = slice(start, start + COLUMNS)
        total[:inputs, cols] += dot(out_turned, normed_held[:, cols])
        total[inputs:, cols] += dot(attended_turned, grad_hidden[:, cols])

    @pl.when(pl.program_id(0) == pl.num_programs(0) - 1)
    def _():
        size = weight_grads.shape[2]
        for i in range(weight_grads.shape[0]):
            weight_grads[i] = total[:, i * size : (i + 1) * size].astype(BF16)

    at_step(1, mlp_end)


def once(spec):
    return pl.BlockSpec(spec.block_shape, spec.index_map, pipeline_mode=pl.Buffered(1))


def by_rows(rows, cols):
    return pl.BlockSpec((rows, cols), lambda i: (i, 0))


def whole(*shape):
    return pl.BlockSpec(shape, lambda i: (0,) * len(shape))


def call_blocks(
    kernel, steps, in_specs, out_shape, out_specs, scratch, flops, bytes_accessed, **remote_params
):
    return pl.pallas_call(
        kernel,
        out_shape=out_shape,
        grid=(steps,),
        in_specs=in_specs,
        out_specs=out_specs,
        scratch_shapes=scratch,
        name=kernel.__name__,
        cost_estimate=pl.CostEstimate(
            flops=flops, bytes_accessed=bytes_accessed, transcendentals=0
        ),
        compiler_params=pltpu.CompilerParams(
            dimension_semantics=("arbitrary",), vmem_limit_bytes=60 * MIB, **remote_params
        ),
    )


TOKEN_BLOCK = 512
HIDDEN_BLOCK = 256


def mlp_forward(normed, weights, active, gate_slope, up_slope):
    size = active.shape[1]
    for start in range(0, size, HIDDEN_BLOCK):
        cols = slice(start, start + HIDDEN_BLOCK)
        gate = dot(normed[...], weights[:, cols])
        up = dot(normed[...], weights[:, size + start : size + start + HIDDEN_BLOCK])
        sigmoid = jax.nn.sigmoid(gate)
        swish = gate * sigmoid
        active[:, cols] = (swish * up).astype(BF16)
        gate_slope[:, cols] = up * sigmoid * (1.0 + gate * (1.0 - sigmoid))
        up_slope[:, cols] = swish


def mlp_backward(cotangent, weights, gate_slope, up_slope, grads):
    size = gate_slope.shape[1]
    for start in range(0, size, HIDDEN_BLOCK):
        cols = slice(start, start + HIDDEN_BLOCK)
        grad = dot(cotangent[...], weights[:, cols])
        grads[:, cols] = (grad * gate_slope[:, cols]).astype(BF16)
        up_cols = slice(size + start, size + start + HIDDEN_BLOCK)
        grads[:, up_cols] = (grad * up_slope[:, cols]).astype(BF16)


def on_device(
    tokens,
    documents,
    cotangent,
    attn_gain,
    query_gain,
    key_norm_scale,
    query_weight,
    key_projection,
    value_projection,
    output_weight,
    mlp_gain,
    gate_weight,
    up_weight,
    down_weight,
):
    n_dp = lax.axis_size("dp")
    dp, mp = lax.axis_index("dp"), lax.axis_index("mp")
    y = dp % 2
    slabs = [[i + 2 * k for k in range(n_dp // 2)] for i in range(2)]
    rows, width = tokens.shape
    seq_length = documents.shape[1]
    seqs = 2 * documents.shape[0]
    share = rows // 4
    head = HEAD_WIDTH
    query_cols, key_cols, hidden_cols = (
        query_weight.shape[1] // 2,
        key_projection.shape[1] // 2,
        gate_weight.shape[1] // 2,
    )
    attn_cols = query_cols + 2 * key_cols

    def y_swap(values):
        return lax.ppermute(values, "dp", [(i, i ^ 1) for i in range(n_dp)])

    def mp_swap(values, bit):
        return lax.ppermute(values, "mp", [(i, i ^ bit) for i in range(4)])

    def in_order(where, mine, other, axis):
        return jnp.where(
            where == 0,
            jnp.concatenate([mine, other], axis),
            jnp.concatenate([other, mine], axis),
        )

    def half(values, which, axis):
        size = values.shape[axis] // 2
        return lax.dynamic_slice_in_dim(values, which * size, size, axis)

    def slab_gather(values):
        return lax.all_gather(values, "dp", axis=0, tiled=True, axis_index_groups=slabs)

    def slab_scatter(values):
        return lax.psum_scatter(
            values, "dp", scatter_dimension=0, tiled=True, axis_index_groups=slabs
        )

    n_gain, n_head = attn_gain.shape[0], query_gain.shape[0]

    def gain_rows(*parts):
        lead = parts[0].shape[:-1]
        pad = [(0, 0)] * len(lead)
        rows_of = jnp.concatenate(
            [
                jnp.pad(part, pad + [(0, -part.shape[-1] % 128)]).reshape(*lead, -1, 128)
                for part in parts
            ],
            -2,
        )
        return jnp.pad(rows_of, pad + [(0, 8 - rows_of.shape[-2]), (0, 0)])

    def gain_parts_of(rows_of):
        lead, parts, at = rows_of.shape[:-2], [], 0
        for size in (n_gain, n_gain, n_head, n_head):
            n = -(-size // 128)
            part = rows_of[..., at : at + n, :].reshape(*lead, n * 128)
            parts.append(part[..., :size])
            at += n
        return parts

    model_rows = query_weight.shape[0]
    pack_cols = attn_cols + query_cols
    pair_rows = 2 * rows
    n_slabs = n_dp // 2
    attn_full, gains, docs_other, normed_one, mlp_mine = call_leg(
        front,
        3,
        "front",
        [VM] * 9 + [ANY] * 3,
        (
            jax.ShapeDtypeStruct((width, pack_cols), BF16),
            jax.ShapeDtypeStruct((n_dp, 8, 128), F32),
            jax.ShapeDtypeStruct(documents.shape, jnp.int32),
            jax.ShapeDtypeStruct((pair_rows, width), BF16),
            jax.ShapeDtypeStruct((2 * model_rows, 2 * hidden_cols), BF16),
        ),
        (VM, VM, VM, ANY, VM),
        [
            pltpu.VMEM((model_rows, pack_cols), BF16),
            pltpu.VMEM((8, 128), F32),
            pltpu.VMEM((pair_rows, width), BF16),
            pltpu.VMEM((model_rows, 2 * hidden_cols), BF16),
            pltpu.VMEM((rows, width), BF16),
            pltpu.VMEM((rows, width), BF16),
            pltpu.VMEM(gate_weight.shape, F32),
            pltpu.VMEM(up_weight.shape, F32),
            pltpu.SemaphoreType.DMA((3,)),
            pltpu.SemaphoreType.DMA((8,)),
            pltpu.SemaphoreType.DMA((2, 4)),
            pltpu.SemaphoreType.DMA((n_dp,)),
            pltpu.SemaphoreType.DMA((n_dp,)),
            pltpu.SemaphoreType.DMA((n_slabs, 2)),
            pltpu.SemaphoreType.DMA((n_slabs, 2)),
        ]
        + Spread.scratch(),
        250 * MIB,
    )(
        query_weight,
        key_projection,
        value_projection,
        output_weight,
        attn_gain.reshape(1, -1),
        mlp_gain.reshape(1, -1),
        query_gain.reshape(1, -1),
        key_norm_scale.reshape(1, -1),
        documents,
        tokens,
        gate_weight,
        up_weight,
    )
    down_low = down_weight.astype(BF16)
    down_given, _ = lax.optimization_barrier((half(down_low, 1 - y, 0).T, docs_other))
    down_got = y_swap(down_given)

    cot_part = lax.dynamic_slice_in_dim(cotangent, mp * share, share, 0)
    cot_part, _ = lax.optimization_barrier((cot_part, docs_other))
    cot_part = y_swap(cot_part)
    gate_up_full = slab_gather(mlp_mine)
    gain_one, gain_two, gain_query, gain_key = (g.reshape(1, -1) for g in gain_parts_of(gains))
    docs = jnp.concatenate([documents, docs_other], 0)
    tokens_share = lax.dynamic_slice_in_dim(tokens, mp * share, share, 0)
    cot_share = lax.dynamic_slice_in_dim(cotangent, mp * share, share, 0)

    raw = dot(normed_one, attn_full[:, :attn_cols])
    starts = sum((docs < i).sum(1, keepdims=True) * (docs == i) for i in range(1, 4))
    positions = (jnp.arange(seq_length, dtype=jnp.int32)[None] - starts).reshape(pair_rows)
    cosine, sine = rope_tables(positions, head)
    starts = starts.reshape(pair_rows, 1).astype(jnp.int32)
    raw, sine, cot_part = lax.optimization_barrier((raw, sine, cot_part))
    cot_across = mp_swap(cot_part, 2)
    attention_args = (raw, cosine, sine, starts, gain_query, gain_key)
    attention_specs = [
        by_rows(seq_length, attn_cols),
        by_rows(seq_length, head),
        by_rows(seq_length, head),
        by_rows(seq_length, 1),
        whole(1, head),
        whole(1, head),
    ]
    pair_flops = pair_rows * seq_length * query_cols
    attended = call_blocks(
        attend_forward,
        seqs,
        attention_specs,
        jax.ShapeDtypeStruct((pair_rows, query_cols), BF16),
        by_rows(seq_length, query_cols),
        [pltpu.VMEM((GROUP, seq_length, head), BF16), pltpu.VMEM((seq_length, head), BF16)],
        2 * pair_flops,
        20 * MIB,
    )(*attention_args)
    attended, cot_across, down_got = lax.optimization_barrier((attended, cot_across, down_got))
    down_full = slab_gather(in_order(y, half(down_low, y, 0).T, down_got, 0))

    def grouped(cols):
        return (2, 2, 2, share, cols)

    half_width = width // 2
    leg_scratch = Reduce.scratch(share, width, half_width) + Gather.scratch(share, width)
    hidden, normed_two, cot_pair = call_leg(
        attention_leg,
        0,
        "attention_leg",
        [VM] * 4 + [ANY] * 3,
        (
            jax.ShapeDtypeStruct((share, width), F32),
            jax.ShapeDtypeStruct(grouped(width), BF16),
            jax.ShapeDtypeStruct((pair_rows, width), BF16),
        ),
        (VM, ANY, ANY),
        [
            pltpu.VMEM((rows + 2 * share, width), BF16),
            pltpu.SemaphoreType.DMA((3,)),
            pltpu.SemaphoreType.DMA((3,)),
            pltpu.SemaphoreType.DMA((2,)),
            pltpu.SemaphoreType.DMA((2,)),
        ]
        + leg_scratch,
        200 * MIB,
    )(
        attended.reshape(grouped(query_cols)),
        attn_full,
        tokens_share,
        gain_two,
        cotangent,
        cot_part,
        cot_across,
    )
    normed_two = normed_two.reshape(pair_rows, width)

    blocks = pair_rows // TOKEN_BLOCK
    hidden_block = by_rows(TOKEN_BLOCK, hidden_cols)
    hidden_shape = (pair_rows, hidden_cols)
    mlp_flops = 2 * pair_rows * width * hidden_cols
    active, gate_slope, up_slope = call_blocks(
        mlp_forward,
        blocks,
        [by_rows(TOKEN_BLOCK, width), whole(width, 2 * hidden_cols)],
        (
            jax.ShapeDtypeStruct(hidden_shape, BF16),
            jax.ShapeDtypeStruct(hidden_shape, F32),
            jax.ShapeDtypeStruct(hidden_shape, F32),
        ),
        (hidden_block,) * 3,
        [],
        2 * mlp_flops,
        30 * MIB,
    )(normed_two, gate_up_full)
    down_part = dot(cot_pair, active, 0, 0).astype(BF16)
    down_grad = slab_scatter(down_part)
    cot_late, _ = lax.optimization_barrier((cot_pair, down_part))
    grad_gate_up = call_blocks(
        mlp_backward,
        blocks,
        [by_rows(TOKEN_BLOCK, width), whole(width, hidden_cols), hidden_block, hidden_block],
        jax.ShapeDtypeStruct((pair_rows, 2 * hidden_cols), BF16),
        by_rows(TOKEN_BLOCK, 2 * hidden_cols),
        [],
        mlp_flops,
        30 * MIB,
    )(cot_late, down_full, gate_slope, up_slope)
    gate_up_part = dot(normed_two, grad_gate_up, 0, 0).astype(BF16)
    gate_up_grad = slab_scatter(gate_up_part)
    grad_gate_up, _, _ = lax.optimization_barrier((grad_gate_up, gate_up_part, down_part))
    grad_hidden, mlp_gain_part, grad_hidden_low = call_leg(
        hidden_leg,
        1,
        "hidden_leg",
        [ANY] * 2 + [VM] * 3,
        (
            jax.ShapeDtypeStruct((share, width), F32),
            jax.ShapeDtypeStruct((1, width), F32),
            jax.ShapeDtypeStruct(grouped(width), BF16),
        ),
        (VM, VM, ANY),
        [
            pltpu.VMEM(grouped(2 * hidden_cols), BF16),
            pltpu.VMEM((width, 2 * hidden_cols), BF16),
            pltpu.SemaphoreType.DMA((2, CHUNKS)),
            pltpu.SemaphoreType.DMA((width // COLUMNS,)),
        ]
        + leg_scratch,
        200 * MIB,
    )(
        grad_gate_up.reshape(grouped(2 * hidden_cols)),
        gate_up_full,
        hidden,
        cot_share,
        gain_two,
    )
    grad_hidden_low = grad_hidden_low.reshape(pair_rows, width)

    raw_grad, head_gain_parts, attn_grad, mlp_total = call_blocks(
        attend_backward,
        seqs,
        [once(spec) for spec in attention_specs]
        + [
            once(by_rows(seq_length, width)),
            ANY,
            once(by_rows(seq_length, query_cols)),
            once(whole(width, pack_cols)),
            ANY,
            ANY,
        ],
        (
            jax.ShapeDtypeStruct((pair_rows, attn_cols), BF16),
            jax.ShapeDtypeStruct((seqs, 8, head), F32),
            jax.ShapeDtypeStruct((n_dp, pack_cols, model_rows), BF16),
            jax.ShapeDtypeStruct((share, width), F32),
        ),
        (
            once(by_rows(seq_length, attn_cols)),
            pl.BlockSpec((1, 8, head), lambda i: (i, 0, 0)),
            once(whole(n_dp, pack_cols, model_rows)),
            once(whole(share, width)),
        ),
        [
            pltpu.VMEM((GROUP, seq_length, head), BF16),
            pltpu.VMEM((seq_length, head), BF16),
            pltpu.VMEM((seq_length, head), BF16),
            pltpu.VMEM((GROUP, seq_length, head), F32),
            pltpu.VMEM((seq_length, head), F32),
            pltpu.VMEM((seq_length, head), F32),
            pltpu.VMEM((GROUP, seq_length, head), BF16),
            pltpu.VMEM((pack_cols, width), F32),
            pltpu.VMEM((seq_length, width), BF16),
            pltpu.VMEM(grouped(hidden_cols), BF16),
            pltpu.VMEM((width, hidden_cols), BF16),
            pltpu.SemaphoreType.DMA((3,)),
        ]
        + Reduce.scratch(share, width, half_width, FEW),
        5 * pair_flops + 2 * pair_rows * width * (pack_cols + query_cols + hidden_cols),
        80 * MIB,
        collective_id=4,
        has_side_effects=True,
    )(
        *attention_args,
        grad_hidden_low,
        normed_one,
        attended,
        attn_full,
        active.reshape(grouped(hidden_cols)),
        down_full,
    )
    head_gain_parts = head_gain_parts.sum(0)
    attn_grad = attn_grad.reshape(n_dp * pack_cols, model_rows)
    attn_grad, raw_grad, gate_up_grad, down_grad = lax.optimization_barrier(
        (attn_grad, raw_grad, gate_up_grad, down_grad)
    )
    attn_parts = attn_grad.reshape(n_dp, pack_cols, model_rows)
    attn_grad = slab_scatter(attn_grad).reshape(2, pack_cols, model_rows)
    gain_parts = gain_rows(
        jnp.zeros((n_dp, n_gain), F32),
        mlp_gain_part.reshape(n_dp, n_gain),
        head_gain_parts[0].reshape(n_dp, n_head),
        head_gain_parts[1].reshape(n_dp, n_head),
    )

    low = 7 * width // 8
    input_grad, gain_sums, gate_up_other, down_other = call_leg(
        output_leg,
        2,
        "output_leg",
        [VM] * 7 + [ANY] * 2,
        (
            jax.ShapeDtypeStruct((share, width), F32),
            jax.ShapeDtypeStruct((8, 128), F32),
            jax.ShapeDtypeStruct((model_rows, 2 * hidden_cols), BF16),
            jax.ShapeDtypeStruct((model_rows, hidden_cols), BF16),
        ),
        (VM, VM, ANY, ANY),
        [
            pltpu.VMEM((n_dp, 8, 128), F32),
            pltpu.SemaphoreType.DMA((2,)),
            pltpu.SemaphoreType.DMA((2,)),
        ]
        + Reduce.scratch(share, width, low)
        + SumGains.scratch(n_dp, 4),
        200 * MIB,
    )(
        raw_grad.reshape(grouped(attn_cols)),
        attn_full,
        tokens_share,
        gain_one,
        gain_parts,
        attn_parts,
        grad_hidden,
        gate_up_grad,
        down_grad,
    )
    attn_given = lax.dynamic_index_in_dim(attn_grad, 1 - y, 0, False)
    attn_given, gate_up_other, down_other, mlp_total = lax.optimization_barrier(
        (attn_given, gate_up_other, down_other, mlp_total)
    )
    layer_output = (hidden + mlp_total).astype(BF16)

    def columns(own, other, start, axis=1):
        own = half(own, y, 0)[:, start : start + hidden_cols]
        other = other[:, start : start + hidden_cols]
        if axis == 0:
            own, other = own.T, other.T
        return in_order(y, own, other, axis).astype(F32)

    gate_grad = columns(gate_up_grad, gate_up_other, 0)
    up_grad = columns(gate_up_grad, gate_up_other, hidden_cols)
    down_grad = columns(down_grad, down_other, 0, 0)

    attn_other = y_swap(attn_given)
    attn_own = lax.dynamic_index_in_dim(attn_grad, y, 0, False)

    query_grad, key_grad, value_grad, output_grad = pl.pallas_call(
        finish_attention,
        out_shape=tuple(
            jax.ShapeDtypeStruct(w.shape, F32)
            for w in (query_weight, key_projection, value_projection, output_weight)
        ),
        in_specs=[VM] * 2,
        out_specs=(VM,) * 4,
        name="finish_attention",
        cost_estimate=pl.CostEstimate(flops=0, bytes_accessed=4 * MIB, transcendentals=0),
        compiler_params=pltpu.CompilerParams(vmem_limit_bytes=32 * MIB),
    )(attn_own, attn_other)
    attn_gain_grad, mlp_gain_grad, query_gain_grad, key_gain_grad = gain_parts_of(gain_sums)
    return (
        layer_output,
        input_grad,
        attn_gain_grad,
        query_gain_grad,
        key_gain_grad,
        query_grad,
        key_grad,
        value_grad,
        output_grad,
        mlp_gain_grad,
        gate_grad,
        up_grad,
        down_grad,
    )


def solution(mesh):
    in_specs = (
        P("dp", None),
        P("dp", None),
        P("dp", None),
        P("dp"),
        P("dp"),
        P("dp"),
        P("dp", "mp"),
        P("dp", "mp"),
        P("dp", "mp"),
        P("mp", "dp"),
        P("dp"),
        P("dp", "mp"),
        P("dp", "mp"),
        P("mp", "dp"),
    )
    out_specs = (
        P(("dp", "mp"), None),
        P(("dp", "mp"), None),
        P("dp"),
        P("dp"),
        P("dp"),
        P("dp", "mp"),
        P("dp", "mp"),
        P("dp", "mp"),
        P("mp", "dp"),
        P("dp"),
        P("dp", "mp"),
        P("dp", "mp"),
        P("mp", "dp"),
    )
    return jax.shard_map(
        on_device, mesh=mesh, in_specs=in_specs, out_specs=out_specs, check_vma=False
    )
```

```python
import functools

import jax
import jax.numpy as jnp
from jax import lax
from jax.experimental import pallas as pl
from jax.experimental.pallas import tpu as pltpu
from jax.sharding import PartitionSpec as P

QUERY_HEADS = 16
KEY_VALUE_HEADS = 8
HEAD_WIDTH = 128
GROUP = QUERY_HEADS // KEY_VALUE_HEADS

EPSILON = 1e-06
MASKED = -1e30
MESH = pl.DeviceIdType.MESH
F32 = jnp.float32
BF16 = jnp.bfloat16
MIB = 2**20


def rope_tables(positions, head_size):
    middle = head_size // 2
    frequency = jnp.power(1000000.0, -2.0 * jnp.arange(middle, dtype=F32) / head_size)
    angles = positions.astype(F32)[:, None] * frequency[None, :]
    cosine_table = jnp.cos(angles)
    sine_table = jnp.sin(angles)
    return (
        jnp.concatenate([cosine_table, cosine_table], -1),
        jnp.concatenate([-sine_table, sine_table], -1),
    )


def norm_parts(values):
    scaling = lax.rsqrt(jnp.mean(values * values, -1, keepdims=True) + EPSILON)
    return (values * scaling, scaling)


def norm_back(grad_normed, normed_hat, scaling, gains):
    scaled = grad_normed * gains
    return scaling * (scaled - normed_hat * jnp.mean(scaled * normed_hat, -1, keepdims=True))


def dot(left, right, left_dim=1, right_dim=0):
    return lax.dot_general(
        left, right, (((left_dim,), (right_dim,)), ((), ())), preferred_element_type=F32
    )


CHUNKS = 4
FEW = 2
TILE = 32
COLUMNS = 512


def neighbours():
    dp, mp = lax.axis_index("dp"), lax.axis_index("mp")
    x, c = mp // 2, mp % 2
    return (
        x,
        c,
        (dp, x * 2 + 1 - c),
        (dp, (1 - x) * 2 + c),
        (dp + 1 - 2 * (dp % 2), mp),
    )


def greet(peers):
    barrier = pltpu.get_barrier_semaphore()
    for peer in peers:
        pl.semaphore_signal(barrier, inc=1, device_id=peer, device_id_type=MESH)


def meet(count):
    pl.semaphore_wait(pltpu.get_barrier_semaphore(), count)


def remote(src, dst, send, recv, peer):
    return pltpu.make_async_remote_copy(
        src_ref=src, dst_ref=dst, send_sem=send, recv_sem=recv, device_id=peer, device_id_type=MESH
    )


def tiles(start, rows, step):
    def body(i, carry):
        step(pl.ds(pl.multiple_of(start + i * TILE, TILE), TILE))
        return carry

    lax.fori_loop(0, rows // TILE, body, 0)


class Reduce:
    STAGES = 5

    def __init__(self, left, right, low, part, mine, got, gx, gy, fx, fy, send, recv, load=None):
        self.left, self.right, self.low, self.load = left, right, low, load
        self.refs = (part, mine, got, gx, gy, fx, fy, send, recv)
        self.chunks = send.shape[1]
        self.rows = mine.shape[2] // self.chunks
        self.width = mine.shape[3]

    @staticmethod
    def scratch(rows, width, low, chunks=CHUNKS):
        high = width - low
        return [
            pltpu.VMEM((2, 2, rows, width), BF16),
            pltpu.VMEM((2, 2, rows, width), BF16),
            pltpu.VMEM((2, 2, rows, width), BF16),
            pltpu.VMEM((2, rows, low), BF16),
            pltpu.VMEM((2, rows, high), BF16),
            pltpu.VMEM((rows, high), BF16),
            pltpu.VMEM((rows, low), BF16),
            pltpu.SemaphoreType.DMA((Reduce.STAGES, chunks)),
            pltpu.SemaphoreType.DMA((Reduce.STAGES, chunks)),
        ]

    def lanes(self):
        return pl.ds(0, self.low), pl.ds(self.low, self.width - self.low)

    def load_left(self, k, own):
        source, _, sems, _ = self.load
        core = neighbours()[1]
        at = (slice(None), slice(None), core if own else 1 - core, pl.ds(k * self.rows, self.rows))
        return pltpu.make_async_copy(source.at[at], self.left.at[at], sems.at[int(own), k])

    def load_right(self, j):
        _, source, _, sems = self.load
        at = pl.ds(pl.multiple_of(j * COLUMNS, COLUMNS), COLUMNS)
        return pltpu.make_async_copy(source.at[at], self.right.at[at], sems.at[j])

    def start_loads(self):
        self.load_left(0, False).start()
        for j in range(self.width // COLUMNS):
            self.load_right(j).start()
        self.load_left(0, True).start()
        for k in range(1, self.chunks):
            for own in (False, True):
                self.load_left(k, own).start()

    def copy(self, k, i):
        part, mine, got, gx, gy, fx, fy, send, recv = self.refs
        x, _, core_peer, x_peer, y_peer = neighbours()
        rows = pl.ds(k * self.rows, self.rows)
        low, high = self.lanes()
        s = [send.at[j, k] for j in range(self.STAGES)]
        r = [recv.at[j, k] for j in range(self.STAGES)]
        all_copies = (
            lambda: remote(part.at[:, :, rows], got.at[:, :, rows], s[0], r[0], core_peer),
            lambda: remote(mine.at[:, 1 - x, rows, low], gx.at[:, rows], s[1], r[1], x_peer),
            lambda: remote(mine.at[1, :, rows, high], gy.at[:, rows], s[2], r[2], y_peer),
            lambda: remote(mine.at[1, x, rows, low], fy.at[rows], s[3], r[3], y_peer),
            lambda: remote(mine.at[0, 1 - x, rows, high], fx.at[rows], s[4], r[4], x_peer),
        )
        return all_copies[i]()

    def produce(self, k, own):
        target = self.refs[1] if own else self.refs[0]
        core = neighbours()[1]
        core = core if own else 1 - core
        rows = pl.ds(k * self.rows, self.rows)
        depth = self.left.shape[4]
        if self.load is not None:
            self.load_left(k, own).wait()

        def tile(j, carry):
            if self.load is not None and k == 0 and not own:
                self.load_right(j).wait()
            cols = pl.ds(pl.multiple_of(j * COLUMNS, COLUMNS), COLUMNS)
            left = self.left[:, :, core, rows, :].reshape(4 * self.rows, depth)
            product = dot(left, self.right[cols, :], 1, 1).astype(BF16)
            target[:, :, rows, cols] = product.reshape(2, 2, self.rows, COLUMNS)
            return carry

        lax.fori_loop(0, self.width // COLUMNS, tile, 0)

    def begin(self, k):
        self.copy(k, 0).start()

    def release(self, k):
        self.copy(k, 0).wait_send()

    def first(self, k):
        mine, got = self.refs[1:3]
        self.copy(k, 0).wait_recv()

        def add(i, carry):
            def step(rows):
                at = (i // 2, i % 2, rows)
                mine[at] = mine[at] + got[at]

            tiles(k * self.rows, self.rows, step)
            return carry

        lax.fori_loop(0, 4, add, 0)
        self.copy(k, 1).start()
        self.copy(k, 2).start()

    def second(self, k):
        mine, _, gx, gy = self.refs[1:5]
        x = neighbours()[0]
        low, high = self.lanes()
        self.copy(k, 1).wait_recv()

        def step_low(rows):
            for i in range(2):
                at = (i, x, rows, low)
                mine[at] = mine[at] + gx[i, rows]

        tiles(k * self.rows, self.rows, step_low)
        self.copy(k, 3).start()
        self.copy(k, 2).wait_recv()

        def step_high(rows):
            for i in range(2):
                at = (0, i, rows, high)
                mine[at] = mine[at] + gy[i, rows]

        tiles(k * self.rows, self.rows, step_high)
        self.copy(k, 4).start()

    def arrive(self, k):
        self.copy(k, 3).wait_recv()
        self.copy(k, 4).wait_recv()

    def take(self, rows):
        mine, fx, fy = self.refs[1], *self.refs[5:7]
        x = neighbours()[0]
        low, high = self.lanes()
        return jnp.concatenate(
            [
                mine[0, x, rows, low].astype(F32) + fy[rows].astype(F32),
                mine[0, x, rows, high].astype(F32) + fx[rows].astype(F32),
            ],
            -1,
        )

    def finish(self):
        for k in range(self.chunks):
            for i in range(1, 5):
                self.copy(k, i).wait_send()


class Gather:
    STAGES = 9

    def __init__(self, mine, full, local, send, recv):
        self.refs = (mine, full, local, send, recv)
        self.rows = mine.shape[0] // CHUNKS
        self.half = mine.shape[1] // 2

    @staticmethod
    def scratch(rows, width):
        return [
            pltpu.VMEM((rows, width), BF16),
            pltpu.SemaphoreType.DMA((CHUNKS,)),
            pltpu.SemaphoreType.DMA((Gather.STAGES, CHUNKS)),
            pltpu.SemaphoreType.DMA((Gather.STAGES, CHUNKS)),
        ]

    def copy(self, k, i):
        mine, full, local, send, recv = self.refs
        x, c, core_peer, x_peer, y_peer = neighbours()
        rows = pl.ds(k * self.rows, self.rows)
        low, high = pl.ds(0, self.half), pl.ds(self.half, self.half)
        s = [send.at[j, k] for j in range(self.STAGES)]
        r = [recv.at[j, k] for j in range(self.STAGES)]

        def pass_on(j, at, peer):
            return lambda: remote(full.at[at], full.at[at], s[j], r[j], peer)

        all_copies = (
            lambda: pltpu.make_async_copy(mine.at[rows], full.at[0, x, c, rows], local.at[k]),
            lambda: remote(mine.at[rows, low], full.at[1, x, c, rows, low], s[0], r[0], y_peer),
            lambda: remote(mine.at[rows, high], full.at[0, x, c, rows, high], s[1], r[1], x_peer),
            lambda: remote(mine.at[rows], full.at[0, x, c, rows], s[2], r[2], core_peer),
            pass_on(3, (slice(None), x, c, rows, low), x_peer),
            lambda: remote(
                full.at[0, :, c, rows, high], full.at[1, :, c, rows, high], s[4], r[4], y_peer
            ),
            pass_on(5, (1, x, c, rows, low), core_peer),
            pass_on(6, (0, 1 - x, c, rows, high), core_peer),
            pass_on(7, (slice(None), 1 - x, c, rows, low), core_peer),
            pass_on(8, (1, slice(None), c, rows, high), core_peer),
        )
        return all_copies[i]()

    def begin(self, k):
        for i in (1, 2, 0, 3):
            self.copy(k, i).start()

    def second(self, k):
        self.copy(k, 0).wait()
        self.copy(k, 1).wait_recv()
        self.copy(k, 4).start()
        self.copy(k, 2).wait_recv()
        for i in (5, 6, 7):
            self.copy(k, i).start()

    def third(self, k):
        for i in (4, 5):
            self.copy(k, i).wait_recv()
            self.copy(k, i + 4).start()

    def finish(self):
        for k in range(CHUNKS):
            for i in (3, 6, 7, 8, 9):
                self.copy(k, i).wait_recv()
            for i in range(1, 10):
                self.copy(k, i).wait_send()


N_REDUCE = len(Reduce.scratch(32, 256, 128))


def nothing():
    pass


def leg(left, right, low, full, step, scratch, at_start=nothing, at_middle=nothing, load=None):
    reduce = Reduce(left, right, low, *scratch[:N_REDUCE], load=load)
    if load is not None:
        reduce.start_loads()
    gather = Gather(scratch[N_REDUCE], full, *scratch[N_REDUCE + 1 :])
    mine = scratch[N_REDUCE]
    greet(neighbours()[2:])
    for k in range(CHUNKS):
        reduce.produce(k, False)
        if k == 0:
            meet(3)
        reduce.begin(k)
        reduce.produce(k, True)
        reduce.first(k)
    at_start()
    for k in range(CHUNKS):
        reduce.second(k)
    at_middle()

    def step_at(rows):
        mine[rows] = step(rows, reduce.take(rows)).astype(BF16)

    for k in range(CHUNKS):
        reduce.arrive(k)
        tiles(k * reduce.rows, reduce.rows, step_at)
        gather.begin(k)
    for k in range(CHUNKS):
        gather.second(k)
    for k in range(CHUNKS):
        gather.third(k)
    gather.finish()
    for k in range(CHUNKS):
        reduce.release(k)
    reduce.finish()


def attention_leg(
    left,
    packed,
    tokens,
    gain,
    cotangent,
    cot_part,
    cot_across,
    hidden,
    normed,
    cot_pair,
    cot_buffer,
    cot_in,
    cot_out,
    cot_send,
    cot_recv,
    *scratch
):
    def step(rows, total):
        h = tokens[rows].astype(F32) + total
        hidden[rows] = h
        return norm_parts(h)[0] * gain[...]

    x, core, core_peer = neighbours()[:3]
    own, share = cotangent.shape[0], cot_part.shape[0]

    def place(at_x, at_core):
        start = own + (at_x * 2 + at_core) * share
        return pl.ds(pl.multiple_of(start, share), share)

    sources = (cotangent, cot_part, cot_across)
    starts = (0, own, own + share)
    places = (pl.ds(0, own), place(x, core), place(1 - x, core))
    loads, stores, sends = [], [], []
    for i in range(3):
        held = cot_buffer.at[pl.ds(starts[i], sources[i].shape[0])]
        loads.append(pltpu.make_async_copy(sources[i], held, cot_in.at[i]))
        stores.append(pltpu.make_async_copy(held, cot_pair.at[places[i]], cot_out.at[i]))
        if i > 0:
            to = cot_pair.at[places[i]]
            sends.append(remote(sources[i], to, cot_send.at[i - 1], cot_recv.at[i - 1], core_peer))

    def at_start():
        for copy in loads + sends:
            copy.start()

    def at_middle():
        for load, store in zip(loads, stores):
            load.wait()
            store.start()

    depth = left.shape[4]
    right = packed.at[:, pl.ds(packed.shape[1] - depth, depth)]
    leg(left, right, right.shape[0] // 2, normed, step, scratch, at_start, at_middle)
    for copy in stores + sends:
        copy.wait()


def hidden_leg(
    left,
    right,
    hidden,
    cotangent,
    gain,
    grad_hidden,
    gain_grad,
    full,
    left_held,
    right_held,
    left_sems,
    right_sems,
    *scratch
):
    def step(rows, grad):
        hat, inv = norm_parts(hidden[rows])
        gain_grad[...] += jnp.sum(grad * hat, 0, keepdims=True)
        grad = cotangent[rows].astype(F32) + norm_back(grad, hat, inv, gain[...])
        grad_hidden[rows] = grad
        return grad

    gain_grad[...] = jnp.zeros_like(gain_grad)
    load = (left, right, left_sems, right_sems)
    leg(left_held, right_held, right.shape[0] // 2, full, step, scratch, load=load)


class SumGains:
    def __init__(self, parts, total, got, mid, others, send, recv, send_mp, recv_mp):
        self.refs = (parts, total, got, mid, others, send, recv, send_mp, recv_mp)
        self.n_dp, self.n_mp = parts.shape[0], others.shape[0] + 1

    @staticmethod
    def scratch(n_dp, n_mp):
        return [
            pltpu.VMEM((n_dp, 8, 128), F32),
            pltpu.VMEM((8, 128), F32),
            pltpu.VMEM((n_mp - 1, 8, 128), F32),
            pltpu.SemaphoreType.DMA((n_dp,)),
            pltpu.SemaphoreType.DMA((n_dp,)),
            pltpu.SemaphoreType.DMA((n_mp,)),
            pltpu.SemaphoreType.DMA((n_mp,)),
        ]

    def across(self, j):
        return (lax.rem(lax.axis_index("dp") + j, self.n_dp), lax.axis_index("mp"))

    def along(self, j):
        return (lax.axis_index("dp"), lax.rem(lax.axis_index("mp") + j, self.n_mp))

    def greet(self):
        barrier = pltpu.get_barrier_semaphore()

        def one(j, carry):
            pl.semaphore_signal(barrier, inc=1, device_id=self.across(j), device_id_type=MESH)
            return carry

        lax.fori_loop(1, self.n_dp, one, 0)
        greet([self.along(j) for j in range(1, self.n_mp)])

    def first(self, j):
        parts, _, got, _, _, send, recv = self.refs[:7]
        to = self.across(j)
        return remote(parts.at[to[0]], got.at[j], send.at[j], recv.at[j], to)

    def second(self, j):
        mid, others = self.refs[3:5]
        send, recv = self.refs[7:]
        return remote(mid, others.at[j - 1], send.at[j], recv.at[j], self.along(j))

    def begin(self):
        def start(j, carry):
            self.first(j).start()
            return carry

        lax.fori_loop(1, self.n_dp, start, 0)

    def pass_on(self):
        parts, _, got, mid = self.refs[:4]
        mid[...] = parts[lax.axis_index("dp")]

        def add(j, carry):
            self.first(j).wait()
            mid[...] += got[j]
            return carry

        lax.fori_loop(1, self.n_dp, add, 0)
        for j in range(1, self.n_mp):
            self.second(j).start()

    def finish(self):
        _, total, _, mid, others = self.refs[:5]
        result = mid[...]
        for j in range(1, self.n_mp):
            self.second(j).wait()
            result += others[j - 1]
        total[...] = result


def output_leg(
    left,
    packed,
    tokens,
    gain,
    gain_parts,
    weight_grads,
    grad_hidden,
    gate_up_grad,
    down_grad,
    input_grad,
    gain_total,
    gate_up_other,
    down_other,
    slots,
    swap_send,
    swap_recv,
    *scratch
):
    low = scratch[3].shape[2]
    depth = left.shape[4]
    right = packed.at[:, pl.ds(0, depth)]
    reduce = Reduce(left, right, low, *scratch[:N_REDUCE])
    sums = SumGains(slots, gain_total, *scratch[N_REDUCE:])
    y, y_peer = lax.axis_index("dp") % 2, neighbours()[4]
    half = gate_up_other.shape[0]
    theirs = pl.ds(pl.multiple_of((1 - y) * half, half), half)
    swaps = [
        remote(gate_up_grad.at[theirs], gate_up_other, swap_send.at[0], swap_recv.at[0], y_peer),
        remote(down_grad.at[theirs], down_other, swap_send.at[1], swap_recv.at[1], y_peer),
    ]

    def step(rows):
        grad = reduce.take(rows)
        hat, inv = norm_parts(tokens[rows].astype(F32))
        input_grad[rows] = grad_hidden[rows] + norm_back(grad, hat, inv, gain[...])

    sums.greet()
    slots[...] = gain_parts[...]
    meet(sums.n_dp + sums.n_mp - 2)
    swaps[0].start()
    for k in range(reduce.chunks):
        reduce.produce(k, False)
        reduce.begin(k)
        reduce.produce(k, True)
        reduce.first(k)
    swaps[1].start()
    owned = weight_grads.shape[2]
    diagonal = lax.broadcasted_iota(jnp.int32, (owned, owned), 0) == lax.broadcasted_iota(
        jnp.int32, (owned, owned), 1
    )
    for i in range(sums.n_dp):
        product = dot(right[i * owned : (i + 1) * owned, :], weight_grads[i, :depth, :])
        sums_of = jnp.sum(jnp.where(diagonal, product, 0.0), 0, keepdims=True)
        sums_of = sums_of / gain[:, i * owned : (i + 1) * owned]
        for j, size in gain_rows_of(owned):
            slots[i, j : j + 1, :size] = sums_of[:, j * 128 : j * 128 + size]
    sums.begin()
    for k in range(reduce.chunks):
        reduce.second(k)
    sums.pass_on()
    for k in range(reduce.chunks):
        reduce.arrive(k)
        tiles(k * reduce.rows, reduce.rows, step)
    sums.finish()
    for k in range(reduce.chunks):
        reduce.release(k)
    for copy in swaps:
        copy.wait()
    reduce.finish()


ANY = pl.BlockSpec(memory_space=pl.ANY)
VM = pl.BlockSpec(memory_space=pltpu.VMEM)


def call_leg(kernel, ident, name, in_specs, out_shape, out_specs, scratch, bytes_moved):
    return pl.pallas_call(
        kernel,
        out_shape=out_shape,
        in_specs=in_specs,
        out_specs=out_specs,
        scratch_shapes=scratch,
        name=name,
        cost_estimate=pl.CostEstimate(flops=0, bytes_accessed=bytes_moved, transcendentals=0),
        compiler_params=pltpu.CompilerParams(
            collective_id=ident, has_side_effects=True, vmem_limit_bytes=60 * MIB
        ),
    )


class Spread:
    STAGES = 4

    def __init__(self, mine, other, send, recv):
        self.refs = (mine, other, send, recv)
        self.rows = mine.shape[0] // 4 // FEW

    @staticmethod
    def scratch():
        return [
            pltpu.SemaphoreType.DMA((Spread.STAGES, FEW)),
            pltpu.SemaphoreType.DMA((Spread.STAGES, FEW)),
        ]

    def copy(self, k, i):
        mine, other, send, recv = self.refs
        x, c, core_peer, x_peer, y_peer = neighbours()

        def rows(at_x):
            start = (at_x * 2 + c) * (mine.shape[0] // 4) + k * self.rows
            return pl.ds(pl.multiple_of(start, self.rows), self.rows)

        at = rows(1 - x) if i == 3 else rows(x)
        peer = (y_peer, x_peer, core_peer, core_peer)[i]
        source = mine if i == 0 else other
        return remote(source.at[at], other.at[at], send.at[i, k], recv.at[i, k], peer)

    def pass_on(self, k):
        self.copy(k, 0).wait_recv()
        self.copy(k, 1).start()
        self.copy(k, 2).start()

    def pass_last(self, k):
        self.copy(k, 1).wait_recv()
        self.copy(k, 3).start()

    def finish(self):
        for k in range(FEW):
            for i in range(4):
                self.copy(k, i).wait_send()


def front(
    q,
    k,
    v,
    o,
    attn_gain,
    mlp_gain,
    query_gain,
    key_gain,
    docs,
    tokens,
    gate,
    up,
    full,
    gains,
    docs_other,
    normed_out,
    gate_up_mine,
    stage,
    gain,
    normed,
    gate_up_stage,
    tokens_mine,
    tokens_other,
    gate_in,
    up_in,
    local,
    stores,
    swap,
    gain_send,
    gain_recv,
    ring_send,
    ring_recv,
    *scratch
):
    dp, mp = lax.axis_index("dp"), lax.axis_index("mp")
    _, _, core_peer, x_peer, y_peer = neighbours()
    n_dp = gains.shape[0]
    n_slabs = n_dp // 2
    y, z = dp % 2, dp // 2
    rows = q.shape[0]
    spread = Spread(tokens, tokens_other, *scratch)

    def peer(j):
        return (lax.rem(dp + j, n_dp), mp)

    def greet_one(j, carry):
        barrier = pltpu.get_barrier_semaphore()
        pl.semaphore_signal(barrier, inc=1, device_id=peer(j), device_id_type=MESH)
        return carry

    lax.fori_loop(1, n_dp, greet_one, 0)
    greet([core_peer, x_peer])
    loads = [
        pltpu.make_async_copy(source, target, local.at[i])
        for i, (source, target) in enumerate(
            ((tokens, tokens_mine), (gate, gate_in), (up, up_in))
        )
    ]
    for load in loads:
        load.start()
    widths = [w.shape[1] // 2 for w in (q, k, v)]
    first = sum(widths)

    def fill(target, row, which):
        at = 0
        for w, size in zip((q, k, v), widths):
            cols = pl.ds(pl.multiple_of(which * size, 128), size)
            target[pl.ds(row, rows), at : at + size] = w[:, cols].astype(BF16)
            at += size
        size = o.shape[0] // 2
        part = o[pl.ds(pl.multiple_of(which * size, 128), size), :].astype(BF16)
        target[pl.ds(row, rows), first : first + size] = part.T

    def block(slab, pair):
        return pl.ds(pl.multiple_of((slab * 2 + pair) * rows, rows), rows)

    swapped = remote(stage, full.at[block(z, y)], swap.at[0, 0], swap.at[1, 0], y_peer)
    docs_swapped = remote(docs, docs_other, swap.at[0, 1], swap.at[1, 1], y_peer)
    mine = pl.ds(pl.multiple_of(y * rows, rows), rows)
    gate_up_swapped = remote(
        gate_up_stage, gate_up_mine.at[mine], swap.at[0, 2], swap.at[1, 2], y_peer
    )

    def ring(step, i):
        slab = lax.rem(z - step + n_slabs, n_slabs)
        at = full.at[block(slab, y if i == 0 else 1 - y)]
        to = (lax.rem(dp + 2, n_dp), mp)
        return remote(at, at, ring_send.at[step, i], ring_recv.at[step, i], to)

    def ring_next(step, i):
        slab = lax.rem(z - step - 1 + 2 * n_slabs, n_slabs)
        at = full.at[block(slab, y if i == 0 else 1 - y)]
        to = (lax.rem(dp + 2, n_dp), mp)
        came = remote(at, at, ring_send.at[step, i], ring_recv.at[step, i], to)
        came.wait_recv()
        if isinstance(step, int) and step + 1 >= n_slabs - 1:
            return
        ring(step + 1, i).start()

    def gain_to(j):
        return remote(gain, gains.at[dp], gain_send.at[j], gain_recv.at[j], peer(j))

    def share(j, carry):
        gain_to(j).start()
        return carry

    def settle(j, carry):
        gain_to(j).wait()
        return carry

    def fill_mlp(gate_up_to, row, which):
        size = gate.shape[1] // 2
        cols = pl.ds(pl.multiple_of(which * size, 128), size)
        gate_up_to[pl.ds(row, rows), :size] = gate_in[:, cols].astype(BF16)
        gate_up_to[pl.ds(row, rows), size:] = up_in[:, cols].astype(BF16)

    fill(stage, 0, 1 - y)
    row = 0
    for values in (attn_gain, mlp_gain, query_gain, key_gain):
        for j, size in gain_rows_of(values.shape[1]):
            part = values[:, j * 128 : j * 128 + size]
            gain[row : row + 1, :size] = part.astype(BF16).astype(F32)
            row += 1
    meet(n_dp - 1 + 2)
    swapped.start()
    fill(full, block(z, y).start, y)
    ring(0, 0).start()
    docs_swapped.start()
    lax.fori_loop(1, n_dp, share, 0)
    for c in range(FEW):
        spread.copy(c, 0).start()
    gains[dp] = gain[...]
    for load in loads[1:]:
        load.wait()
    fill_mlp(gate_up_stage, 0, 1 - y)
    gate_up_swapped.start()
    swapped.wait_recv()
    ring(0, 1).start()
    lax.fori_loop(1, n_dp, settle, 0)
    owned = gain_rows_of(full.shape[0] // n_dp)
    gain_row = jnp.concatenate(
        [gains[i, j : j + 1, :size] for i in range(n_dp) for j, size in owned], -1
    )

    def norm(source, base, start, count):
        def step(at):
            hat = norm_parts(source[at].astype(F32))[0]
            to = pl.ds(pl.multiple_of(base + at.start, TILE), TILE)
            normed[to] = (hat * gain_row).astype(BF16)

        tiles(start, count, step)

    total = tokens.shape[0]
    quarter = total // 4

    def store(i):
        at = pl.ds(i * quarter, quarter)
        return pltpu.make_async_copy(normed.at[at], normed_out.at[at], stores.at[i])

    def norm_mine(i):
        norm(tokens_mine, 0, i * quarter, quarter)
        store(i).start()

    def norm_other():
        for c in range(FEW):
            for i in (2, 3):
                spread.copy(c, i).wait_recv()
        for i in range(4):
            norm(tokens_other, total, i * quarter, quarter)
            store(4 + i).start()

    loads[0].wait()
    early = [functools.partial(fill_mlp, gate_up_mine, mine.start, y)]
    early += [functools.partial(norm_mine, i) for i in range(4)]
    late = [functools.partial(spread.pass_on, c) for c in range(FEW)]
    late += [functools.partial(spread.pass_last, c) for c in range(FEW)]

    def run(jobs):
        for job in jobs:
            job()

    if n_slabs == 4:
        ring_next(0, 0)
        run(early[:3])
        ring_next(0, 1)
        run(early[3:])
        spread.pass_on(0)
        ring_next(1, 0)
        spread.pass_on(1)
        spread.pass_last(0)
        ring_next(1, 1)
        spread.pass_last(1)
        norm_other()
        ring_next(2, 0)
        ring_next(2, 1)
    else:
        run(early)
        run(late)

        def turn(step, carry):
            for i in range(2):
                ring_next(step, i)
            return carry

        lax.fori_loop(0, n_slabs - 2, turn, 0)
        for i in range(2):
            ring_next(n_slabs - 2, i)
        norm_other()
    spread.finish()
    for i in range(8):
        store(i).wait()
    docs_swapped.wait()
    swapped.wait_send()
    gate_up_swapped.wait()

    def sent(step, carry):
        for i in range(2):
            ring(step, i).wait_send()
        return carry

    lax.fori_loop(0, n_slabs - 1, sent, 0)


def gain_rows_of(size):
    return [(j, min(128, size - j * 128)) for j in range(-(-size // 128))]


def finish_attention(own, other, q, k, v, o):
    y = lax.axis_index("dp") % 2

    def place(source, which):
        at = 0
        for w in (q, k, v):
            size = w.shape[1] // 2
            cols = pl.ds(pl.multiple_of(which * size, 128), size)
            w[:, cols] = source[at : at + size, :].T.astype(F32)
            at += size
        size = o.shape[0] // 2
        rows = pl.ds(pl.multiple_of(which * size, size), size)
        o[rows, :] = source[at : at + size, :].astype(F32)

    place(own, y)
    place(other, 1 - y)


QUERY_BLOCK = 256
LONGEST = 512


def rolled(values):
    return pltpu.roll(values, HEAD_WIDTH // 2, 1)


def lane_mean(values):
    high = values.astype(BF16)
    low = (values - high.astype(F32)).astype(BF16)
    share = jnp.full((HEAD_WIDTH, HEAD_WIDTH), 1.0 / HEAD_WIDTH, BF16)
    return dot(high, share) + dot(low, share)


def head_norm(raw, h):
    values = raw[:, h * HEAD_WIDTH : (h + 1) * HEAD_WIDTH]
    scaling = lax.rsqrt(lane_mean(values * values) + EPSILON)
    return (values * scaling, scaling)


def rope_of(normed, cosine, sine):
    return (normed * cosine[...] + rolled(normed) * sine[...]).astype(BF16)


def blocks_of(length):
    for start in range(0, length, QUERY_BLOCK):
        first = max(0, start - LONGEST)
        yield slice(start, start + QUERY_BLOCK), slice(first, start + QUERY_BLOCK)


def together(values, rows):
    return values[:, rows].reshape(GROUP * QUERY_BLOCK, HEAD_WIDTH)


def weights_of(query, key, starts, rows, cols):
    size = cols.stop - cols.start
    scores = dot(query, key, 1, 1).reshape(GROUP, QUERY_BLOCK, size)
    shape = (QUERY_BLOCK, size)
    query_index = rows.start + lax.broadcasted_iota(jnp.int32, shape, 0)
    key_index = cols.start + lax.broadcasted_iota(jnp.int32, shape, 1)
    allowed = (key_index <= query_index) & (key_index >= starts[rows])
    scores = jnp.where(allowed[None], scores, MASKED)
    highest = jnp.max(scores, -1, keepdims=True)
    exponent = jnp.exp((scores - highest) * HEAD_WIDTH ** (-0.5))
    weights = exponent * (1.0 / jnp.sum(exponent, -1, keepdims=True))
    return weights.reshape(GROUP * QUERY_BLOCK, size)


def prepare_heads(raw, cosine, sine, gain_query, gain_key, q, k):
    for h in range(GROUP):
        q[h] = rope_of(head_norm(raw, h)[0] * gain_query[...], cosine, sine)
    k[...] = rope_of(head_norm(raw, GROUP)[0] * gain_key[...], cosine, sine)


def attend_forward(raw, cosine, sine, starts, gain_query, gain_key, out, q, k):
    prepare_heads(raw, cosine, sine, gain_query, gain_key, q, k)
    at = (GROUP + 1) * HEAD_WIDTH
    for rows, cols in blocks_of(raw.shape[0]):
        weights = weights_of(together(q, rows), k[cols], starts, rows, cols).astype(BF16)
        value = raw[cols, at : at + HEAD_WIDTH].astype(BF16)
        result = dot(weights, value).astype(BF16).reshape(GROUP, QUERY_BLOCK, HEAD_WIDTH)
        for h in range(GROUP):
            out[rows, h * HEAD_WIDTH : (h + 1) * HEAD_WIDTH] = result[h]


def attend_backward(
    raw,
    cosine,
    sine,
    starts,
    gain_query,
    gain_key,
    grad_hidden,
    normed,
    attended,
    packed,
    mlp_left,
    mlp_right,
    out,
    gains,
    weight_grads,
    output,
    q,
    k,
    v,
    dq,
    dk,
    dv,
    grad,
    total,
    normed_held,
    mlp_left_held,
    mlp_right_held,
    loads,
    *scratch
):
    factor = HEAD_WIDTH ** (-0.5)
    at = (GROUP + 1) * HEAD_WIDTH
    inputs = (GROUP + 2) * HEAD_WIDTH
    mlp = Reduce(mlp_left_held, mlp_right_held, mlp_right.shape[0] // 2, *scratch)
    length = raw.shape[0]
    here = pl.ds(pl.multiple_of(pl.program_id(0) * length, length), length)
    normed_load = pltpu.make_async_copy(normed.at[here], normed_held, loads.at[0])
    mlp_loads = [
        pltpu.make_async_copy(source, target, loads.at[i + 1])
        for i, (source, target) in enumerate(
            ((mlp_left, mlp_left_held), (mlp_right, mlp_right_held))
        )
    ]

    def mlp_load():
        greet(neighbours()[2:])
        for load in mlp_loads:
            load.start()

    def mlp_begin():
        for load in mlp_loads:
            load.wait()
        for c in range(FEW):
            mlp.produce(c, False)
            if c == 0:
                meet(3)
            mlp.begin(c)
        for c in range(FEW):
            mlp.produce(c, True)
            mlp.first(c)

    def mlp_second():
        for c in range(FEW):
            mlp.second(c)

    def mlp_end():
        def step(rows):
            output[rows] = mlp.take(rows)


        for c in range(FEW):
            mlp.arrive(c)
            tiles(c * mlp.rows, mlp.rows, step)
        for c in range(FEW):
            mlp.release(c)
        mlp.finish()

    def at_step(step, job):
        pl.when(pl.program_id(0) == step)(job)

    at_step(0, mlp_load)
    normed_load.start()
    prepare_heads(raw, cosine, sine, gain_query, gain_key, q, k)
    v[...] = raw[:, at : at + HEAD_WIDTH].astype(BF16)
    dk[...] = jnp.zeros_like(dk)
    dv[...] = jnp.zeros_like(dv)
    for h in range(GROUP):
        lanes = slice(inputs + h * HEAD_WIDTH, inputs + (h + 1) * HEAD_WIDTH)
        grad[h] = dot(grad_hidden[...], packed[:, lanes]).astype(BF16)
    at_step(0, mlp_begin)
    for n, (rows, cols) in enumerate(blocks_of(length)):
        query, block_grad = together(q, rows), together(grad, rows)
        weights = weights_of(query, k[cols], starts, rows, cols)
        grad_weights = dot(block_grad, v[cols], 1, 1)
        inner = jnp.sum(weights * grad_weights, -1, keepdims=True)
        grad_scores = (weights * (grad_weights - inner)).astype(BF16)
        dq[:, rows] = (dot(grad_scores, k[cols]) * factor).reshape(GROUP, QUERY_BLOCK, HEAD_WIDTH)
        dk[cols] += dot(grad_scores, query, 0, 0) * factor
        dv[cols] += dot(weights.astype(BF16), block_grad, 0, 0)
        if n == 0:
            at_step(1, mlp_second)
    gains[...] = jnp.zeros_like(gains)

    def undo(rot_grad, h, gain, row):
        normed_grad = rot_grad * cosine[...] - rolled(rot_grad) * sine[...]
        hat, inv = head_norm(raw, h)
        gains[0, row : row + 1] += jnp.sum(normed_grad * hat, 0, keepdims=True)
        lanes = slice(h * HEAD_WIDTH, (h + 1) * HEAD_WIDTH)
        scaled = normed_grad * gain[...]
        out[:, lanes] = (inv * (scaled - hat * lane_mean(scaled * hat))).astype(BF16)

    for h in range(GROUP):
        undo(dq[h], h, gain_query, 0)
    undo(dk[...], GROUP, gain_key, 1)
    out[:, at : at + HEAD_WIDTH] = dv[...].astype(BF16)

    @pl.when(pl.program_id(0) == 0)
    def _():
        total[...] = jnp.zeros_like(total)

    out_turned, attended_turned = out[...].T, attended[...].T
    normed_load.wait()
    for start in range(0, normed.shape[1], COLUMNS):
        cols = slice(start, start + COLUMNS)
        total[:inputs, cols] += dot(out_turned, normed_held[:, cols])
        total[inputs:, cols] += dot(attended_turned, grad_hidden[:, cols])

    @pl.when(pl.program_id(0) == pl.num_programs(0) - 1)
    def _():
        size = weight_grads.shape[2]
        for i in range(weight_grads.shape[0]):
            weight_grads[i] = total[:, i * size : (i + 1) * size].astype(BF16)

    at_step(1, mlp_end)


def once(spec):
    return pl.BlockSpec(spec.block_shape, spec.index_map, pipeline_mode=pl.Buffered(1))


def by_rows(rows, cols):
    return pl.BlockSpec((rows, cols), lambda i: (i, 0))


def whole(*shape):
    return pl.BlockSpec(shape, lambda i: (0,) * len(shape))


def call_blocks(
    kernel, steps, in_specs, out_shape, out_specs, scratch, flops, bytes_accessed, **remote_params
):
    return pl.pallas_call(
        kernel,
        out_shape=out_shape,
        grid=(steps,),
        in_specs=in_specs,
        out_specs=out_specs,
        scratch_shapes=scratch,
        name=kernel.__name__,
        cost_estimate=pl.CostEstimate(
            flops=flops, bytes_accessed=bytes_accessed, transcendentals=0
        ),
        compiler_params=pltpu.CompilerParams(
            dimension_semantics=("arbitrary",), vmem_limit_bytes=60 * MIB, **remote_params
        ),
    )


TOKEN_BLOCK = 512
HIDDEN_BLOCK = 256


def mlp_forward(normed, weights, active, gate_slope, up_slope):
    size = active.shape[1]
    for start in range(0, size, HIDDEN_BLOCK):
        cols = slice(start, start + HIDDEN_BLOCK)
        gate = dot(normed[...], weights[:, cols])
        up = dot(normed[...], weights[:, size + start : size + start + HIDDEN_BLOCK])
        sigmoid = jax.nn.sigmoid(gate)
        swish = gate * sigmoid
        active[:, cols] = (swish * up).astype(BF16)
        gate_slope[:, cols] = up * sigmoid * (1.0 + gate * (1.0 - sigmoid))
        up_slope[:, cols] = swish


def mlp_backward(cotangent, weights, gate_slope, up_slope, grads):
    size = gate_slope.shape[1]
    for start in range(0, size, HIDDEN_BLOCK):
        cols = slice(start, start + HIDDEN_BLOCK)
        grad = dot(cotangent[...], weights[:, cols])
        grads[:, cols] = (grad * gate_slope[:, cols]).astype(BF16)
        up_cols = slice(size + start, size + start + HIDDEN_BLOCK)
        grads[:, up_cols] = (grad * up_slope[:, cols]).astype(BF16)


def on_device(
    tokens,
    documents,
    cotangent,
    attn_gain,
    query_gain,
    key_norm_scale,
    query_weight,
    key_projection,
    value_projection,
    output_weight,
    mlp_gain,
    gate_weight,
    up_weight,
    down_weight,
):
    n_dp = lax.axis_size("dp")
    dp, mp = lax.axis_index("dp"), lax.axis_index("mp")
    y = dp % 2
    slabs = [[i + 2 * k for k in range(n_dp // 2)] for i in range(2)]
    rows, width = tokens.shape
    seq_length = documents.shape[1]
    seqs = 2 * documents.shape[0]
    share = rows // 4
    head = HEAD_WIDTH
    query_cols, key_cols, hidden_cols = (
        query_weight.shape[1] // 2,
        key_projection.shape[1] // 2,
        gate_weight.shape[1] // 2,
    )
    attn_cols = query_cols + 2 * key_cols

    def y_swap(values):
        return lax.ppermute(values, "dp", [(i, i ^ 1) for i in range(n_dp)])

    def mp_swap(values, bit):
        return lax.ppermute(values, "mp", [(i, i ^ bit) for i in range(4)])

    def in_order(where, mine, other, axis):
        return jnp.where(
            where == 0,
            jnp.concatenate([mine, other], axis),
            jnp.concatenate([other, mine], axis),
        )

    def half(values, which, axis):
        size = values.shape[axis] // 2
        return lax.dynamic_slice_in_dim(values, which * size, size, axis)

    def slab_gather(values):
        return lax.all_gather(values, "dp", axis=0, tiled=True, axis_index_groups=slabs)

    def slab_scatter(values):
        return lax.psum_scatter(
            values, "dp", scatter_dimension=0, tiled=True, axis_index_groups=slabs
        )

    n_gain, n_head = attn_gain.shape[0], query_gain.shape[0]

    def gain_rows(*parts):
        lead = parts[0].shape[:-1]
        pad = [(0, 0)] * len(lead)
        rows_of = jnp.concatenate(
            [
                jnp.pad(part, pad + [(0, -part.shape[-1] % 128)]).reshape(*lead, -1, 128)
                for part in parts
            ],
            -2,
        )
        return jnp.pad(rows_of, pad + [(0, 8 - rows_of.shape[-2]), (0, 0)])

    def gain_parts_of(rows_of):
        lead, parts, at = rows_of.shape[:-2], [], 0
        for size in (n_gain, n_gain, n_head, n_head):
            n = -(-size // 128)
            part = rows_of[..., at : at + n, :].reshape(*lead, n * 128)
            parts.append(part[..., :size])
            at += n
        return parts

    model_rows = query_weight.shape[0]
    pack_cols = attn_cols + query_cols
    pair_rows = 2 * rows
    n_slabs = n_dp // 2
    attn_full, gains, docs_other, normed_one, mlp_mine = call_leg(
        front,
        3,
        "front",
        [VM] * 9 + [ANY] * 3,
        (
            jax.ShapeDtypeStruct((width, pack_cols), BF16),
            jax.ShapeDtypeStruct((n_dp, 8, 128), F32),
            jax.ShapeDtypeStruct(documents.shape, jnp.int32),
            jax.ShapeDtypeStruct((pair_rows, width), BF16),
            jax.ShapeDtypeStruct((2 * model_rows, 2 * hidden_cols), BF16),
        ),
        (VM, VM, VM, ANY, VM),
        [
            pltpu.VMEM((model_rows, pack_cols), BF16),
            pltpu.VMEM((8, 128), F32),
            pltpu.VMEM((pair_rows, width), BF16),
            pltpu.VMEM((model_rows, 2 * hidden_cols), BF16),
            pltpu.VMEM((rows, width), BF16),
            pltpu.VMEM((rows, width), BF16),
            pltpu.VMEM(gate_weight.shape, F32),
            pltpu.VMEM(up_weight.shape, F32),
            pltpu.SemaphoreType.DMA((3,)),
            pltpu.SemaphoreType.DMA((8,)),
            pltpu.SemaphoreType.DMA((2, 4)),
            pltpu.SemaphoreType.DMA((n_dp,)),
            pltpu.SemaphoreType.DMA((n_dp,)),
            pltpu.SemaphoreType.DMA((n_slabs, 2)),
            pltpu.SemaphoreType.DMA((n_slabs, 2)),
        ]
        + Spread.scratch(),
        250 * MIB,
    )(
        query_weight,
        key_projection,
        value_projection,
        output_weight,
        attn_gain.reshape(1, -1),
        mlp_gain.reshape(1, -1),
        query_gain.reshape(1, -1),
        key_norm_scale.reshape(1, -1),
        documents,
        tokens,
        gate_weight,
        up_weight,
    )
    down_low = down_weight.astype(BF16)
    down_given, _ = lax.optimization_barrier((half(down_low, 1 - y, 0).T, docs_other))
    down_got = y_swap(down_given)

    cot_part = lax.dynamic_slice_in_dim(cotangent, mp * share, share, 0)
    cot_part, _ = lax.optimization_barrier((cot_part, docs_other))
    cot_part = y_swap(cot_part)
    gate_up_full = slab_gather(mlp_mine)
    gain_one, gain_two, gain_query, gain_key = (g.reshape(1, -1) for g in gain_parts_of(gains))
    docs = jnp.concatenate([documents, docs_other], 0)
    tokens_share = lax.dynamic_slice_in_dim(tokens, mp * share, share, 0)
    cot_share = lax.dynamic_slice_in_dim(cotangent, mp * share, share, 0)

    raw = dot(normed_one, attn_full[:, :attn_cols])
    starts = sum((docs < i).sum(1, keepdims=True) * (docs == i) for i in range(1, 4))
    positions = (jnp.arange(seq_length, dtype=jnp.int32)[None] - starts).reshape(pair_rows)
    cosine, sine = rope_tables(positions, head)
    starts = starts.reshape(pair_rows, 1).astype(jnp.int32)
    raw, sine, cot_part = lax.optimization_barrier((raw, sine, cot_part))
    cot_across = mp_swap(cot_part, 2)
    attention_args = (raw, cosine, sine, starts, gain_query, gain_key)
    attention_specs = [
        by_rows(seq_length, attn_cols),
        by_rows(seq_length, head),
        by_rows(seq_length, head),
        by_rows(seq_length, 1),
        whole(1, head),
        whole(1, head),
    ]
    pair_flops = pair_rows * seq_length * query_cols
    attended = call_blocks(
        attend_forward,
        seqs,
        attention_specs,
        jax.ShapeDtypeStruct((pair_rows, query_cols), BF16),
        by_rows(seq_length, query_cols),
        [pltpu.VMEM((GROUP, seq_length, head), BF16), pltpu.VMEM((seq_length, head), BF16)],
        2 * pair_flops,
        20 * MIB,
    )(*attention_args)
    attended, cot_across, down_got = lax.optimization_barrier((attended, cot_across, down_got))
    down_full = slab_gather(in_order(y, half(down_low, y, 0).T, down_got, 0))

    def grouped(cols):
        return (2, 2, 2, share, cols)

    half_width = width // 2
    leg_scratch = Reduce.scratch(share, width, half_width) + Gather.scratch(share, width)
    hidden, normed_two, cot_pair = call_leg(
        attention_leg,
        0,
        "attention_leg",
        [VM] * 4 + [ANY] * 3,
        (
            jax.ShapeDtypeStruct((share, width), F32),
            jax.ShapeDtypeStruct(grouped(width), BF16),
            jax.ShapeDtypeStruct((pair_rows, width), BF16),
        ),
        (VM, ANY, ANY),
        [
            pltpu.VMEM((rows + 2 * share, width), BF16),
            pltpu.SemaphoreType.DMA((3,)),
            pltpu.SemaphoreType.DMA((3,)),
            pltpu.SemaphoreType.DMA((2,)),
            pltpu.SemaphoreType.DMA((2,)),
        ]
        + leg_scratch,
        200 * MIB,
    )(
        attended.reshape(grouped(query_cols)),
        attn_full,
        tokens_share,
        gain_two,
        cotangent,
        cot_part,
        cot_across,
    )
    normed_two = normed_two.reshape(pair_rows, width)

    blocks = pair_rows // TOKEN_BLOCK
    hidden_block = by_rows(TOKEN_BLOCK, hidden_cols)
    hidden_shape = (pair_rows, hidden_cols)
    mlp_flops = 2 * pair_rows * width * hidden_cols
    active, gate_slope, up_slope = call_blocks(
        mlp_forward,
        blocks,
        [by_rows(TOKEN_BLOCK, width), whole(width, 2 * hidden_cols)],
        (
            jax.ShapeDtypeStruct(hidden_shape, BF16),
            jax.ShapeDtypeStruct(hidden_shape, F32),
            jax.ShapeDtypeStruct(hidden_shape, F32),
        ),
        (hidden_block,) * 3,
        [],
        2 * mlp_flops,
        30 * MIB,
    )(normed_two, gate_up_full)
    down_part = dot(cot_pair, active, 0, 0).astype(BF16)
    down_grad = slab_scatter(down_part)
    cot_late, _ = lax.optimization_barrier((cot_pair, down_part))
    grad_gate_up = call_blocks(
        mlp_backward,
        blocks,
        [by_rows(TOKEN_BLOCK, width), whole(width, hidden_cols), hidden_block, hidden_block],
        jax.ShapeDtypeStruct((pair_rows, 2 * hidden_cols), BF16),
        by_rows(TOKEN_BLOCK, 2 * hidden_cols),
        [],
        mlp_flops,
        30 * MIB,
    )(cot_late, down_full, gate_slope, up_slope)
    gate_up_part = dot(normed_two, grad_gate_up, 0, 0).astype(BF16)
    gate_up_grad = slab_scatter(gate_up_part)
    grad_gate_up, _, _ = lax.optimization_barrier((grad_gate_up, gate_up_part, down_part))
    grad_hidden, mlp_gain_part, grad_hidden_low = call_leg(
        hidden_leg,
        1,
        "hidden_leg",
        [ANY] * 2 + [VM] * 3,
        (
            jax.ShapeDtypeStruct((share, width), F32),
            jax.ShapeDtypeStruct((1, width), F32),
            jax.ShapeDtypeStruct(grouped(width), BF16),
        ),
        (VM, VM, ANY),
        [
            pltpu.VMEM(grouped(2 * hidden_cols), BF16),
            pltpu.VMEM((width, 2 * hidden_cols), BF16),
            pltpu.SemaphoreType.DMA((2, CHUNKS)),
            pltpu.SemaphoreType.DMA((width // COLUMNS,)),
        ]
        + leg_scratch,
        200 * MIB,
    )(
        grad_gate_up.reshape(grouped(2 * hidden_cols)),
        gate_up_full,
        hidden,
        cot_share,
        gain_two,
    )
    grad_hidden_low = grad_hidden_low.reshape(pair_rows, width)

    raw_grad, head_gain_parts, attn_grad, mlp_total = call_blocks(
        attend_backward,
        seqs,
        [once(spec) for spec in attention_specs]
        + [
            once(by_rows(seq_length, width)),
            ANY,
            once(by_rows(seq_length, query_cols)),
            once(whole(width, pack_cols)),
            ANY,
            ANY,
        ],
        (
            jax.ShapeDtypeStruct((pair_rows, attn_cols), BF16),
            jax.ShapeDtypeStruct((seqs, 8, head), F32),
            jax.ShapeDtypeStruct((n_dp, pack_cols, model_rows), BF16),
            jax.ShapeDtypeStruct((share, width), F32),
        ),
        (
            once(by_rows(seq_length, attn_cols)),
            pl.BlockSpec((1, 8, head), lambda i: (i, 0, 0)),
            once(whole(n_dp, pack_cols, model_rows)),
            once(whole(share, width)),
        ),
        [
            pltpu.VMEM((GROUP, seq_length, head), BF16),
            pltpu.VMEM((seq_length, head), BF16),
            pltpu.VMEM((seq_length, head), BF16),
            pltpu.VMEM((GROUP, seq_length, head), F32),
            pltpu.VMEM((seq_length, head), F32),
            pltpu.VMEM((seq_length, head), F32),
            pltpu.VMEM((GROUP, seq_length, head), BF16),
            pltpu.VMEM((pack_cols, width), F32),
            pltpu.VMEM((seq_length, width), BF16),
            pltpu.VMEM(grouped(hidden_cols), BF16),
            pltpu.VMEM((width, hidden_cols), BF16),
            pltpu.SemaphoreType.DMA((3,)),
        ]
        + Reduce.scratch(share, width, half_width, FEW),
        5 * pair_flops + 2 * pair_rows * width * (pack_cols + query_cols + hidden_cols),
        80 * MIB,
        collective_id=4,
        has_side_effects=True,
    )(
        *attention_args,
        grad_hidden_low,
        normed_one,
        attended,
        attn_full,
        active.reshape(grouped(hidden_cols)),
        down_full,
    )
    head_gain_parts = head_gain_parts.sum(0)
    attn_grad = attn_grad.reshape(n_dp * pack_cols, model_rows)
    attn_grad, raw_grad, gate_up_grad, down_grad = lax.optimization_barrier(
        (attn_grad, raw_grad, gate_up_grad, down_grad)
    )
    attn_parts = attn_grad.reshape(n_dp, pack_cols, model_rows)
    attn_grad = slab_scatter(attn_grad).reshape(2, pack_cols, model_rows)
    gain_parts = gain_rows(
        jnp.zeros((n_dp, n_gain), F32),
        mlp_gain_part.reshape(n_dp, n_gain),
        head_gain_parts[0].reshape(n_dp, n_head),
        head_gain_parts[1].reshape(n_dp, n_head),
    )

    low = 7 * width // 8
    input_grad, gain_sums, gate_up_other, down_other = call_leg(
        output_leg,
        2,
        "output_leg",
        [VM] * 7 + [ANY] * 2,
        (
            jax.ShapeDtypeStruct((share, width), F32),
            jax.ShapeDtypeStruct((8, 128), F32),
            jax.ShapeDtypeStruct((model_rows, 2 * hidden_cols), BF16),
            jax.ShapeDtypeStruct((model_rows, hidden_cols), BF16),
        ),
        (VM, VM, ANY, ANY),
        [
            pltpu.VMEM((n_dp, 8, 128), F32),
            pltpu.SemaphoreType.DMA((2,)),
            pltpu.SemaphoreType.DMA((2,)),
        ]
        + Reduce.scratch(share, width, low)
        + SumGains.scratch(n_dp, 4),
        200 * MIB,
    )(
        raw_grad.reshape(grouped(attn_cols)),
        attn_full,
        tokens_share,
        gain_one,
        gain_parts,
        attn_parts,
        grad_hidden,
        gate_up_grad,
        down_grad,
    )
    attn_given = lax.dynamic_index_in_dim(attn_grad, 1 - y, 0, False)
    attn_given, gate_up_other, down_other = lax.optimization_barrier(
        (attn_given, gate_up_other, down_other)
    )
    layer_output = (hidden + mlp_total).astype(BF16)

    def columns(own, other, start, axis=1):
        own = half(own, y, 0)[:, start : start + hidden_cols]
        other = other[:, start : start + hidden_cols]
        if axis == 0:
            own, other = own.T, other.T
        return in_order(y, own, other, axis).astype(F32)

    gate_grad = columns(gate_up_grad, gate_up_other, 0)
    up_grad = columns(gate_up_grad, gate_up_other, hidden_cols)
    down_grad = columns(down_grad, down_other, 0, 0)

    attn_other = y_swap(attn_given)
    attn_own = lax.dynamic_index_in_dim(attn_grad, y, 0, False)

    query_grad, key_grad, value_grad, output_grad = pl.pallas_call(
        finish_attention,
        out_shape=tuple(
            jax.ShapeDtypeStruct(w.shape, F32)
            for w in (query_weight, key_projection, value_projection, output_weight)
        ),
        in_specs=[VM] * 2,
        out_specs=(VM,) * 4,
        name="finish_attention",
        cost_estimate=pl.CostEstimate(flops=0, bytes_accessed=4 * MIB, transcendentals=0),
        compiler_params=pltpu.CompilerParams(vmem_limit_bytes=32 * MIB),
    )(attn_own, attn_other)
    attn_gain_grad, mlp_gain_grad, query_gain_grad, key_gain_grad = gain_parts_of(gain_sums)
    return (
        layer_output,
        input_grad,
        attn_gain_grad,
        query_gain_grad,
        key_gain_grad,
        query_grad,
        key_grad,
        value_grad,
        output_grad,
        mlp_gain_grad,
        gate_grad,
        up_grad,
        down_grad,
    )


def solution(mesh):
    in_specs = (
        P("dp", None),
        P("dp", None),
        P("dp", None),
        P("dp"),
        P("dp"),
        P("dp"),
        P("dp", "mp"),
        P("dp", "mp"),
        P("dp", "mp"),
        P("mp", "dp"),
        P("dp"),
        P("dp", "mp"),
        P("dp", "mp"),
        P("mp", "dp"),
    )
    out_specs = (
        P(("dp", "mp"), None),
        P(("dp", "mp"), None),
        P("dp"),
        P("dp"),
        P("dp"),
        P("dp", "mp"),
        P("dp", "mp"),
        P("dp", "mp"),
        P("mp", "dp"),
        P("dp"),
        P("dp", "mp"),
        P("dp", "mp"),
        P("mp", "dp"),
    )
    return jax.shard_map(
        on_device, mesh=mesh, in_specs=in_specs, out_specs=out_specs, check_vma=False
    )
```
